256 devices in a mesh: dp: 16 (over z_hi, y), ctx: 16 (over x, z_lo, core).
Axes of the slice: x: 4, y: 4, z: 8 (z_hi: 4, z_lo: 2; z = z_hi * 2 + z_lo), core: 2. Of those that a mesh axis runs over, the one named last changes fastest.
Arguments:
- layer_input: bfloat16 [16, 2048, 4096], P('dp', 'ctx'), may hold values from -6 to 6
- query_states: bfloat16 [16, 2048, 512], P('dp', 'ctx'), may hold values from -9 to 9
- key_states: bfloat16 [16, 2048, 128], P('dp', 'ctx'), may hold values from -9 to 9
- value_states: bfloat16 [16, 2048, 128], P('dp', 'ctx'), may hold values from -6 to 6
- output_grad: bfloat16 [16, 2048, 512], P('dp', 'ctx'), may hold values from -6 to 6
- doc_lengths: int32 [16, 8], P('dp'), may hold values from 1 to 1024, 2048 in all within a row
Outputs:
- query_grad: bfloat16 [16, 2048, 512], P('dp', 'ctx')
- key_grad: bfloat16 [16, 2048, 128], P('dp', 'ctx')
- value_grad: bfloat16 [16, 2048, 128], P('dp', 'ctx')
- kv_weight_grad: float32 [4096, 256], P(('dp', 'ctx'))
The draws below stay inside these ranges and needn't reach their ends.
All inputs are finite; a program needn't handle non-finite values.
Results may differ from the reference program's by a relative error of at most 0.014.
Values may be sent and summed in bfloat16 or wider, within the bound.
No kernel may reach another device: no remote copies, remote signals or barrier semaphores. Data moves between devices by JAX's collectives and lax.ppermute only.
A program may use at most 64 MiB of HBM per device.

```python
import math
import jax
import jax.numpy as jnp
import numpy as np
from jax import lax

D = 4096
HEADS = 4
HEAD = 128
DOCS = 8
SEQ = 2048
SEQUENCES = 16


def draw_key_states(key, part):
    drawn_draw = jax.random.normal(jax.random.fold_in(key, 7002), (SEQUENCES, SEQ, HEAD), jnp.float32)
    return jnp.clip(drawn_draw, -4.0, 4.0).astype(jnp.bfloat16)


def draw_query_states(key, part):
    drawn_draw = jnp.clip(jax.random.normal(jax.random.fold_in(key, 7003), (SEQUENCES, SEQ, HEADS * HEAD), jnp.float32), -4.0, 4.0)
    return drawn_draw.astype(jnp.bfloat16)


def with_spikes(array, own_key, source, target, parts, factor):
    def block_of(dim):
        return (jnp.arange(array.shape[dim]) // (array.shape[dim] // parts)).reshape((-1,) + (1,) * (array.ndim - 1 - dim))

    near = jax.random.permutation(own_key, parts)[block_of(target)]
    other_side = (block_of(target) + parts // 2) % parts
    return jnp.where((block_of(source) == near) | (block_of(source) == other_side), factor * array, array)


def steps_of(own_key, dims, shards, low, largest):
    def one(dim, shards_of):
        steps = jax.random.uniform(jax.random.fold_in(jax.random.fold_in(own_key, 6), dim), (shards_of,), jnp.float32, low / len(shards), largest / len(shards))
        return jnp.repeat(jnp.exp(steps), dims[dim] // shards_of).reshape((-1,) + (1,) * (len(dims) - dim - 1))

    gain = one(*shards[0])
    for cut in shards[1:]:
        gain = gain * one(*cut)
    return gain


def profile(amount, total, reach, lean):
    loads = [(1 << 20) // math.isqrt(rank ** lean) + 1 for rank in range(2, amount + 1)]
    rest, counts = total - reach - (amount - 1), [1] * (amount - 1)
    while rest > 0:
        movable = [i for i in range(amount - 1) if counts[i] < reach]
        mass, remaining = sum([loads[i] for i in movable]), rest
        for i in movable:
            more = min(reach - counts[i], max(1, remaining * loads[i] // mass), rest)
            counts[i] = counts[i] + more
            rest = rest - more
    return np.array([reach] + counts)


def uneven(rng, amount, total, bound, slope):
    if amount == 2:
        one = jax.random.randint(rng, (), max(1, total - bound), min(bound, total - 1) + 1)
        return jnp.stack([one, total - one])
    sizes = jnp.asarray(profile(amount, total, bound, slope), jnp.int32)
    pairs = (amount - 1) // 2
    donor, taker = sizes[1:1 + 2 * pairs:2], sizes[2:2 + 2 * pairs:2]
    slack = jnp.minimum(donor - 1, bound - taker)
    shifted = jax.random.randint(jax.random.fold_in(rng, 1), (pairs,), 0, 1 << 20) % (slack + 1)
    sizes = sizes.at[1:1 + 2 * pairs:2].set(donor - shifted).at[2:2 + 2 * pairs:2].set(taker + shifted)
    return sizes[jax.random.permutation(jax.random.fold_in(rng, 2), amount)]


def gaussian(own_key, shape, deviation, reach, shards=(), held_as=jnp.bfloat16):
    array = jax.random.normal(own_key, shape, jnp.float32) * deviation
    if len(shards) > 0:
        array = steps_of(own_key, shape, shards, -0.22, 0.18) * array
    return jnp.clip(array, min=-reach, max=reach).astype(held_as)


def bell_draw_with(own_key, extent, scale, most, pieces, heavy, held_as=jnp.bfloat16):
    drawn = scale * jax.random.normal(own_key, extent, jnp.float32)
    if pieces:
        drawn = drawn * steps_of(own_key, extent, pieces, -0.22, 0.18)
    return jnp.clip(with_spikes(drawn, jax.random.fold_in(own_key, 3), *heavy), -most, most).astype(held_as)


def setup_inputs(seed: int = 0) -> dict:
    splits = jax.random.split(jax.random.key(seed), 7)
    return {
        "layer_input": bell_draw_with(splits[0], (SEQUENCES, SEQ, D), 1.0, 6.0, ((0, 16), (1, 16)), (1, 2, 16, 2.0)),
        "query_states": draw_query_states(jax.random.fold_in(splits[6], 71), 0),
        "key_states": draw_key_states(jax.random.fold_in(splits[6], 71), 0),
        "value_states": gaussian(splits[3], (SEQUENCES, SEQ, HEAD), 1.0, 6.0, ((0, 16), (1, 16))),
        "output_grad": gaussian(splits[4], (SEQUENCES, SEQ, HEADS * HEAD), 1.0, 6.0, ((0, 16), (1, 16))),
        "doc_lengths": jax.vmap(lambda own: uneven(own, DOCS, SEQ, SEQ // 2, 2))(jax.random.split(splits[5], SEQUENCES)).reshape((SEQUENCES, DOCS)).astype(jnp.int32),
    }


rope_base = 500000.0


def rope_tables(positions, head_width):
    half_width = head_width // 2
    frequency = jnp.exp(jnp.arange(half_width, dtype=jnp.float32) * (-2.0 * math.log(rope_base) / head_width))
    angles = positions.astype(jnp.float32)[:, None] * frequency[None, :]
    cosine_table = jnp.cos(angles)
    sine_table = jnp.sin(angles)
    return jnp.concatenate([cosine_table, cosine_table], 1), jnp.concatenate([sine_table, sine_table], 1)


def rotate(values, cosine_table, sine_table):
    half_width = values.shape[-1] // 2
    turned = jnp.concatenate([-values[..., half_width:], values[..., :half_width]], -1)
    return values * cosine_table[:, None, :] + turned * sine_table[:, None, :]


def document_of(positions, lengths):
    doc_ends = jnp.cumsum(lengths)
    return jnp.sum((positions[:, None] >= doc_ends[None, :]).astype(jnp.int32), axis=1)


def to_low(values):
    return lax.optimization_barrier(values.astype(jnp.bfloat16)).astype(jnp.float32)


def one_sequence(layer_rows, query_rows, key_rows, value_rows, grad_rows, lengths):
    score_scale = HEAD ** -0.5
    positions = jnp.arange(SEQ, dtype=jnp.int32)
    cosine_table, sine_table = rope_tables(positions, HEAD)
    doc_ids = document_of(positions, lengths)
    query_rot = to_low(rotate(query_rows.reshape(SEQ, HEADS, HEAD).astype(jnp.float32), cosine_table, sine_table)).transpose(1, 0, 2)
    key_rot = to_low(rotate(key_rows[:, None, :].astype(jnp.float32), cosine_table, sine_table)[:, 0])
    value_full = value_rows.astype(jnp.float32)
    grad_heads = grad_rows.reshape(SEQ, HEADS, HEAD).transpose(1, 0, 2).astype(jnp.float32)
    block_rows = min(512, SEQ)

    def query_block(key_acc, block_index):
        first_row = (block_index * block_rows).astype(jnp.int32)
        query_part = lax.dynamic_slice_in_dim(query_rot, first_row, block_rows, 1)
        grad_part = lax.dynamic_slice_in_dim(grad_heads, first_row, block_rows, 1)
        query_pos = lax.dynamic_slice_in_dim(positions, first_row, block_rows, 0)
        query_doc = lax.dynamic_slice_in_dim(doc_ids, first_row, block_rows, 0)
        allowed = (positions[None, :] <= query_pos[:, None]) & (doc_ids[None, :] == query_doc[:, None])
        scores = jnp.einsum("hqe,ke->hqk", query_part, key_rot) * score_scale
        masked = jnp.where(allowed[None], scores, -jnp.inf)
        row_max = jnp.max(masked, -1, keepdims=True)
        log_total = row_max + jnp.log(jnp.sum(jnp.exp(masked - row_max), -1, keepdims=True))
        soft_probs = jnp.where(allowed[None], jnp.exp(scores - log_total), 0.0)
        dprobs = jnp.einsum("hqe,ke->hqk", grad_part, value_full)
        grad_delta = jnp.sum(soft_probs * dprobs, -1, keepdims=True)
        dscores = to_low(soft_probs * (dprobs - grad_delta))
        probs_low = to_low(soft_probs)
        query_part_grad = jnp.einsum("hqk,ke->hqe", dscores, key_rot) * score_scale
        key_part = jnp.einsum("hqk,hqe->ke", dscores, query_part)
        value_part = jnp.einsum("hqk,hqe->ke", probs_low, grad_part)
        return key_acc + jnp.concatenate([key_part, value_part], 1), query_part_grad

    key_acc, query_blocks = lax.scan(query_block, jnp.zeros((SEQ, 2 * HEAD), jnp.float32), jnp.arange(SEQ // block_rows, dtype=jnp.int32))
    query_flat = query_blocks.transpose(1, 0, 2, 3).reshape(HEADS, SEQ, HEAD).transpose(1, 0, 2)
    query_back = rotate(query_flat, cosine_table, -sine_table).astype(jnp.bfloat16).reshape(SEQ, HEADS * HEAD)
    key_back = rotate((key_acc[:, :HEAD] * score_scale)[:, None, :], cosine_table, -sine_table)[:, 0].astype(jnp.bfloat16)
    value_back = key_acc[:, HEAD:].astype(jnp.bfloat16)
    grads_low = jnp.concatenate([key_back, value_back], 1)
    partial_sum = lax.dot_general(layer_rows, grads_low, (((0,), (0,)), ((), ())), preferred_element_type=jnp.float32)
    return query_back, key_back, value_back, partial_sum


def reference(layer_input, query_states, key_states, value_states, output_grad, doc_lengths):
    def per_sequence(inputs):
        return one_sequence(inputs[0], inputs[1], inputs[2], inputs[3], inputs[4], inputs[5])

    outputs = lax.map(per_sequence, (layer_input, query_states, key_states, value_states, output_grad, doc_lengths))
    return outputs[0], outputs[1], outputs[2], jnp.sum(outputs[3], axis=0)
```

```python
import math

import jax
import jax.numpy as jnp
from jax import lax
from jax.experimental import pallas as pl
from jax.experimental.pallas import tpu as pltpu
from jax.sharding import PartitionSpec as P

ROPE_BASE = 500000.0
NEG = -1e30
B = 128
WINDOW = 12
NT = (((1,), (1,)), ((), ()))
TN = (((0,), (0,)), ((), ()))
NN = (((1,), (0,)), ((), ()))


def dot(a, b, dims):
    return lax.dot_general(a, b, dims, preferred_element_type=jnp.float32)


def rope_table(positions):
    half = B // 2
    frequency = jnp.exp(jnp.arange(half, dtype=jnp.float32) * (-2.0 * math.log(ROPE_BASE) / B))
    angles = positions.astype(jnp.float32)[:, None] * frequency[None, :]
    return jnp.concatenate([jnp.cos(angles), jnp.sin(angles)], 1)


def split_table(table):
    lane = lax.broadcasted_iota(jnp.int32, table.shape, 1)
    swapped = pltpu.roll(table, B // 2, 1)
    low = lane < B // 2
    return jnp.where(low, table, swapped), jnp.where(low, -swapped, table)


def rotated(u, cosine, sine):
    return u * cosine + pltpu.roll(u, B // 2, 1) * sine


def attention_kernel(
    where_ref, len_ref, q_ref, g_ref, own_ref, z_ref, c_ref, cz_ref, tab_ref,
    qgrad_ref, keep_ref, send_ref,
    k_s, v_s, q_s, g_s, s_s, d_s, m_s, l_s, w_s, dq_s,
):
    rank = where_ref[0]
    slab = rank // 4
    col = rank % 4
    first = (slab - 2) * 4
    scale = B**-0.5

    q_base = rank * B
    q_pos = q_base + lax.broadcasted_iota(jnp.int32, (1, B), 1)
    start = jnp.zeros((1, B), jnp.int32)
    low = jnp.int32(0)
    end = jnp.int32(0)
    for d in range(8):
        end = end + len_ref[0, d]
        start = jnp.where(q_pos >= end, end, start)
        low = jnp.where(q_base >= end, end, low)
    lo = jnp.maximum(low // B - first, 0)
    hi = 9 + col

    for source, ref in ((0, own_ref), (1, c_ref), (2, z_ref), (3, cz_ref)):
        column = col ^ source
        for b in range(3):
            block = (2 - b) * 4 + column

            @pl.when((block >= lo) & (block < hi))
            def _():
                at = pl.ds(pl.multiple_of(block * B, B), B)
                cosine, sine = split_table(tab_ref[at, :])
                rows = ref[b * B : (b + 1) * B, :]
                k_s[at, :] = rotated(rows[:, :B].astype(jnp.float32), cosine, sine).astype(jnp.bfloat16)
                v_s[at, :] = rows[:, B:]

    own_at = pl.ds(pl.multiple_of((8 + col) * B, B), B)
    cosine, sine = split_table(tab_ref[own_at, :])
    for h in range(4):
        u = q_ref[:, h * B : (h + 1) * B].astype(jnp.float32)
        q_s[h * B : (h + 1) * B, :] = rotated(u, cosine, sine).astype(jnp.bfloat16)
        g_s[h * B : (h + 1) * B, :] = g_ref[:, h * B : (h + 1) * B]

    m_s[...] = jnp.full(m_s.shape, NEG, jnp.float32)
    l_s[...] = jnp.zeros(l_s.shape, jnp.float32)
    w_s[...] = jnp.zeros(w_s.shape, jnp.float32)
    dq_s[...] = jnp.zeros(dq_s.shape, jnp.float32)
    keep_ref[...] = jnp.zeros(keep_ref.shape, keep_ref.dtype)
    send_ref[...] = jnp.zeros(send_ref.shape, send_ref.dtype)

    def scores(block, carry):
        at = pl.ds(pl.multiple_of(block * B, B), B)
        s = dot(k_s[at, :], q_s[...], NT) * scale
        key_pos = (first + block) * B + lax.broadcasted_iota(jnp.int32, (B, B), 0)
        allowed = (key_pos <= q_pos) & (key_pos >= start)
        d_s[at, :] = dot(v_s[at, :], g_s[...], NT)
        for h in range(4):
            part = jnp.where(allowed, s[:, h * B : (h + 1) * B], NEG)
            s_s[at, h * B : (h + 1) * B] = part
            m_s[:, h * B : (h + 1) * B] = jnp.maximum(
                m_s[:, h * B : (h + 1) * B], jnp.max(part.reshape(16, 8, B), axis=0)
            )
        return carry

    lax.fori_loop(lo, hi, scores, 0)
    top = jnp.max(m_s[...], axis=0, keepdims=True)

    def weights(block, carry):
        at = pl.ds(pl.multiple_of(block * B, B), B)
        p = jnp.exp(s_s[at, :] - top)
        s_s[at, :] = p
        l_s[...] += jnp.sum(p.reshape(16, 8, 4 * B), axis=0)
        w_s[...] += jnp.sum((p * d_s[at, :]).reshape(16, 8, 4 * B), axis=0)
        return carry

    lax.fori_loop(lo, hi, weights, 0)
    inverse = 1.0 / jnp.sum(l_s[...], axis=0, keepdims=True)
    delta = jnp.sum(w_s[...], axis=0, keepdims=True) * inverse

    def gradients(block, carry):
        at = pl.ds(pl.multiple_of(block * B, B), B)
        p = s_s[at, :] * inverse
        ds = (p * (d_s[at, :] - delta)).astype(jnp.bfloat16)
        dv = dot(p.astype(jnp.bfloat16), g_s[...], NN)
        dk = dot(ds, q_s[...], NN) * scale
        dq_s[...] += dot(k_s[at, :], ds, TN)
        relative = (block % 4) ^ col
        out_at = pl.ds(pl.multiple_of(((relative // 2) * 3 + 2 - block // 4) * B, B), B)

        @pl.when(relative % 2 == 0)
        def _():
            keep_ref[out_at, :B] = dk
            keep_ref[out_at, B:] = dv

        @pl.when(relative % 2 == 1)
        def _():
            send_ref[out_at, :B] = dk.astype(jnp.bfloat16)
            send_ref[out_at, B:] = dv.astype(jnp.bfloat16)

        return carry

    lax.fori_loop(lo, hi, gradients, 0)
    for h in range(4):
        u = dq_s[:, h * B : (h + 1) * B].T * scale
        qgrad_ref[:, h * B : (h + 1) * B] = rotated(u, cosine, -sine).astype(jnp.bfloat16)


def attention(rank, lengths, q, g, own, z, c, cz, table):
    vmem = pl.BlockSpec(memory_space=pltpu.VMEM)
    smem = pl.BlockSpec(memory_space=pltpu.SMEM)
    rows = WINDOW * B
    return pl.pallas_call(
        attention_kernel,
        out_shape=(
            jax.ShapeDtypeStruct((B, 4 * B), jnp.bfloat16),
            jax.ShapeDtypeStruct((6 * B, 2 * B), jnp.float32),
            jax.ShapeDtypeStruct((6 * B, 2 * B), jnp.bfloat16),
        ),
        in_specs=[smem, smem] + [vmem] * 7,
        out_specs=(vmem, vmem, vmem),
        scratch_shapes=[
            pltpu.VMEM((rows, B), jnp.bfloat16),
            pltpu.VMEM((rows, B), jnp.bfloat16),
            pltpu.VMEM((4 * B, B), jnp.bfloat16),
            pltpu.VMEM((4 * B, B), jnp.bfloat16),
            pltpu.VMEM((rows, 4 * B), jnp.float32),
            pltpu.VMEM((rows, 4 * B), jnp.float32),
            pltpu.VMEM((8, 4 * B), jnp.float32),
            pltpu.VMEM((8, 4 * B), jnp.float32),
            pltpu.VMEM((8, 4 * B), jnp.float32),
            pltpu.VMEM((B, 4 * B), jnp.float32),
        ],
        compiler_params=pltpu.CompilerParams(vmem_limit_bytes=40 * 1024 * 1024),
        cost_estimate=pl.CostEstimate(flops=755_000_000, bytes_accessed=6_000_000, transcendentals=590_000),
        name="attention",
    )(rank, lengths, q, g, own, z, c, cz, table)


def slices_kernel(where_ref, x_ref, o0, o1, o2, o3):
    slab = where_ref[0] // 4
    for k, out in enumerate((o0, o1, o2, o3)):
        target = (slab + k) % 4
        for dp in range(16):
            at = pl.ds(pl.multiple_of(dp * 2 * B + (target // 2) * B, B), B)
            tile = x_ref[:, at].T

            @pl.when(target % 2 == 0)
            def _():
                out[dp * 64 : (dp + 1) * 64, :] = tile[:64]

            @pl.when(target % 2 == 1)
            def _():
                out[dp * 64 : (dp + 1) * 64, :] = tile[64:]


def slices(rank, x):
    vmem = pl.BlockSpec(memory_space=pltpu.VMEM)
    return pl.pallas_call(
        slices_kernel,
        out_shape=[jax.ShapeDtypeStruct((1024, B), jnp.bfloat16)] * 4,
        in_specs=[pl.BlockSpec(memory_space=pltpu.SMEM), vmem],
        out_specs=[vmem] * 4,
        cost_estimate=pl.CostEstimate(flops=0, bytes_accessed=2_000_000, transcendentals=0),
        name="slices",
    )(rank, x)


def weight_kernel(where_ref, x0, x1, x2, x3, g0, g1, g2, g3, keep_ref, send_ref, acc):
    core = where_ref[0] % 2
    total = dot(x0[...], g0[...], NN)
    for x, g in ((x1, g1), (x2, g2), (x3, g3)):
        total = total + dot(x[...], g[...], NN)
    acc[...] = total
    for i in range(32):
        mine = pl.ds(pl.multiple_of(i * 32 + core * 16, 16), 16)
        other = pl.ds(pl.multiple_of(i * 32 + (1 - core) * 16, 16), 16)
        keep_ref[i * 16 : (i + 1) * 16, :] = acc[mine, :]
        send_ref[i * 16 : (i + 1) * 16, :] = acc[other, :].astype(jnp.bfloat16)


def weight_part(rank, xs, gs):
    vmem = pl.BlockSpec(memory_space=pltpu.VMEM)
    return pl.pallas_call(
        weight_kernel,
        out_shape=(
            jax.ShapeDtypeStruct((512, 256), jnp.float32),
            jax.ShapeDtypeStruct((512, 256), jnp.bfloat16),
        ),
        in_specs=[pl.BlockSpec(memory_space=pltpu.SMEM)] + [vmem] * 8,
        out_specs=(vmem, vmem),
        scratch_shapes=[pltpu.VMEM((1024, 256), jnp.float32)],
        cost_estimate=pl.CostEstimate(flops=268_000_000, bytes_accessed=2_000_000, transcendentals=0),
        name="weight",
    )(rank, *xs, *gs)


def body(layer_input, query_states, key_states, value_states, output_grad, doc_lengths):
    rank = lax.axis_index("ctx").astype(jnp.int32)
    where = rank[None]

    def back(array, slabs):
        pairs = [(i, i + 4 * slabs) for i in range(16) if i + 4 * slabs < 16]
        return lax.ppermute(array, "ctx", pairs)

    def ahead(array, slabs):
        pairs = [(i, i - 4 * slabs) for i in range(16) if i >= 4 * slabs]
        return lax.ppermute(array, "ctx", pairs)

    def around(array, slabs):
        return lax.ppermute(array, "ctx", [(i, (i + 4 * slabs) % 16) for i in range(16)])

    def swap(array, bit):
        return lax.ppermute(array, "ctx", [(i, i ^ bit) for i in range(16)])

    kv = jnp.concatenate([key_states[0], value_states[0]], 1)
    own = jnp.concatenate([kv, back(kv, 1), back(kv, 2)], 0)
    from_z = swap(own, 2)
    from_c = swap(own, 1)
    from_cz = swap(from_z, 1)

    xs = slices(where, layer_input[0])
    xs = [xs[0]] + [around(xs[k], k) for k in (1, 2, 3)]

    first = (rank // 4 - 2) * 4 * B
    table = rope_table(first + jnp.arange(WINDOW * B, dtype=jnp.int32))
    query_grad, keep, send = attention(
        where, doc_lengths, query_states[0], output_grad[0], own, from_z, from_c, from_cz, table
    )

    both = keep + swap(send, 1).astype(jnp.float32)
    column = both[: 3 * B] + swap(both[3 * B :].astype(jnp.bfloat16), 2).astype(jnp.float32)
    low = column.astype(jnp.bfloat16)
    total = (
        column[:B]
        + ahead(low[B : 2 * B], 1).astype(jnp.float32)
        + ahead(low[2 * B :], 2).astype(jnp.float32)
    )
    own_table = lax.dynamic_slice_in_dim(table, (8 + rank % 4) * B, B, 0)
    half = B // 2
    cosine, sine = own_table[:, :half], own_table[:, half:]
    u1, u2 = total[:, :half], total[:, half:B]
    grads = jnp.concatenate(
        [u1 * cosine + u2 * sine, u2 * cosine - u1 * sine, total[:, B:]], 1
    ).astype(jnp.bfloat16)

    gs = [grads] + [around(grads, k) for k in (1, 2, 3)]
    part, part_send = weight_part(where, xs, gs)
    part = part + swap(part_send, 1).astype(jnp.float32)
    blocks = part.astype(jnp.bfloat16).reshape(32, 16, 256)
    groups = [
        [dp * 16 + slab * 4 + z * 2 + core for dp in range(16) for z in range(2)]
        for slab in range(4)
        for core in range(2)
    ]
    arrived = lax.all_to_all(
        blocks, ("dp", "ctx"), split_axis=0, concat_axis=0, tiled=True, axis_index_groups=groups
    )
    weight_grad = jnp.sum(arrived.astype(jnp.float32), axis=0)
    return query_grad[None], grads[None, :, :B], grads[None, :, B:], weight_grad


def solution(mesh):
    split = P("dp", "ctx", None)
    return jax.shard_map(
        body,
        mesh=mesh,
        in_specs=(split,) * 5 + (P("dp", None),),
        out_specs=(split, split, split, P(("dp", "ctx"), None)),
        check_vma=False,
    )
```

```python
import math

import jax
import jax.numpy as jnp
from jax import lax
from jax.experimental import pallas as pl
from jax.experimental.pallas import tpu as pltpu
from jax.sharding import PartitionSpec as P


ROPE_BASE = 500000.0
NEG = -1e30
MIB = 1024 * 1024
B = 128
WINDOW = 12
NT = (((1,), (1,)), ((), ()))
TN = (((0,), (0,)), ((), ()))
NN = (((1,), (0,)), ((), ()))


def dot(a, b, dims):
    return lax.dot_general(a, b, dims, preferred_element_type=jnp.float32)


def prepare_kernel(where_ref, key_ref, value_ref, kv_ref, tab_ref):
    half = B // 2
    index = lax.broadcasted_iota(jnp.int32, (1, half), 1).astype(jnp.float32)
    frequency = jnp.exp(index * (-2.0 * math.log(ROPE_BASE) / B))
    position = where_ref[0] * B + lax.broadcasted_iota(jnp.int32, (B, 1), 0)
    angles = position.astype(jnp.float32) * frequency
    table = jnp.concatenate([jnp.cos(angles), jnp.sin(angles)], 1)
    tab_ref[...] = table
    cosine, sine = split_table(table)
    kv_ref[:, :B] = rotated(key_ref[...].astype(jnp.float32), cosine, sine).astype(jnp.bfloat16)
    kv_ref[:, B:] = value_ref[...]


def prepare(rank, keys, values):
    vmem = pl.BlockSpec(memory_space=pltpu.VMEM)
    return pl.pallas_call(
        prepare_kernel,
        out_shape=(
            jax.ShapeDtypeStruct((B, 2 * B), jnp.bfloat16),
            jax.ShapeDtypeStruct((B, B), jnp.float32),
        ),
        in_specs=[pl.BlockSpec(memory_space=pltpu.SMEM), vmem, vmem],
        out_specs=(vmem, vmem),
        compiler_params=pltpu.CompilerParams(vmem_limit_bytes=4 * MIB),
        cost_estimate=pl.CostEstimate(flops=1_000_000, bytes_accessed=200_000, transcendentals=16_000),
        name="prepare",
    )(rank, keys, values)


def split_table(table):
    lane = lax.broadcasted_iota(jnp.int32, table.shape, 1)
    swapped = pltpu.roll(table, B // 2, 1)
    low = lane < B // 2
    return jnp.where(low, table, swapped), jnp.where(low, -swapped, table)


def rotated(u, cosine, sine):
    return u * cosine + pltpu.roll(u, B // 2, 1) * sine


def attention_kernel(
    where_ref, len_ref, q_ref, g_ref, own_ref, z_ref, c_ref, cz_ref, tab_ref,
    qgrad_ref, keep_ref, send_ref,
    k_s, v_s, q_s, g_s, s_s, d_s, m_s, l_s, w_s, dq_s,
):
    rank = where_ref[0]
    slab = rank // 4
    col = rank % 4
    first = (slab - 2) * 4
    scale = B**-0.5

    q_base = rank * B
    q_pos = q_base + lax.broadcasted_iota(jnp.int32, (1, B), 1)
    start = jnp.zeros((1, B), jnp.int32)
    low = jnp.int32(0)
    end = jnp.int32(0)
    for d in range(8):
        end = end + len_ref[0, d]
        start = jnp.where(q_pos >= end, end, start)
        low = jnp.where(q_base >= end, end, low)
    lo = jnp.maximum(low // B - first, 0)
    hi = 9 + col

    for source, ref in ((0, own_ref), (1, c_ref), (2, z_ref), (3, cz_ref)):
        column = col ^ source
        for b in range(3):
            at = pl.ds(pl.multiple_of(((2 - b) * 4 + column) * B, B), B)
            k_s[at, :] = ref[b * B : (b + 1) * B, :B]
            v_s[at, :] = ref[b * B : (b + 1) * B, B:]

    cosine, sine = split_table(tab_ref[...])
    for h in range(4):
        u = q_ref[:, h * B : (h + 1) * B].astype(jnp.float32)
        q_s[h * B : (h + 1) * B, :] = rotated(u, cosine, sine).astype(jnp.bfloat16)
        g_s[h * B : (h + 1) * B, :] = g_ref[:, h * B : (h + 1) * B]

    m_s[...] = jnp.full(m_s.shape, NEG, jnp.float32)
    l_s[...] = jnp.zeros(l_s.shape, jnp.float32)
    w_s[...] = jnp.zeros(w_s.shape, jnp.float32)
    dq_s[...] = jnp.zeros(dq_s.shape, jnp.float32)
    keep_ref[...] = jnp.zeros(keep_ref.shape, keep_ref.dtype)
    send_ref[...] = jnp.zeros(send_ref.shape, send_ref.dtype)

    pair_lo = lo // 2
    pair_hi = (hi + 1) // 2

    def rows_of(pair):
        return pl.ds(pl.multiple_of(pair * 2 * B, 2 * B), 2 * B)

    def scores(pair, carry):
        at = rows_of(pair)
        s = dot(k_s[at, :], q_s[...], NT) * scale
        d_s[at, :] = dot(v_s[at, :], g_s[...], NT)
        key_pos = (first + 2 * pair) * B + lax.broadcasted_iota(jnp.int32, (2 * B, B), 0)
        allowed = (key_pos <= q_pos) & (key_pos >= start)
        for h in range(4):
            part = jnp.where(allowed, s[:, h * B : (h + 1) * B], NEG)
            s_s[at, h * B : (h + 1) * B] = part
            m_s[:, h * B : (h + 1) * B] = jnp.maximum(
                m_s[:, h * B : (h + 1) * B], jnp.max(part.reshape(32, 8, B), axis=0)
            )
        return carry

    lax.fori_loop(pair_lo, pair_hi, scores, 0)
    top = jnp.max(m_s[...], axis=0, keepdims=True)

    def weights(pair, carry):
        at = rows_of(pair)
        p = jnp.exp(s_s[at, :] - top)
        s_s[at, :] = p
        l_s[...] += jnp.sum(p.reshape(32, 8, 4 * B), axis=0)
        w_s[...] += jnp.sum((p * d_s[at, :]).reshape(32, 8, 4 * B), axis=0)
        return carry

    lax.fori_loop(pair_lo, pair_hi, weights, 0)
    inverse = 1.0 / jnp.sum(l_s[...], axis=0, keepdims=True)
    delta = jnp.sum(w_s[...], axis=0, keepdims=True) * inverse

    def gradients(pair, carry):
        at = rows_of(pair)
        p = s_s[at, :] * inverse
        ds = (p * (d_s[at, :] - delta)).astype(jnp.bfloat16)
        dv = dot(p.astype(jnp.bfloat16), g_s[...], NN)
        dk = dot(ds, q_s[...], NN) * scale
        dq_s[...] += dot(k_s[at, :], ds, TN)
        for i in range(2):
            block = 2 * pair + i
            part = slice(i * B, (i + 1) * B)
            relative = (block % 4) ^ col
            out_at = pl.ds(pl.multiple_of(((relative // 2) * 3 + 2 - block // 4) * B, B), B)

            @pl.when(relative % 2 == 0)
            def _():
                keep_ref[out_at, :B] = dk[part]
                keep_ref[out_at, B:] = dv[part]

            @pl.when(relative % 2 == 1)
            def _():
                send_ref[out_at, :B] = dk[part].astype(jnp.bfloat16)
                send_ref[out_at, B:] = dv[part].astype(jnp.bfloat16)

        return carry

    lax.fori_loop(pair_lo, pair_hi, gradients, 0)
    for h in range(4):
        u = dq_s[:, h * B : (h + 1) * B].T * scale
        qgrad_ref[:, h * B : (h + 1) * B] = rotated(u, cosine, -sine).astype(jnp.bfloat16)


def attention(rank, lengths, q, g, own, z, c, cz, table):
    vmem = pl.BlockSpec(memory_space=pltpu.VMEM)
    smem = pl.BlockSpec(memory_space=pltpu.SMEM)
    rows = WINDOW * B
    return pl.pallas_call(
        attention_kernel,
        out_shape=(
            jax.ShapeDtypeStruct((B, 4 * B), jnp.bfloat16),
            jax.ShapeDtypeStruct((6 * B, 2 * B), jnp.float32),
            jax.ShapeDtypeStruct((6 * B, 2 * B), jnp.bfloat16),
        ),
        in_specs=[smem, smem] + [vmem] * 7,
        out_specs=(vmem, vmem, vmem),
        scratch_shapes=[
            pltpu.VMEM((rows, B), jnp.bfloat16),
            pltpu.VMEM((rows, B), jnp.bfloat16),
            pltpu.VMEM((4 * B, B), jnp.bfloat16),
            pltpu.VMEM((4 * B, B), jnp.bfloat16),
            pltpu.VMEM((rows, 4 * B), jnp.float32),
            pltpu.VMEM((rows, 4 * B), jnp.float32),
            pltpu.VMEM((8, 4 * B), jnp.float32),
            pltpu.VMEM((8, 4 * B), jnp.float32),
            pltpu.VMEM((8, 4 * B), jnp.float32),
            pltpu.VMEM((B, 4 * B), jnp.float32),
        ],
        compiler_params=pltpu.CompilerParams(vmem_limit_bytes=16 * MIB),
        cost_estimate=pl.CostEstimate(flops=755_000_000, bytes_accessed=6_000_000, transcendentals=590_000),
        name="attention",
    )(rank, lengths, q, g, own, z, c, cz, table)


def slices_kernel(where_ref, x_ref, o0, o1, o2, o3, turned):
    slab = where_ref[0] // 4
    for i in range(32):
        turned[i * B : (i + 1) * B, :] = x_ref[:, i * B : (i + 1) * B].T
    for k, out in enumerate((o0, o1, o2, o3)):
        target = (slab + k) % 4
        for dp in range(16):
            at = pl.ds(pl.multiple_of(dp * 256 + target * 64, 64), 64)
            out[dp * 64 : (dp + 1) * 64, :] = turned[at, :]


def slices(rank, x):
    vmem = pl.BlockSpec(memory_space=pltpu.VMEM)
    return pl.pallas_call(
        slices_kernel,
        out_shape=[jax.ShapeDtypeStruct((1024, B), jnp.bfloat16)] * 4,
        in_specs=[pl.BlockSpec(memory_space=pltpu.SMEM), vmem],
        out_specs=[vmem] * 4,
        scratch_shapes=[pltpu.VMEM((4096, B), jnp.bfloat16)],
        compiler_params=pltpu.CompilerParams(vmem_limit_bytes=8 * MIB),
        cost_estimate=pl.CostEstimate(flops=0, bytes_accessed=2_000_000, transcendentals=0),
        name="slices",
    )(rank, x)


def weight_kernel(where_ref, x0, x1, x2, x3, g0, g1, g2, g3, keep_ref, send_ref, acc):
    core = where_ref[0] % 2
    total = dot(x0[...], g0[...], NN)
    for x, g in ((x1, g1), (x2, g2), (x3, g3)):
        total = total + dot(x[...], g[...], NN)
    acc[...] = total
    for i in range(32):
        mine = pl.ds(pl.multiple_of(i * 32 + core * 16, 16), 16)
        other = pl.ds(pl.multiple_of(i * 32 + (1 - core) * 16, 16), 16)
        keep_ref[i * 16 : (i + 1) * 16, :] = acc[mine, :]
        send_ref[i * 16 : (i + 1) * 16, :] = acc[other, :].astype(jnp.bfloat16)


def weight_part(rank, xs, gs):
    vmem = pl.BlockSpec(memory_space=pltpu.VMEM)
    return pl.pallas_call(
        weight_kernel,
        out_shape=(
            jax.ShapeDtypeStruct((512, 256), jnp.float32),
            jax.ShapeDtypeStruct((512, 256), jnp.bfloat16),
        ),
        in_specs=[pl.BlockSpec(memory_space=pltpu.SMEM)] + [vmem] * 8,
        out_specs=(vmem, vmem),
        scratch_shapes=[pltpu.VMEM((1024, 256), jnp.float32)],
        compiler_params=pltpu.CompilerParams(vmem_limit_bytes=12 * MIB),
        cost_estimate=pl.CostEstimate(flops=268_000_000, bytes_accessed=2_000_000, transcendentals=0),
        name="weight",
    )(rank, *xs, *gs)


def compute(layer_input, query_states, key_states, value_states, output_grad, doc_lengths):
    rank = lax.axis_index("ctx").astype(jnp.int32)
    where = rank[None]

    def back(array, slabs):
        pairs = [(i, i + 4 * slabs) for i in range(16) if i + 4 * slabs < 16]
        return lax.ppermute(array, "ctx", pairs)

    def ahead(array, slabs):
        pairs = [(i, i - 4 * slabs) for i in range(16) if i >= 4 * slabs]
        return lax.ppermute(array, "ctx", pairs)

    def around(array, slabs):
        return lax.ppermute(array, "ctx", [(i, (i + 4 * slabs) % 16) for i in range(16)])

    def swap(array, bit):
        return lax.ppermute(array, "ctx", [(i, i ^ bit) for i in range(16)])

    kv, table = prepare(where, key_states[0], value_states[0])
    near = back(kv, 1)
    far = back(kv, 2)
    own = jnp.concatenate([kv, near, far], 0)
    from_z = swap(own, 2)
    from_c = swap(own, 1)
    from_cz = swap(from_z, 1)

    xs = slices(where, layer_input[0])
    shared = [xs[0]]
    for k in (1, 2, 3):
        shared.append(around(xs[k], k))
    xs = shared

    query_grad, keep, send = attention(
        where, doc_lengths, query_states[0], output_grad[0], own, from_z, from_c, from_cz, table
    )

    both = keep + swap(send, 1).astype(jnp.float32)
    column = both[: 3 * B] + swap(both[3 * B :].astype(jnp.bfloat16), 2).astype(jnp.float32)
    low = column.astype(jnp.bfloat16)
    total = (
        column[:B]
        + ahead(low[B : 2 * B], 1).astype(jnp.float32)
        + ahead(low[2 * B :], 2).astype(jnp.float32)
    )
    half = B // 2
    cosine, sine = table[:, :half], table[:, half:]
    u1, u2 = total[:, :half], total[:, half:B]
    grads = jnp.concatenate(
        [u1 * cosine + u2 * sine, u2 * cosine - u1 * sine, total[:, B:]], 1
    ).astype(jnp.bfloat16)

    gs = [grads] + [around(grads, k) for k in (1, 2, 3)]
    part, part_send = weight_part(where, xs, gs)
    part = part + swap(part_send, 1).astype(jnp.float32)
    blocks = part.astype(jnp.bfloat16).reshape(32, 16, 256)
    groups = [
        [dp * 16 + slab * 4 + z * 2 + core for dp in range(16) for z in range(2)]
        for slab in range(4)
        for core in range(2)
    ]
    arrived = lax.all_to_all(
        blocks, ("dp", "ctx"), split_axis=0, concat_axis=0, tiled=True, axis_index_groups=groups
    )
    weight_grad = jnp.sum(arrived.astype(jnp.float32), axis=0)
    return query_grad[None], grads[None, :, :B], grads[None, :, B:], weight_grad


def solution(mesh):
    split = P("dp", "ctx", None)
    return jax.shard_map(
        compute,
        mesh=mesh,
        in_specs=(split,) * 5 + (P("dp", None),),
        out_specs=(split, split, split, P(("dp", "ctx"), None)),
        check_vma=False,
    )
```

```python
import math

import jax
import jax.numpy as jnp
from jax import lax
from jax.experimental import pallas as pl
from jax.experimental.pallas import tpu as pltpu
from jax.sharding import PartitionSpec as P


ROPE_BASE = 500000.0
NEG = -1e30
MIB = 1024 * 1024
B = 128
HEADS = 4
HALF = HEADS * 2 * B
NT = (((1,), (1,)), ((), ()))
TN = (((0,), (0,)), ((), ()))
NN = (((1,), (0,)), ((), ()))
SCALE = B**-0.5


VMEM = pl.BlockSpec(memory_space=pltpu.VMEM)
SMEM = pl.BlockSpec(memory_space=pltpu.SMEM)
HBM = pl.BlockSpec(memory_space=pltpu.HBM)


def dot(a, b, dims):
    return lax.dot_general(a, b, dims, preferred_element_type=jnp.float32)


def shape(dims, dtype):
    return jax.ShapeDtypeStruct(dims, dtype)


def rope_table(first):
    half = B // 2
    index = lax.broadcasted_iota(jnp.int32, (1, half), 1).astype(jnp.float32)
    frequency = jnp.exp(index * (-2.0 * math.log(ROPE_BASE) / B))
    position = first + lax.broadcasted_iota(jnp.int32, (B, 1), 0)
    angles = position.astype(jnp.float32) * frequency
    return jnp.concatenate([jnp.cos(angles), jnp.sin(angles)], 1)


def split_table(table):
    lane = lax.broadcasted_iota(jnp.int32, table.shape, 1)
    swapped = pltpu.roll(table, B // 2, 1)
    low = lane < B // 2
    return jnp.where(low, table, swapped), jnp.where(low, -swapped, table)


def rotated(u, cosine, sine):
    return u * cosine + pltpu.roll(u, B // 2, 1) * sine


def rows(index, size=B):
    return pl.ds(pl.multiple_of(index * size, size), size)


def prepare_kernel(where_ref, key_ref, value_ref, query_ref, grad_ref, kv_ref, qg_ref, key_s, query_s, sem):
    copies = [
        pltpu.make_async_copy(key_ref, key_s, sem.at[0]),
        pltpu.make_async_copy(query_ref, query_s, sem.at[1]),
        pltpu.make_async_copy(value_ref, kv_ref.at[:, B:], sem.at[2]),
        pltpu.make_async_copy(grad_ref, qg_ref.at[:, HEADS * B :], sem.at[3]),
    ]
    for copy in copies:
        copy.start()
    cosine, sine = split_table(rope_table(where_ref[0] * B))
    copies[0].wait()
    kv_ref[:, :B] = rotated(key_s[...].astype(jnp.float32), cosine, sine).astype(jnp.bfloat16)
    copies[1].wait()
    for h in range(HEADS):
        part = slice(h * B, (h + 1) * B)
        u = query_s[:, part].astype(jnp.float32)
        qg_ref[:, part] = rotated(u, cosine, sine).astype(jnp.bfloat16)
    copies[2].wait()
    copies[3].wait()


def prepare(rank, keys, values, queries, grads):
    return pl.pallas_call(
        prepare_kernel,
        out_shape=(shape((B, 2 * B), jnp.bfloat16), shape((B, 2 * HEADS * B), jnp.bfloat16)),
        in_specs=[SMEM, HBM, HBM, HBM, HBM],
        out_specs=(VMEM, VMEM),
        scratch_shapes=[
            pltpu.VMEM((B, B), jnp.bfloat16),
            pltpu.VMEM((B, HEADS * B), jnp.bfloat16),
            pltpu.SemaphoreType.DMA((4,)),
        ],
        compiler_params=pltpu.CompilerParams(vmem_limit_bytes=67_043_328 - 360 * 1024),
        cost_estimate=pl.CostEstimate(flops=1_000_000, bytes_accessed=640_000, transcendentals=16_000),
        name="prepare",
    )(rank, keys, values, queries, grads)


def slices_kernel(where_ref, x_ref, o0, o1, o2, o3, tab_ref, x_s, turned, sem):
    copy = pltpu.make_async_copy(x_ref, x_s, sem)
    copy.start()
    rank = where_ref[0]
    slab = rank // 4
    for k in range(4):
        tab_ref[k * B : (k + 1) * B, :] = rope_table(((slab - k + 4) % 4 * 4 + rank % 4) * B)
    copy.wait()
    for i in range(32):
        turned[i * B : (i + 1) * B, :] = x_s[:, i * B : (i + 1) * B].T
    for k, out in enumerate((o0, o1, o2, o3)):
        target = (slab + k) % 4
        for dp in range(16):
            out[dp * 64 : (dp + 1) * 64, :] = turned[rows(dp * 4 + target, 64), :]


def slices(rank, x):
    return pl.pallas_call(
        slices_kernel,
        out_shape=[shape((1024, B), jnp.bfloat16)] * 4 + [shape((4 * B, B), jnp.float32)],
        in_specs=[SMEM, HBM],
        out_specs=[VMEM] * 5,
        scratch_shapes=[
            pltpu.VMEM((B, 4096), jnp.bfloat16),
            pltpu.VMEM((4096, B), jnp.bfloat16),
            pltpu.SemaphoreType.DMA,
        ],
        compiler_params=pltpu.CompilerParams(vmem_limit_bytes=8 * MIB),
        cost_estimate=pl.CostEstimate(flops=0, bytes_accessed=3_000_000, transcendentals=64_000),
        name="slices",
    )(rank, x)


def document_start(len_ref, position):
    start = position * 0
    end = jnp.int32(0)
    for d in range(8):
        end = end + len_ref[0, d]
        start = jnp.where(position >= end, end, start)
    return start


def unit_needed(rank, b, half, lows):
    key_first = (rank - 4 * b) * B
    query_first = (rank // 4 * 4 + 2 * half) * B
    low = jnp.where(half == 0, lows[0], lows[1])
    return (key_first <= query_first + 2 * B - 1) & (key_first + B > low)


def half_lows(len_ref, rank):
    return [document_start(len_ref, (rank // 4 * 4 + 2 * half) * B) for half in range(2)]


def scores_kernel(
    where_ref, len_ref, kv0, kv1, kv2, qg0, qg1, qg2, qg3,
    p_ref, d_ref, q_ref, g_ref, stat_ref,
    k_s, v_s, m_s, l_s, w_s, start_s,
):
    rank = where_ref[0]
    slab, col = rank // 4, rank % 4
    lows = half_lows(len_ref, rank)
    for b, ref in enumerate((kv0, kv1, kv2)):
        k_s[b * B : (b + 1) * B, :] = ref[:, :B]
        v_s[b * B : (b + 1) * B, :] = ref[:, B:]
    for source, ref in enumerate((qg0, qg1, qg2, qg3)):
        column = col ^ source
        for h in range(HEADS):
            at = rows(column // 2 * 8 + h * 2 + column % 2)
            q_ref[at, :] = ref[:, h * B : (h + 1) * B]
            g_ref[at, :] = ref[:, (HEADS + h) * B : (HEADS + h + 1) * B]
    m_s[...] = jnp.full(m_s.shape, NEG, jnp.float32)
    l_s[...] = jnp.zeros(l_s.shape, jnp.float32)
    w_s[...] = jnp.zeros(w_s.shape, jnp.float32)
    start_s[...] = document_start(
        len_ref, slab * 4 * B + lax.broadcasted_iota(jnp.int32, (1, 4 * B), 1)
    )

    def first_pass(unit, carry):
        b, half = unit // 2, unit % 2

        @pl.when(unit_needed(rank, b, half, lows))
        def _():
            keys, queries = rows(b), rows(half, HALF)
            s = dot(k_s[keys, :], q_ref[queries, :], NT) * SCALE
            d_ref[keys, queries] = dot(v_s[keys, :], g_ref[queries, :], NT)
            key_pos = (rank - 4 * b) * B + lax.broadcasted_iota(jnp.int32, (B, 2 * B), 0)
            query_pos = (slab * 4 + 2 * half) * B + lax.broadcasted_iota(jnp.int32, (1, 2 * B), 1)
            allowed = (key_pos <= query_pos) & (key_pos >= start_s[:, rows(half, 2 * B)])
            for h in range(HEADS):
                lanes = rows(half * HEADS + h, 2 * B)
                part = jnp.where(allowed, s[:, h * 2 * B : (h + 1) * 2 * B], NEG)
                p_ref[keys, lanes] = part
                m_s[:, lanes] = jnp.maximum(m_s[:, lanes], jnp.max(part.reshape(16, 8, 2 * B), axis=0))

        return carry

    lax.fori_loop(0, 6, first_pass, 0)
    top = jnp.max(m_s[...], axis=0, keepdims=True)
    stat_ref[0:1, :] = top

    def second_pass(unit, carry):
        b, half = unit // 2, unit % 2

        @pl.when(unit_needed(rank, b, half, lows))
        def _():
            keys, queries = rows(b), rows(half, HALF)
            p = jnp.exp(p_ref[keys, queries] - stat_ref[0:1, queries])
            p_ref[keys, queries] = p
            l_s[:, queries] += jnp.sum(p.reshape(16, 8, HALF), axis=0)
            w_s[:, queries] += jnp.sum((p * d_ref[keys, queries]).reshape(16, 8, HALF), axis=0)

        return carry

    lax.fori_loop(0, 6, second_pass, 0)
    stat_ref[1:2, :] = jnp.sum(l_s[...], axis=0, keepdims=True)
    stat_ref[2:3, :] = jnp.sum(w_s[...], axis=0, keepdims=True)
    stat_ref[3:8, :] = jnp.zeros((5, 2 * HALF), jnp.float32)


def scores(rank, lengths, kvs, qgs):
    wide = (3 * B, 2 * HALF)
    return pl.pallas_call(
        scores_kernel,
        out_shape=(
            shape(wide, jnp.float32),
            shape(wide, jnp.float32),
            shape((2 * HALF, B), jnp.bfloat16),
            shape((2 * HALF, B), jnp.bfloat16),
            shape((8, 2 * HALF), jnp.float32),
        ),
        in_specs=[SMEM, SMEM] + [VMEM] * 7,
        out_specs=(VMEM,) * 5,
        scratch_shapes=[
            pltpu.VMEM((3 * B, B), jnp.bfloat16),
            pltpu.VMEM((3 * B, B), jnp.bfloat16),
            pltpu.VMEM((8, 2 * HALF), jnp.float32),
            pltpu.VMEM((8, 2 * HALF), jnp.float32),
            pltpu.VMEM((8, 2 * HALF), jnp.float32),
            pltpu.VMEM((1, 4 * B), jnp.int32),
        ],
        compiler_params=pltpu.CompilerParams(vmem_limit_bytes=20 * MIB),
        cost_estimate=pl.CostEstimate(flops=400_000_000, bytes_accessed=8_000_000, transcendentals=790_000),
        name="scores",
    )(rank, lengths, *kvs, *qgs)


def gradients_kernel(
    where_ref, len_ref, kv0, kv1, kv2, p_ref, d_ref, q_ref, g_ref, st0, st1, st2, st3,
    keep_ref, send_ref, dq_keep_ref, dq_send_ref,
    k_s, dq_s, f_s, delta_s,
):
    rank = where_ref[0]
    lows = half_lows(len_ref, rank)
    for b, ref in enumerate((kv0, kv1, kv2)):
        k_s[b * B : (b + 1) * B, :] = ref[:, :B]
    tops = [st[0:1, :] for st in (st0, st1, st2, st3)]
    top = jnp.maximum(jnp.maximum(tops[0], tops[1]), jnp.maximum(tops[2], tops[3]))
    factors = [jnp.exp(t - top) for t in tops]
    total = sum(st[1:2, :] * f for st, f in zip((st0, st1, st2, st3), factors))
    weighted = sum(st[2:3, :] * f for st, f in zip((st0, st1, st2, st3), factors))
    inverse = 1.0 / total
    f_s[...] = factors[0] * inverse
    delta_s[...] = weighted * inverse
    keep_ref[...] = jnp.zeros(keep_ref.shape, jnp.float32)
    dq_s[...] = jnp.zeros(dq_s.shape, jnp.float32)

    def one_pass(unit, carry):
        b, half = unit // 2, unit % 2

        @pl.when(unit_needed(rank, b, half, lows))
        def _():
            keys, queries = rows(b), rows(half, HALF)
            p = p_ref[keys, queries] * f_s[:, queries]
            ds = (p * (d_ref[keys, queries] - delta_s[:, queries])).astype(jnp.bfloat16)
            keep_ref[keys, B:] += dot(p.astype(jnp.bfloat16), g_ref[queries, :], NN)
            keep_ref[keys, :B] += dot(ds, q_ref[queries, :], NN) * SCALE
            dq_s[:, queries] += dot(k_s[keys, :], ds, TN)

        return carry

    lax.fori_loop(0, 6, one_pass, 0)
    send_ref[...] = keep_ref[...].astype(jnp.bfloat16)
    z = rank % 4 // 2
    dq_keep_ref[...] = dq_s[:, rows(z, HALF)]
    dq_send_ref[...] = dq_s[:, rows(1 - z, HALF)].astype(jnp.bfloat16)


def gradients(rank, lengths, kvs, p, d, q, g, stats):
    return pl.pallas_call(
        gradients_kernel,
        out_shape=(
            shape((3 * B, 2 * B), jnp.float32),
            shape((3 * B, 2 * B), jnp.bfloat16),
            shape((B, HALF), jnp.float32),
            shape((B, HALF), jnp.bfloat16),
        ),
        in_specs=[SMEM, SMEM] + [VMEM] * 11,
        out_specs=(VMEM,) * 4,
        scratch_shapes=[
            pltpu.VMEM((3 * B, B), jnp.bfloat16),
            pltpu.VMEM((B, 2 * HALF), jnp.float32),
            pltpu.VMEM((1, 2 * HALF), jnp.float32),
            pltpu.VMEM((1, 2 * HALF), jnp.float32),
        ],
        compiler_params=pltpu.CompilerParams(vmem_limit_bytes=20 * MIB),
        cost_estimate=pl.CostEstimate(flops=600_000_000, bytes_accessed=8_000_000, transcendentals=8_000),
        name="gradients",
    )(rank, lengths, *kvs, p, d, q, g, *stats)


def query_fold_kernel(where_ref, keep_ref, arrived_ref, mine_ref, send_ref):
    core = where_ref[0] % 2
    for h in range(HEADS):
        part = slice(h * B, (h + 1) * B)
        mine, other = rows(h * 2 + core), rows(h * 2 + 1 - core)
        mine_ref[:, part] = keep_ref[:, mine] + arrived_ref[:, mine].astype(jnp.float32)
        both = keep_ref[:, other] + arrived_ref[:, other].astype(jnp.float32)
        send_ref[:, part] = both.astype(jnp.bfloat16)


def query_fold(rank, keep, arrived):
    return pl.pallas_call(
        query_fold_kernel,
        out_shape=(shape((B, HEADS * B), jnp.float32), shape((B, HEADS * B), jnp.bfloat16)),
        in_specs=[SMEM, VMEM, VMEM],
        out_specs=(VMEM, VMEM),
        compiler_params=pltpu.CompilerParams(vmem_limit_bytes=4 * MIB),
        cost_estimate=pl.CostEstimate(flops=300_000, bytes_accessed=1_200_000, transcendentals=0),
        name="query_fold",
    )(rank, keep, arrived)


def query_end_kernel(mine_ref, arrived_ref, tab_ref, out_ref):
    cosine, sine = split_table(tab_ref[:B, :])
    for h in range(HEADS):
        part = slice(h * B, (h + 1) * B)
        u = (mine_ref[:, part] + arrived_ref[:, part].astype(jnp.float32)).T * SCALE
        out_ref[:, part] = rotated(u, cosine, -sine).astype(jnp.bfloat16)


def query_end(mine, arrived, table):
    return pl.pallas_call(
        query_end_kernel,
        out_shape=shape((B, HEADS * B), jnp.bfloat16),
        in_specs=[VMEM, VMEM, VMEM],
        out_specs=VMEM,
        compiler_params=pltpu.CompilerParams(vmem_limit_bytes=4 * MIB),
        cost_estimate=pl.CostEstimate(flops=300_000, bytes_accessed=700_000, transcendentals=0),
        name="query_end",
    )(mine, arrived, table)


def weight_kernel(
    where_ref, keep_ref, r1, r2, r3, tab_ref, x0, x1, x2, x3,
    key_ref, value_ref, own_ref, send_c, send_z, send_cz, acc,
):
    column = where_ref[0] % 4
    parts = (keep_ref, r1, r2, r3)
    total = None
    for k, x in enumerate((x0, x1, x2, x3)):
        grad = None
        for b in range(3):
            part = parts[(k - b) % 4][b * B : (b + 1) * B, :].astype(jnp.float32)
            grad = part if grad is None else grad + part
        cosine, sine = split_table(tab_ref[k * B : (k + 1) * B, :])
        key = rotated(grad[:, :B], cosine, -sine).astype(jnp.bfloat16)
        value = grad[:, B:].astype(jnp.bfloat16)
        if k == 0:
            key_ref[...] = key
            value_ref[...] = value
        term = dot(x[...], jnp.concatenate([key, value], 1), NN)
        total = term if total is None else total + term
    acc[...] = total
    for source, out in enumerate((own_ref, send_c, send_z, send_cz)):
        target = column ^ source
        for dp in range(16):
            out[dp * 16 : (dp + 1) * 16, :] = acc[rows(dp * 4 + target, 16), :].astype(out.dtype)


def weight_part(rank, keep, arrived, table, xs):
    return pl.pallas_call(
        weight_kernel,
        out_shape=(
            shape((B, B), jnp.bfloat16),
            shape((B, B), jnp.bfloat16),
            shape((256, 256), jnp.float32),
            shape((256, 256), jnp.bfloat16),
            shape((256, 256), jnp.bfloat16),
            shape((256, 256), jnp.bfloat16),
        ),
        in_specs=[SMEM] + [VMEM] * 9,
        out_specs=(VMEM,) * 6,
        scratch_shapes=[pltpu.VMEM((1024, 256), jnp.float32)],
        compiler_params=pltpu.CompilerParams(vmem_limit_bytes=12 * MIB),
        cost_estimate=pl.CostEstimate(flops=268_000_000, bytes_accessed=3_000_000, transcendentals=0),
        name="weight",
    )(rank, keep, *arrived, table, *xs)


def compute(layer_input, query_states, key_states, value_states, output_grad, doc_lengths):
    where = lax.axis_index("ctx").astype(jnp.int32)[None]

    def permute(array, pairs):
        return lax.ppermute(array, "ctx", pairs)

    def back(array, slabs):
        return permute(array, [(i, i + 4 * slabs) for i in range(16) if i + 4 * slabs < 16])

    def around(array, slabs):
        return permute(array, [(i, (i + 4 * slabs) % 16) for i in range(16)])

    def swap(array, bits):
        return permute(array, [(i, i ^ bits) for i in range(16)])

    kv, qg = prepare(where, key_states[0], value_states[0], query_states[0], output_grad[0])
    qg_z = swap(qg, 2)
    kvs = [kv, back(kv, 1), back(kv, 2)]
    qg_c = swap(qg, 1)
    qg_cz = swap(qg_z, 1)

    *xs, table = slices(where, layer_input[0])
    xs = [xs[0]] + [around(xs[k], k) for k in (1, 2, 3)]

    p, d, q, g, stat = scores(where, doc_lengths, kvs, (qg, qg_c, qg_z, qg_cz))
    stats = [stat] + [swap(stat, bits) for bits in (1, 2, 3)]
    keep, send, dq_keep, dq_send = gradients(where, doc_lengths, kvs, p, d, q, g, stats)

    arrived = [around(send, k) for k in (1, 2, 3)]
    dq_z = swap(dq_send, 2)
    dq_mine, dq_send = query_fold(where, dq_keep, dq_z)
    dq_c = swap(dq_send, 1)
    query_grad = query_end(dq_mine, dq_c, table)

    key_grad, value_grad, own, *sends = weight_part(where, keep, arrived, table, xs)
    for bits, part in zip((1, 2, 3), sends):
        own = own + swap(part, bits).astype(jnp.float32)
    blocks = own.astype(jnp.bfloat16).reshape(16, 16, 256)
    blocks = lax.all_to_all(blocks, "dp", split_axis=0, concat_axis=0, tiled=True)
    weight_grad = jnp.sum(blocks.astype(jnp.float32), axis=0)
    return query_grad[None], key_grad[None], value_grad[None], weight_grad


def solution(mesh):
    split = P("dp", "ctx", None)
    return jax.shard_map(
        compute,
        mesh=mesh,
        in_specs=(split,) * 5 + (P("dp", None),),
        out_specs=(split, split, split, P(("dp", "ctx"), None)),
        check_vma=False,
    )
```

```python
import math

import jax
import jax.numpy as jnp
from jax import lax
from jax.experimental import pallas as pl
from jax.experimental.pallas import tpu as pltpu
from jax.sharding import PartitionSpec as P


ROPE_BASE = 500000.0
NEG = -1e30
MIB = 1024 * 1024
B = 128
HEADS = 4
HALF = HEADS * 2 * B
NT = (((1,), (1,)), ((), ()))
TN = (((0,), (0,)), ((), ()))
NN = (((1,), (0,)), ((), ()))
SCALE = B**-0.5


VMEM = pl.BlockSpec(memory_space=pltpu.VMEM)
SMEM = pl.BlockSpec(memory_space=pltpu.SMEM)
HBM = pl.BlockSpec(memory_space=pltpu.HBM)


def dot(a, b, dims):
    return lax.dot_general(a, b, dims, preferred_element_type=jnp.float32)


def shape(dims, dtype):
    return jax.ShapeDtypeStruct(dims, dtype)


def rope_table(first):
    half = B // 2
    index = lax.broadcasted_iota(jnp.int32, (1, half), 1).astype(jnp.float32)
    frequency = jnp.exp(index * (-2.0 * math.log(ROPE_BASE) / B))
    position = first + lax.broadcasted_iota(jnp.int32, (B, 1), 0)
    angles = position.astype(jnp.float32) * frequency
    return jnp.concatenate([jnp.cos(angles), jnp.sin(angles)], 1)


def split_table(table):
    lane = lax.broadcasted_iota(jnp.int32, table.shape, 1)
    swapped = pltpu.roll(table, B // 2, 1)
    low = lane < B // 2
    return jnp.where(low, table, swapped), jnp.where(low, -swapped, table)


def rotated(u, cosine, sine):
    return u * cosine + pltpu.roll(u, B // 2, 1) * sine


def rows(index, size=B):
    return pl.ds(pl.multiple_of(index * size, size), size)


def prepare_kernel(
    where_ref, key_ref, value_ref, query_ref, grad_ref, x_ref, len_ref,
    kv_ref, qg_ref, x_out, len_out,
    key_s, query_s, sem,
):
    copies = [
        pltpu.make_async_copy(key_ref, key_s, sem.at[0]),
        pltpu.make_async_copy(query_ref, query_s, sem.at[1]),
        pltpu.make_async_copy(value_ref, kv_ref.at[:, B:], sem.at[2]),
        pltpu.make_async_copy(grad_ref, qg_ref.at[:, HEADS * B :], sem.at[3]),
        pltpu.make_async_copy(len_ref, len_out, sem.at[4]),
        pltpu.make_async_copy(x_ref, x_out, sem.at[5]),
    ]
    for copy in copies:
        copy.start()
    cosine, sine = split_table(rope_table(where_ref[0] * B))
    copies[0].wait()
    kv_ref[:, :B] = rotated(key_s[...].astype(jnp.float32), cosine, sine).astype(jnp.bfloat16)
    copies[1].wait()
    for h in range(HEADS):
        part = slice(h * B, (h + 1) * B)
        u = query_s[:, part].astype(jnp.float32)
        qg_ref[:, part] = rotated(u, cosine, sine).astype(jnp.bfloat16)
    for copy in copies[2:]:
        copy.wait()


def prepare(rank, keys, values, queries, grads, x, lengths):
    hbm = [pltpu.with_memory_space_constraint(a, pltpu.HBM) for a in (keys, values, queries, grads, x, lengths)]
    keys, values, queries, grads, x, lengths = hbm
    return pl.pallas_call(
        prepare_kernel,
        out_shape=(
            shape((B, 2 * B), jnp.bfloat16),
            shape((B, 2 * HEADS * B), jnp.bfloat16),
            shape((B, 4096), jnp.bfloat16),
            shape((1, 8), jnp.int32),
        ),
        in_specs=[SMEM] + [HBM] * 6,
        out_specs=(VMEM,) * 4,
        scratch_shapes=[
            pltpu.VMEM((B, B), jnp.bfloat16),
            pltpu.VMEM((B, HEADS * B), jnp.bfloat16),
            pltpu.SemaphoreType.DMA((6,)),
        ],
        compiler_params=pltpu.CompilerParams(vmem_limit_bytes=4 * MIB),
        name="prepare",
    )(rank, keys, values, queries, grads, x, lengths)


def slices_kernel(where_ref, x_ref, o0, o1, o2, o3, turned):
    slab = where_ref[0] // 4
    for i in range(32):
        turned[i * B : (i + 1) * B, :] = x_ref[:, i * B : (i + 1) * B].T
    for k, out in enumerate((o0, o1, o2, o3)):
        target = (slab + k) % 4
        for dp in range(16):
            out[dp * 64 : (dp + 1) * 64, :] = turned[rows(dp * 4 + target, 64), :]


def slices(rank, x):
    return pl.pallas_call(
        slices_kernel,
        out_shape=[shape((1024, B), jnp.bfloat16)] * 4,
        in_specs=[SMEM, VMEM],
        out_specs=[VMEM] * 4,
        scratch_shapes=[pltpu.VMEM((4096, B), jnp.bfloat16)],
        compiler_params=pltpu.CompilerParams(vmem_limit_bytes=8 * MIB),
        cost_estimate=pl.CostEstimate(flops=0, bytes_accessed=2_000_000, transcendentals=0),
        name="slices",
    )(rank, x)


def tables_kernel(where_ref, tab_ref):
    rank = where_ref[0]
    for k in range(4):
        tab_ref[k * B : (k + 1) * B, :] = rope_table(((rank // 4 - k + 4) % 4 * 4 + rank % 4) * B)


def tables(rank):
    return pl.pallas_call(
        tables_kernel,
        out_shape=shape((4 * B, B), jnp.float32),
        in_specs=[SMEM],
        out_specs=VMEM,
        compiler_params=pltpu.CompilerParams(vmem_limit_bytes=4 * MIB),
        cost_estimate=pl.CostEstimate(flops=2_000_000, bytes_accessed=260_000, transcendentals=64_000),
        name="tables",
    )(rank)


def document_start(len_ref, position):
    start = position * 0
    end = jnp.int32(0)
    for d in range(8):
        end = end + len_ref[0, d]
        start = jnp.where(position >= end, end, start)
    return start


def unit_needed(rank, b, half, lows):
    key_first = (rank - 4 * b) * B
    query_first = (rank // 4 * 4 + 2 * half) * B
    low = jnp.where(half == 0, lows[0], lows[1])
    return (key_first <= query_first + 2 * B - 1) & (key_first + B > low)


def half_lows(len_ref, rank):
    return [document_start(len_ref, (rank // 4 * 4 + 2 * half) * B) for half in range(2)]


def scores_kernel(
    where_ref, len_ref, kv0, kv1, kv2, qg0, qg1, qg2, qg3,
    p_ref, d_ref, q_ref, g_ref, stat_ref,
    k_s, v_s, m_s, l_s, w_s, start_s,
):
    rank = where_ref[0]
    slab, col = rank // 4, rank % 4
    lows = half_lows(len_ref, rank)
    for b, ref in enumerate((kv0, kv1, kv2)):
        k_s[b * B : (b + 1) * B, :] = ref[:, :B]
        v_s[b * B : (b + 1) * B, :] = ref[:, B:]
    for source, ref in enumerate((qg0, qg1, qg2, qg3)):
        column = col ^ source
        for h in range(HEADS):
            at = rows(column // 2 * 8 + h * 2 + column % 2)
            q_ref[at, :] = ref[:, h * B : (h + 1) * B]
            g_ref[at, :] = ref[:, (HEADS + h) * B : (HEADS + h + 1) * B]
    m_s[...] = jnp.full(m_s.shape, NEG, jnp.float32)
    l_s[...] = jnp.zeros(l_s.shape, jnp.float32)
    w_s[...] = jnp.zeros(w_s.shape, jnp.float32)
    start_s[...] = document_start(
        len_ref, slab * 4 * B + lax.broadcasted_iota(jnp.int32, (1, 4 * B), 1)
    )

    def first_pass(unit, carry):
        b, half = unit // 2, unit % 2

        @pl.when(unit_needed(rank, b, half, lows))
        def _():
            keys, queries = rows(b), rows(half, HALF)
            s = dot(k_s[keys, :], q_ref[queries, :], NT) * SCALE
            d_ref[keys, queries] = dot(v_s[keys, :], g_ref[queries, :], NT)
            key_pos = (rank - 4 * b) * B + lax.broadcasted_iota(jnp.int32, (B, 2 * B), 0)
            query_pos = (slab * 4 + 2 * half) * B + lax.broadcasted_iota(jnp.int32, (1, 2 * B), 1)
            allowed = (key_pos <= query_pos) & (key_pos >= start_s[:, rows(half, 2 * B)])
            for h in range(HEADS):
                lanes = rows(half * HEADS + h, 2 * B)
                part = jnp.where(allowed, s[:, h * 2 * B : (h + 1) * 2 * B], NEG)
                p_ref[keys, lanes] = part
                m_s[:, lanes] = jnp.maximum(m_s[:, lanes], jnp.max(part.reshape(16, 8, 2 * B), axis=0))

        return carry

    lax.fori_loop(0, 6, first_pass, 0)
    top = jnp.max(m_s[...], axis=0, keepdims=True)
    stat_ref[0:1, :] = top

    def second_pass(unit, carry):
        b, half = unit // 2, unit % 2

        @pl.when(unit_needed(rank, b, half, lows))
        def _():
            keys, queries = rows(b), rows(half, HALF)
            p = jnp.exp(p_ref[keys, queries] - stat_ref[0:1, queries])
            p_ref[keys, queries] = p
            l_s[:, queries] += jnp.sum(p.reshape(16, 8, HALF), axis=0)
            w_s[:, queries] += jnp.sum((p * d_ref[keys, queries]).reshape(16, 8, HALF), axis=0)

        return carry

    lax.fori_loop(0, 6, second_pass, 0)
    stat_ref[1:2, :] = jnp.sum(l_s[...], axis=0, keepdims=True)
    stat_ref[2:3, :] = jnp.sum(w_s[...], axis=0, keepdims=True)
    stat_ref[3:4, :] = jnp.zeros((1, 2 * HALF), jnp.float32)


def scores(rank, lengths, kvs, qgs):
    wide = (3 * B, 2 * HALF)
    return pl.pallas_call(
        scores_kernel,
        out_shape=(
            shape(wide, jnp.float32),
            shape(wide, jnp.float32),
            shape((2 * HALF, B), jnp.bfloat16),
            shape((2 * HALF, B), jnp.bfloat16),
            shape((4, 2 * HALF), jnp.float32),
        ),
        in_specs=[SMEM, SMEM] + [VMEM] * 7,
        out_specs=(VMEM,) * 5,
        scratch_shapes=[
            pltpu.VMEM((3 * B, B), jnp.bfloat16),
            pltpu.VMEM((3 * B, B), jnp.bfloat16),
            pltpu.VMEM((8, 2 * HALF), jnp.float32),
            pltpu.VMEM((8, 2 * HALF), jnp.float32),
            pltpu.VMEM((8, 2 * HALF), jnp.float32),
            pltpu.VMEM((1, 4 * B), jnp.int32),
        ],
        compiler_params=pltpu.CompilerParams(vmem_limit_bytes=20 * MIB),
        cost_estimate=pl.CostEstimate(flops=400_000_000, bytes_accessed=8_000_000, transcendentals=790_000),
        name="scores",
    )(rank, lengths, *kvs, *qgs)


def gradients_kernel(
    where_ref, len_ref, kv0, kv1, kv2, p_ref, d_ref, q_ref, g_ref, st0, st1, st2, st3,
    keep_ref, send_ref, dq_keep_ref, dq_send_ref,
    k_s, dq_s, f_s, delta_s,
):
    rank = where_ref[0]
    lows = half_lows(len_ref, rank)
    for b, ref in enumerate((kv0, kv1, kv2)):
        k_s[b * B : (b + 1) * B, :] = ref[:, :B]
    tops = [st[0:1, :] for st in (st0, st1, st2, st3)]
    top = jnp.maximum(jnp.maximum(tops[0], tops[1]), jnp.maximum(tops[2], tops[3]))
    factors = [jnp.exp(t - top) for t in tops]
    total = sum(st[1:2, :] * f for st, f in zip((st0, st1, st2, st3), factors))
    weighted = sum(st[2:3, :] * f for st, f in zip((st0, st1, st2, st3), factors))
    inverse = 1.0 / total
    f_s[...] = factors[0] * inverse
    delta_s[...] = weighted * inverse
    keep_ref[...] = jnp.zeros(keep_ref.shape, jnp.float32)
    dq_s[...] = jnp.zeros(dq_s.shape, jnp.float32)

    def one_pass(unit, carry):
        b, half = unit // 2, unit % 2

        @pl.when(unit_needed(rank, b, half, lows))
        def _():
            keys, queries = rows(b), rows(half, HALF)
            p = p_ref[keys, queries] * f_s[:, queries]
            ds = (p * (d_ref[keys, queries] - delta_s[:, queries])).astype(jnp.bfloat16)
            keep_ref[keys, B:] += dot(p.astype(jnp.bfloat16), g_ref[queries, :], NN)
            keep_ref[keys, :B] += dot(ds, q_ref[queries, :], NN) * SCALE
            dq_s[:, queries] += dot(k_s[keys, :], ds, TN)

        return carry

    lax.fori_loop(0, 6, one_pass, 0)
    send_ref[...] = keep_ref[...].astype(jnp.bfloat16)
    z = rank % 4 // 2
    dq_keep_ref[...] = dq_s[:, rows(z, HALF)]
    dq_send_ref[...] = dq_s[:, rows(1 - z, HALF)].astype(jnp.bfloat16)


def gradients(rank, lengths, kvs, p, d, q, g, stats):
    return pl.pallas_call(
        gradients_kernel,
        out_shape=(
            shape((3 * B, 2 * B), jnp.float32),
            shape((3 * B, 2 * B), jnp.bfloat16),
            shape((B, HALF), jnp.float32),
            shape((B, HALF), jnp.bfloat16),
        ),
        in_specs=[SMEM, SMEM] + [VMEM] * 11,
        out_specs=(VMEM,) * 4,
        scratch_shapes=[
            pltpu.VMEM((3 * B, B), jnp.bfloat16),
            pltpu.VMEM((B, 2 * HALF), jnp.float32),
            pltpu.VMEM((1, 2 * HALF), jnp.float32),
            pltpu.VMEM((1, 2 * HALF), jnp.float32),
        ],
        compiler_params=pltpu.CompilerParams(vmem_limit_bytes=20 * MIB),
        cost_estimate=pl.CostEstimate(flops=600_000_000, bytes_accessed=8_000_000, transcendentals=8_000),
        name="gradients",
    )(rank, lengths, *kvs, p, d, q, g, *stats)


def query_fold_kernel(where_ref, keep_ref, arrived_ref, mine_ref, send_ref):
    core = where_ref[0] % 2
    for h in range(HEADS):
        part = slice(h * B, (h + 1) * B)
        mine, other = rows(h * 2 + core), rows(h * 2 + 1 - core)
        mine_ref[:, part] = keep_ref[:, mine] + arrived_ref[:, mine].astype(jnp.float32)
        both = keep_ref[:, other] + arrived_ref[:, other].astype(jnp.float32)
        send_ref[:, part] = both.astype(jnp.bfloat16)


def query_fold(rank, keep, arrived):
    return pl.pallas_call(
        query_fold_kernel,
        out_shape=(shape((B, HEADS * B), jnp.float32), shape((B, HEADS * B), jnp.bfloat16)),
        in_specs=[SMEM, VMEM, VMEM],
        out_specs=(VMEM, VMEM),
        compiler_params=pltpu.CompilerParams(vmem_limit_bytes=4 * MIB),
        cost_estimate=pl.CostEstimate(flops=300_000, bytes_accessed=1_200_000, transcendentals=0),
        name="query_fold",
    )(rank, keep, arrived)


def query_end_kernel(mine_ref, arrived_ref, tab_ref, out_ref):
    cosine, sine = split_table(tab_ref[:B, :])
    for h in range(HEADS):
        part = slice(h * B, (h + 1) * B)
        u = (mine_ref[:, part] + arrived_ref[:, part].astype(jnp.float32)).T * SCALE
        out_ref[:, part] = rotated(u, cosine, -sine).astype(jnp.bfloat16)


def query_end(mine, arrived, table):
    return pl.pallas_call(
        query_end_kernel,
        out_shape=shape((B, HEADS * B), jnp.bfloat16),
        in_specs=[VMEM, VMEM, VMEM],
        out_specs=VMEM,
        compiler_params=pltpu.CompilerParams(vmem_limit_bytes=4 * MIB),
        cost_estimate=pl.CostEstimate(flops=300_000, bytes_accessed=700_000, transcendentals=0),
        name="query_end",
    )(mine, arrived, table)


def weight_kernel(
    where_ref, keep_ref, r1, r2, r3, tab_ref, x0, x1, x2, x3,
    key_ref, value_ref, own_ref, send_ref, acc,
):
    core = where_ref[0] % 2
    parts = (keep_ref, r1, r2, r3)
    total = None
    for k, x in enumerate((x0, x1, x2, x3)):
        grad = None
        for b in range(3):
            part = parts[(k - b) % 4][b * B : (b + 1) * B, :].astype(jnp.float32)
            grad = part if grad is None else grad + part
        cosine, sine = split_table(tab_ref[k * B : (k + 1) * B, :])
        key = rotated(grad[:, :B], cosine, -sine).astype(jnp.bfloat16)
        value = grad[:, B:].astype(jnp.bfloat16)
        if k == 0:
            key_ref[...] = key
            value_ref[...] = value
        term = dot(x[...], jnp.concatenate([key, value], 1), NN)
        total = term if total is None else total + term
    acc[...] = total
    for i in range(32):
        part = slice(i * 16, (i + 1) * 16)
        own_ref[part, :] = acc[rows(i * 2 + core, 16), :]
        send_ref[part, :] = acc[rows(i * 2 + 1 - core, 16), :].astype(jnp.bfloat16)


def weight_part(rank, keep, arrived, table, xs):
    return pl.pallas_call(
        weight_kernel,
        out_shape=(
            shape((B, B), jnp.bfloat16),
            shape((B, B), jnp.bfloat16),
            shape((512, 256), jnp.float32),
            shape((512, 256), jnp.bfloat16),
        ),
        in_specs=[SMEM] + [VMEM] * 9,
        out_specs=(VMEM,) * 4,
        scratch_shapes=[pltpu.VMEM((1024, 256), jnp.float32)],
        compiler_params=pltpu.CompilerParams(vmem_limit_bytes=12 * MIB),
        cost_estimate=pl.CostEstimate(flops=268_000_000, bytes_accessed=3_000_000, transcendentals=0),
        name="weight",
    )(rank, keep, *arrived, table, *xs)


def compute(layer_input, query_states, key_states, value_states, output_grad, doc_lengths):
    where = lax.axis_index("ctx").astype(jnp.int32)[None]

    def permute(array, pairs):
        return lax.ppermute(array, "ctx", pairs)

    def around(array, slabs):
        return permute(array, [(i, (i + 4 * slabs) % 16) for i in range(16)])

    def swap(array, bits):
        return permute(array, [(i, i ^ bits) for i in range(16)])

    kv, qg, x, lengths = prepare(
        where,
        key_states[0],
        value_states[0],
        query_states[0],
        output_grad[0],
        layer_input[0],
        doc_lengths,
    )
    qg_z = swap(qg, 2)
    kvs = [kv, around(kv, 1), around(kv, 2)]
    qg_c = swap(qg, 1)
    qg_cz = swap(qg_z, 1)

    xs = slices(where, x)
    xs = [xs[0]] + [around(xs[k], k) for k in (1, 2, 3)]

    p, d, q, g, stat = scores(where, lengths, kvs, (qg, qg_c, qg_z, qg_cz))
    stats = [stat] + [swap(stat, bits) for bits in (1, 2, 3)]
    table = tables(where)
    keep, send, dq_keep, dq_send = gradients(where, lengths, kvs, p, d, q, g, stats)

    arrived = [around(send, k) for k in (1, 2, 3)]
    dq_z = swap(dq_send, 2)
    dq_mine, dq_send = query_fold(where, dq_keep, dq_z)
    dq_c = swap(dq_send, 1)
    query_grad = query_end(dq_mine, dq_c, table)

    key_grad, value_grad, own, send = weight_part(where, keep, arrived, table, xs)
    own = own + swap(send, 1).astype(jnp.float32)
    blocks = own.astype(jnp.bfloat16).reshape(32, 16, 256)
    groups = [
        [dp * 16 + slab * 4 + z * 2 + core for dp in range(16) for z in range(2)]
        for slab in range(4)
        for core in range(2)
    ]
    blocks = lax.all_to_all(
        blocks, ("dp", "ctx"), split_axis=0, concat_axis=0, tiled=True, axis_index_groups=groups
    )
    weight_grad = jnp.sum(blocks.astype(jnp.float32), axis=0)
    return query_grad[None], key_grad[None], value_grad[None], weight_grad


def solution(mesh):
    split = P("dp", "ctx", None)
    return jax.shard_map(
        compute,
        mesh=mesh,
        in_specs=(split,) * 5 + (P("dp", None),),
        out_specs=(split, split, split, P(("dp", "ctx"), None)),
        check_vma=False,
    )
```

```python
import math

import jax
import jax.numpy as jnp
from jax import lax
from jax.experimental import pallas as pl
from jax.experimental.pallas import tpu as pltpu
from jax.sharding import PartitionSpec as P


ROPE_BASE = 500000.0
NEG = -1e30
MIB = 1024 * 1024
B = 128
HEADS = 4
HALF = HEADS * 2 * B
NT = (((1,), (1,)), ((), ()))
TN = (((0,), (0,)), ((), ()))
NN = (((1,), (0,)), ((), ()))
SCALE = B**-0.5


VMEM = pl.BlockSpec(memory_space=pltpu.VMEM)
SMEM = pl.BlockSpec(memory_space=pltpu.SMEM)
HBM = pl.BlockSpec(memory_space=pltpu.HBM)


def dot(a, b, dims):
    return lax.dot_general(a, b, dims, preferred_element_type=jnp.float32)


def shape(dims, dtype):
    return jax.ShapeDtypeStruct(dims, dtype)


def rope_table(first):
    half = B // 2
    index = lax.broadcasted_iota(jnp.int32, (1, half), 1).astype(jnp.float32)
    frequency = jnp.exp(index * (-2.0 * math.log(ROPE_BASE) / B))
    position = first + lax.broadcasted_iota(jnp.int32, (B, 1), 0)
    angles = position.astype(jnp.float32) * frequency
    return jnp.concatenate([jnp.cos(angles), jnp.sin(angles)], 1)


def split_table(table):
    lane = lax.broadcasted_iota(jnp.int32, table.shape, 1)
    swapped = pltpu.roll(table, B // 2, 1)
    low = lane < B // 2
    return jnp.where(low, table, swapped), jnp.where(low, -swapped, table)


def rotated(u, cosine, sine):
    return u * cosine + pltpu.roll(u, B // 2, 1) * sine


def rows(index, size=B):
    return pl.ds(pl.multiple_of(index * size, size), size)


def prepare_kernel(
    where_ref, key_ref, value_ref, query_ref, grad_ref, x_ref, len_ref,
    kv_ref, qg_ref, x_out, len_out,
    key_s, query_s, sem,
):
    copies = [
        pltpu.make_async_copy(key_ref, key_s, sem.at[0]),
        pltpu.make_async_copy(query_ref, query_s, sem.at[1]),
        pltpu.make_async_copy(value_ref, kv_ref.at[:, B:], sem.at[2]),
        pltpu.make_async_copy(grad_ref, qg_ref.at[:, HEADS * B :], sem.at[3]),
        pltpu.make_async_copy(len_ref, len_out, sem.at[4]),
        pltpu.make_async_copy(x_ref, x_out, sem.at[5]),
    ]
    for copy in copies:
        copy.start()
    cosine, sine = split_table(rope_table(where_ref[0] * B))
    copies[0].wait()
    kv_ref[:, :B] = rotated(key_s[...].astype(jnp.float32), cosine, sine).astype(jnp.bfloat16)
    copies[1].wait()
    for h in range(HEADS):
        part = slice(h * B, (h + 1) * B)
        u = query_s[:, part].astype(jnp.float32)
        qg_ref[:, part] = rotated(u, cosine, sine).astype(jnp.bfloat16)
    for copy in copies[2:]:
        copy.wait()


def prepare(rank, keys, values, queries, grads, x, lengths):
    hbm = [pltpu.with_memory_space_constraint(a, pltpu.HBM) for a in (keys, values, queries, grads, x, lengths)]
    keys, values, queries, grads, x, lengths = hbm
    return pl.pallas_call(
        prepare_kernel,
        out_shape=(
            shape((B, 2 * B), jnp.bfloat16),
            shape((B, 2 * HEADS * B), jnp.bfloat16),
            shape((B, 4096), jnp.bfloat16),
            shape((1, 8), jnp.int32),
        ),
        in_specs=[SMEM] + [HBM] * 6,
        out_specs=(VMEM,) * 4,
        scratch_shapes=[
            pltpu.VMEM((B, B), jnp.bfloat16),
            pltpu.VMEM((B, HEADS * B), jnp.bfloat16),
            pltpu.SemaphoreType.DMA((6,)),
        ],
        compiler_params=pltpu.CompilerParams(vmem_limit_bytes=4 * MIB),
        name="prepare",
    )(rank, keys, values, queries, grads, x, lengths)


def slices_kernel(where_ref, x_ref, o0, o1, o2, o3, turned):
    slab = where_ref[0] // 4
    for i in range(32):
        turned[i * B : (i + 1) * B, :] = x_ref[:, i * B : (i + 1) * B].T
    for k, out in enumerate((o0, o1, o2, o3)):
        target = (slab + k) % 4
        for dp in range(16):
            out[dp * 64 : (dp + 1) * 64, :] = turned[rows(dp * 4 + target, 64), :]


def slices(rank, x):
    return pl.pallas_call(
        slices_kernel,
        out_shape=[shape((1024, B), jnp.bfloat16)] * 4,
        in_specs=[SMEM, VMEM],
        out_specs=[VMEM] * 4,
        scratch_shapes=[pltpu.VMEM((4096, B), jnp.bfloat16)],
        compiler_params=pltpu.CompilerParams(vmem_limit_bytes=8 * MIB),
        cost_estimate=pl.CostEstimate(flops=0, bytes_accessed=2_000_000, transcendentals=0),
        name="slices",
    )(rank, x)


def tables_kernel(where_ref, tab_ref):
    rank = where_ref[0]
    for k in range(4):
        tab_ref[k * B : (k + 1) * B, :] = rope_table(((rank // 4 - k + 4) % 4 * 4 + rank % 4) * B)


def tables(rank):
    return pl.pallas_call(
        tables_kernel,
        out_shape=shape((4 * B, B), jnp.float32),
        in_specs=[SMEM],
        out_specs=VMEM,
        compiler_params=pltpu.CompilerParams(vmem_limit_bytes=4 * MIB),
        cost_estimate=pl.CostEstimate(flops=2_000_000, bytes_accessed=260_000, transcendentals=64_000),
        name="tables",
    )(rank)


def document_start(len_ref, position):
    start = position * 0
    end = jnp.int32(0)
    for d in range(8):
        end = end + len_ref[0, d]
        start = jnp.where(position >= end, end, start)
    return start


def unit_needed(rank, b, half, lows):
    key_first = (rank - 4 * b) * B
    query_first = (rank // 4 * 4 + 2 * half) * B
    low = jnp.where(half == 0, lows[0], lows[1])
    return (key_first <= query_first + 2 * B - 1) & (key_first + B > low)


def half_lows(len_ref, rank):
    return [document_start(len_ref, (rank // 4 * 4 + 2 * half) * B) for half in range(2)]


def scores_kernel(
    where_ref, len_ref, kv0, kv1, kv2, qg0, qg1, qg2, qg3,
    p_ref, d_ref, q_ref, g_ref, stat_ref,
    k_s, v_s, m_s, l_s, w_s, start_s,
):
    rank = where_ref[0]
    slab, col = rank // 4, rank % 4
    lows = half_lows(len_ref, rank)
    for b, ref in enumerate((kv0, kv1, kv2)):
        k_s[b * B : (b + 1) * B, :] = ref[:, :B]
        v_s[b * B : (b + 1) * B, :] = ref[:, B:]
    for source, ref in enumerate((qg0, qg1, qg2, qg3)):
        column = col ^ source
        for h in range(HEADS):
            at = rows(column // 2 * 8 + h * 2 + column % 2)
            q_ref[at, :] = ref[:, h * B : (h + 1) * B]
            g_ref[at, :] = ref[:, (HEADS + h) * B : (HEADS + h + 1) * B]
    m_s[...] = jnp.full(m_s.shape, NEG, jnp.float32)
    l_s[...] = jnp.zeros(l_s.shape, jnp.float32)
    w_s[...] = jnp.zeros(w_s.shape, jnp.float32)
    start_s[...] = document_start(
        len_ref, slab * 4 * B + lax.broadcasted_iota(jnp.int32, (1, 4 * B), 1)
    )

    def first_pass(unit, carry):
        b, half = unit // 2, unit % 2

        @pl.when(unit_needed(rank, b, half, lows))
        def _():
            keys, queries = rows(b), rows(half, HALF)
            s = dot(k_s[keys, :], q_ref[queries, :], NT) * SCALE
            d_ref[keys, queries] = dot(v_s[keys, :], g_ref[queries, :], NT)
            key_pos = (rank - 4 * b) * B + lax.broadcasted_iota(jnp.int32, (B, 2 * B), 0)
            query_pos = (slab * 4 + 2 * half) * B + lax.broadcasted_iota(jnp.int32, (1, 2 * B), 1)
            allowed = (key_pos <= query_pos) & (key_pos >= start_s[:, rows(half, 2 * B)])
            for h in range(HEADS):
                lanes = rows(half * HEADS + h, 2 * B)
                part = jnp.where(allowed, s[:, h * 2 * B : (h + 1) * 2 * B], NEG)
                p_ref[keys, lanes] = part
                m_s[:, lanes] = jnp.maximum(m_s[:, lanes], jnp.max(part.reshape(16, 8, 2 * B), axis=0))

        return carry

    lax.fori_loop(0, 6, first_pass, 0)
    top = jnp.max(m_s[...], axis=0, keepdims=True)
    stat_ref[0:1, :] = top

    def second_pass(unit, carry):
        b, half = unit // 2, unit % 2

        @pl.when(unit_needed(rank, b, half, lows))
        def _():
            keys, queries = rows(b), rows(half, HALF)
            p = jnp.exp(p_ref[keys, queries] - stat_ref[0:1, queries])
            p_ref[keys, queries] = p
            l_s[:, queries] += jnp.sum(p.reshape(16, 8, HALF), axis=0)
            w_s[:, queries] += jnp.sum((p * d_ref[keys, queries]).reshape(16, 8, HALF), axis=0)

        return carry

    lax.fori_loop(0, 6, second_pass, 0)
    stat_ref[1:2, :] = jnp.sum(l_s[...], axis=0, keepdims=True)
    stat_ref[2:3, :] = jnp.sum(w_s[...], axis=0, keepdims=True)
    stat_ref[3:4, :] = jnp.zeros((1, 2 * HALF), jnp.float32)


def scores(rank, lengths, kvs, qgs):
    wide = (3 * B, 2 * HALF)
    return pl.pallas_call(
        scores_kernel,
        out_shape=(
            shape(wide, jnp.float32),
            shape(wide, jnp.float32),
            shape((2 * HALF, B), jnp.bfloat16),
            shape((2 * HALF, B), jnp.bfloat16),
            shape((4, 2 * HALF), jnp.float32),
        ),
        in_specs=[SMEM, SMEM] + [VMEM] * 7,
        out_specs=(VMEM,) * 5,
        scratch_shapes=[
            pltpu.VMEM((3 * B, B), jnp.bfloat16),
            pltpu.VMEM((3 * B, B), jnp.bfloat16),
            pltpu.VMEM((8, 2 * HALF), jnp.float32),
            pltpu.VMEM((8, 2 * HALF), jnp.float32),
            pltpu.VMEM((8, 2 * HALF), jnp.float32),
            pltpu.VMEM((1, 4 * B), jnp.int32),
        ],
        compiler_params=pltpu.CompilerParams(vmem_limit_bytes=20 * MIB),
        cost_estimate=pl.CostEstimate(flops=400_000_000, bytes_accessed=8_000_000, transcendentals=790_000),
        name="scores",
    )(rank, lengths, *kvs, *qgs)


def gradients_kernel(
    where_ref, len_ref, kv0, kv1, kv2, p_ref, d_ref, q_ref, g_ref, st0, st1, st2, st3,
    keep_ref, send_ref, dq_keep_ref, dq_send_ref,
    k_s, dq_s, f_s, delta_s,
):
    rank = where_ref[0]
    lows = half_lows(len_ref, rank)
    for b, ref in enumerate((kv0, kv1, kv2)):
        k_s[b * B : (b + 1) * B, :] = ref[:, :B]
    tops = [st[0:1, :] for st in (st0, st1, st2, st3)]
    top = jnp.maximum(jnp.maximum(tops[0], tops[1]), jnp.maximum(tops[2], tops[3]))
    factors = [jnp.exp(t - top) for t in tops]
    total = sum(st[1:2, :] * f for st, f in zip((st0, st1, st2, st3), factors))
    weighted = sum(st[2:3, :] * f for st, f in zip((st0, st1, st2, st3), factors))
    inverse = 1.0 / total
    f_s[...] = factors[0] * inverse
    delta_s[...] = weighted * inverse
    keep_ref[...] = jnp.zeros(keep_ref.shape, jnp.float32)
    dq_s[...] = jnp.zeros(dq_s.shape, jnp.float32)

    def one_pass(unit, carry):
        b, half = unit // 2, unit % 2

        @pl.when(unit_needed(rank, b, half, lows))
        def _():
            keys, queries = rows(b), rows(half, HALF)
            p = p_ref[keys, queries] * f_s[:, queries]
            ds = (p * (d_ref[keys, queries] - delta_s[:, queries])).astype(jnp.bfloat16)
            keep_ref[keys, B:] += dot(p.astype(jnp.bfloat16), g_ref[queries, :], NN)
            keep_ref[keys, :B] += dot(ds, q_ref[queries, :], NN) * SCALE
            dq_s[:, queries] += dot(k_s[keys, :], ds, TN)

        return carry

    lax.fori_loop(0, 6, one_pass, 0)
    send_ref[...] = keep_ref[...].astype(jnp.bfloat16)
    z = rank % 4 // 2
    dq_keep_ref[...] = dq_s[:, rows(z, HALF)]
    dq_send_ref[...] = dq_s[:, rows(1 - z, HALF)].astype(jnp.bfloat16)


def gradients(rank, lengths, kvs, p, d, q, g, stats):
    return pl.pallas_call(
        gradients_kernel,
        out_shape=(
            shape((3 * B, 2 * B), jnp.float32),
            shape((3 * B, 2 * B), jnp.bfloat16),
            shape((B, HALF), jnp.float32),
            shape((B, HALF), jnp.bfloat16),
        ),
        in_specs=[SMEM, SMEM] + [VMEM] * 11,
        out_specs=(VMEM,) * 4,
        scratch_shapes=[
            pltpu.VMEM((3 * B, B), jnp.bfloat16),
            pltpu.VMEM((B, 2 * HALF), jnp.float32),
            pltpu.VMEM((1, 2 * HALF), jnp.float32),
            pltpu.VMEM((1, 2 * HALF), jnp.float32),
        ],
        compiler_params=pltpu.CompilerParams(vmem_limit_bytes=20 * MIB),
        cost_estimate=pl.CostEstimate(flops=600_000_000, bytes_accessed=8_000_000, transcendentals=8_000),
        name="gradients",
    )(rank, lengths, *kvs, p, d, q, g, *stats)


def query_fold_kernel(where_ref, keep_ref, arrived_ref, mine_ref, send_ref):
    core = where_ref[0] % 2
    for h in range(HEADS):
        part = slice(h * B, (h + 1) * B)
        mine, other = rows(h * 2 + core), rows(h * 2 + 1 - core)
        mine_ref[:, part] = keep_ref[:, mine] + arrived_ref[:, mine].astype(jnp.float32)
        both = keep_ref[:, other] + arrived_ref[:, other].astype(jnp.float32)
        send_ref[:, part] = both.astype(jnp.bfloat16)


def query_fold(rank, keep, arrived):
    return pl.pallas_call(
        query_fold_kernel,
        out_shape=(shape((B, HEADS * B), jnp.float32), shape((B, HEADS * B), jnp.bfloat16)),
        in_specs=[SMEM, VMEM, VMEM],
        out_specs=(VMEM, VMEM),
        compiler_params=pltpu.CompilerParams(vmem_limit_bytes=4 * MIB),
        cost_estimate=pl.CostEstimate(flops=300_000, bytes_accessed=1_200_000, transcendentals=0),
        name="query_fold",
    )(rank, keep, arrived)


def query_end_kernel(mine_ref, arrived_ref, tab_ref, out_ref):
    cosine, sine = split_table(tab_ref[:B, :])
    for h in range(HEADS):
        part = slice(h * B, (h + 1) * B)
        u = (mine_ref[:, part] + arrived_ref[:, part].astype(jnp.float32)).T * SCALE
        out_ref[:, part] = rotated(u, cosine, -sine).astype(jnp.bfloat16)


def query_end(mine, arrived, table):
    return pl.pallas_call(
        query_end_kernel,
        out_shape=shape((B, HEADS * B), jnp.bfloat16),
        in_specs=[VMEM, VMEM, VMEM],
        out_specs=VMEM,
        compiler_params=pltpu.CompilerParams(vmem_limit_bytes=4 * MIB),
        cost_estimate=pl.CostEstimate(flops=300_000, bytes_accessed=700_000, transcendentals=0),
        name="query_end",
    )(mine, arrived, table)


def weight_kernel(
    where_ref, keep_ref, r1, r2k, r2v, r3, tab_ref, x0, x1, x2, x3,
    key_ref, value_ref, own_ref, send_ref, acc,
):
    core = where_ref[0] % 2

    def part(source, b, lanes):
        at = slice(b * B, (b + 1) * B)
        if source == 2:
            return (r2k, r2v)[lanes][at, :].astype(jnp.float32)
        ref = (keep_ref, r1, None, r3)[source]
        return ref[at, lanes * B : (lanes + 1) * B].astype(jnp.float32)

    grads = []
    for k in range(4):
        key, value = (
            part(k, 0, lanes) + part((k - 1) % 4, 1, lanes) + part((k - 2) % 4, 2, lanes) for lanes in (0, 1)
        )
        cosine, sine = split_table(tab_ref[k * B : (k + 1) * B, :])
        key = rotated(key, cosine, -sine).astype(jnp.bfloat16)
        value = value.astype(jnp.bfloat16)
        if k == 0:
            key_ref[...] = key
            value_ref[...] = value
        grads.append(jnp.concatenate([key, value], 1))
    total = dot(jnp.concatenate([x0[...], x1[...]], 1), jnp.concatenate(grads[:2], 0), NN)
    total = total + dot(jnp.concatenate([x2[...], x3[...]], 1), jnp.concatenate(grads[2:], 0), NN)
    acc[...] = total
    for i in range(32):
        part = slice(i * 16, (i + 1) * 16)
        own_ref[part, :] = acc[rows(i * 2 + core, 16), :]
        send_ref[part, :] = acc[rows(i * 2 + 1 - core, 16), :].astype(jnp.bfloat16)


def weight_part(rank, keep, arrived, table, xs):
    return pl.pallas_call(
        weight_kernel,
        out_shape=(
            shape((B, B), jnp.bfloat16),
            shape((B, B), jnp.bfloat16),
            shape((512, 256), jnp.float32),
            shape((512, 256), jnp.bfloat16),
        ),
        in_specs=[SMEM] + [VMEM] * 10,
        out_specs=(VMEM,) * 4,
        scratch_shapes=[pltpu.VMEM((1024, 256), jnp.float32)],
        compiler_params=pltpu.CompilerParams(vmem_limit_bytes=12 * MIB),
        cost_estimate=pl.CostEstimate(flops=268_000_000, bytes_accessed=3_000_000, transcendentals=0),
        name="weight",
    )(rank, keep, *arrived, table, *xs)


def weight_fold_kernel(own_ref, arrived_ref, out_ref):
    out_ref[...] = (own_ref[...] + arrived_ref[...].astype(jnp.float32)).astype(jnp.bfloat16)


def weight_fold(own, arrived):
    return pl.pallas_call(
        weight_fold_kernel,
        out_shape=pltpu.VMEM((512, 256), jnp.bfloat16),
        in_specs=[VMEM, VMEM],
        out_specs=VMEM,
        compiler_params=pltpu.CompilerParams(vmem_limit_bytes=4 * MIB),
        cost_estimate=pl.CostEstimate(flops=131_072, bytes_accessed=1_000_000, transcendentals=0),
        name="weight_fold",
    )(own, arrived)


def compute(layer_input, query_states, key_states, value_states, output_grad, doc_lengths):
    where = lax.axis_index("ctx").astype(jnp.int32)[None]

    def permute(array, pairs):
        return lax.ppermute(array, "ctx", pairs)

    def around(array, slabs):
        return permute(array, [(i, (i + 4 * slabs) % 16) for i in range(16)])

    def swap(array, bits):
        return permute(array, [(i, i ^ bits) for i in range(16)])

    kv, qg, x, lengths = prepare(
        where,
        key_states[0],
        value_states[0],
        query_states[0],
        output_grad[0],
        layer_input[0],
        doc_lengths,
    )
    qg_z = swap(qg, 2)
    kvs = [kv, around(kv, 1), around(kv, 2)]
    qg_c = swap(qg, 1)
    qg_cz = swap(qg_z, 1)

    xs = slices(where, x)
    xs = [xs[0]] + [around(xs[k], k) for k in (1, 2, 3)]

    p, d, q, g, stat = scores(where, lengths, kvs, (qg, qg_c, qg_z, qg_cz))
    stats = [stat] + [swap(stat, bits) for bits in (1, 2, 3)]
    table = tables(where)
    keep, send, dq_keep, dq_send = gradients(where, lengths, kvs, p, d, q, g, stats)

    one, three = around(send, 1), around(send, 3)
    arrived = [one, around(one[:, :B], 1), around(three[:, B:], 3), three]
    dq_z = swap(dq_send, 2)
    dq_mine, dq_send = query_fold(where, dq_keep, dq_z)
    dq_c = swap(dq_send, 1)
    query_grad = query_end(dq_mine, dq_c, table)

    key_grad, value_grad, own, send = weight_part(where, keep, arrived, table, xs)
    arrived = swap(send, 1)
    blocks = weight_fold(own, arrived).reshape(32, 16, 256)
    groups = [
        [dp * 16 + slab * 4 + z * 2 + core for dp in range(16) for z in range(2)]
        for slab in range(4)
        for core in range(2)
    ]
    blocks = lax.all_to_all(
        blocks, ("dp", "ctx"), split_axis=0, concat_axis=0, tiled=True, axis_index_groups=groups
    )
    weight_grad = jnp.sum(blocks.astype(jnp.float32), axis=0)
    return query_grad[None], key_grad[None], value_grad[None], weight_grad


def solution(mesh):
    split = P("dp", "ctx", None)
    return jax.shard_map(
        compute,
        mesh=mesh,
        in_specs=(split,) * 5 + (P("dp", None),),
        out_specs=(split, split, split, P(("dp", "ctx"), None)),
        check_vma=False,
    )
```

```python
import math

import jax
import jax.numpy as jnp
from jax import lax
from jax.experimental import pallas as pl
from jax.experimental.pallas import tpu as pltpu
from jax.sharding import PartitionSpec as P


ROPE_BASE = 500000.0
NEG = -1e30
MIB = 1024 * 1024
B = 128
HEADS = 4
HALF = HEADS * 2 * B
NT = (((1,), (1,)), ((), ()))
TN = (((0,), (0,)), ((), ()))
NN = (((1,), (0,)), ((), ()))
SCALE = B**-0.5


VMEM = pl.BlockSpec(memory_space=pltpu.VMEM)
SMEM = pl.BlockSpec(memory_space=pltpu.SMEM)
HBM = pl.BlockSpec(memory_space=pltpu.HBM)


def dot(a, b, dims):
    return lax.dot_general(a, b, dims, preferred_element_type=jnp.float32)


def shape(dims, dtype):
    return jax.ShapeDtypeStruct(dims, dtype)


def rope_table(first):
    half = B // 2
    index = lax.broadcasted_iota(jnp.int32, (1, half), 1).astype(jnp.float32)
    frequency = jnp.exp(index * (-2.0 * math.log(ROPE_BASE) / B))
    position = first + lax.broadcasted_iota(jnp.int32, (B, 1), 0)
    angles = position.astype(jnp.float32) * frequency
    return jnp.concatenate([jnp.cos(angles), jnp.sin(angles)], 1)


def split_table(table):
    lane = lax.broadcasted_iota(jnp.int32, table.shape, 1)
    swapped = pltpu.roll(table, B // 2, 1)
    low = lane < B // 2
    return jnp.where(low, table, swapped), jnp.where(low, -swapped, table)


def rotated(u, cosine, sine):
    return u * cosine + pltpu.roll(u, B // 2, 1) * sine


def rows(index, size=B):
    return pl.ds(pl.multiple_of(index * size, size), size)


def prepare_kernel(
    where_ref, key_ref, value_ref, query_ref, grad_ref, x_ref, len_ref,
    kv_ref, qg_ref, x_out, len_out,
    key_s, query_s, sem,
):
    copies = [
        pltpu.make_async_copy(key_ref, key_s, sem.at[0]),
        pltpu.make_async_copy(query_ref, query_s, sem.at[1]),
        pltpu.make_async_copy(value_ref, kv_ref.at[:, B:], sem.at[2]),
        pltpu.make_async_copy(grad_ref, qg_ref.at[:, HEADS * B :], sem.at[3]),
        pltpu.make_async_copy(len_ref, len_out, sem.at[4]),
        pltpu.make_async_copy(x_ref, x_out, sem.at[5]),
    ]
    for copy in copies:
        copy.start()
    cosine, sine = split_table(rope_table(where_ref[0] * B))
    copies[0].wait()
    kv_ref[:, :B] = rotated(key_s[...].astype(jnp.float32), cosine, sine).astype(jnp.bfloat16)
    copies[1].wait()
    for h in range(HEADS):
        part = slice(h * B, (h + 1) * B)
        u = query_s[:, part].astype(jnp.float32)
        qg_ref[:, part] = rotated(u, cosine, sine).astype(jnp.bfloat16)
    for copy in copies[2:]:
        copy.wait()


def prepare(rank, keys, values, queries, grads, x, lengths):
    hbm = [pltpu.with_memory_space_constraint(a, pltpu.HBM) for a in (keys, values, queries, grads, x, lengths)]
    keys, values, queries, grads, x, lengths = hbm
    return pl.pallas_call(
        prepare_kernel,
        out_shape=(
            shape((B, 2 * B), jnp.bfloat16),
            shape((B, 2 * HEADS * B), jnp.bfloat16),
            shape((B, 4096), jnp.bfloat16),
            shape((1, 8), jnp.int32),
        ),
        in_specs=[SMEM] + [HBM] * 6,
        out_specs=(VMEM,) * 4,
        scratch_shapes=[
            pltpu.VMEM((B, B), jnp.bfloat16),
            pltpu.VMEM((B, HEADS * B), jnp.bfloat16),
            pltpu.SemaphoreType.DMA((6,)),
        ],
        compiler_params=pltpu.CompilerParams(vmem_limit_bytes=4 * MIB),
        name="prepare",
    )(rank, keys, values, queries, grads, x, lengths)


def slices_kernel(where_ref, x_ref, o0, o1, o2, o3, turned):
    slab = where_ref[0] // 4
    for i in range(32):
        turned[i * B : (i + 1) * B, :] = x_ref[:, i * B : (i + 1) * B].T
    plan = ((o0, 0, 0, 16), (o1, 1, 0, 16), (o2, 2, 0, 8), (o3, 3, 0, 16), (o3, 2, 8, 16))
    for out, k, low, high in plan:
        base = 1024 - 512 if (k, low) == (2, 8) else 0
        target = (slab + k) % 4
        for dp in range(low, high):
            at = base + dp * 64
            out[at : at + 64, :] = turned[rows(dp * 4 + target, 64), :]


def slices(rank, x):
    return pl.pallas_call(
        slices_kernel,
        out_shape=[shape((size, B), jnp.bfloat16) for size in (1024, 1024, 512, 1536)],
        in_specs=[SMEM, VMEM],
        out_specs=[VMEM] * 4,
        scratch_shapes=[pltpu.VMEM((4096, B), jnp.bfloat16)],
        compiler_params=pltpu.CompilerParams(vmem_limit_bytes=8 * MIB),
        cost_estimate=pl.CostEstimate(flops=0, bytes_accessed=2_000_000, transcendentals=0),
        name="slices",
    )(rank, x)


def tables_kernel(where_ref, tab_ref):
    rank = where_ref[0]
    for k in range(4):
        tab_ref[k * B : (k + 1) * B, :] = rope_table(((rank // 4 - k + 4) % 4 * 4 + rank % 4) * B)


def tables(rank):
    return pl.pallas_call(
        tables_kernel,
        out_shape=shape((4 * B, B), jnp.float32),
        in_specs=[SMEM],
        out_specs=VMEM,
        compiler_params=pltpu.CompilerParams(vmem_limit_bytes=4 * MIB),
        cost_estimate=pl.CostEstimate(flops=2_000_000, bytes_accessed=260_000, transcendentals=64_000),
        name="tables",
    )(rank)


def document_start(len_ref, position):
    start = position * 0
    end = jnp.int32(0)
    for d in range(8):
        end = end + len_ref[0, d]
        start = jnp.where(position >= end, end, start)
    return start


def unit_needed(rank, b, half, lows):
    key_first = (rank - 4 * b) * B
    query_first = (rank // 4 * 4 + 2 * half) * B
    low = jnp.where(half == 0, lows[0], lows[1])
    return (key_first <= query_first + 2 * B - 1) & (key_first + B > low)


def half_lows(len_ref, rank):
    return [document_start(len_ref, (rank // 4 * 4 + 2 * half) * B) for half in range(2)]


def scores_kernel(
    where_ref, len_ref, kv0, kv1, kv2, qg0, qg1, qg2, qg3,
    p_ref, d_ref, q_ref, g_ref, stat_ref,
    k_s, v_s, m_s, l_s, w_s, start_s,
):
    rank = where_ref[0]
    slab, col = rank // 4, rank % 4
    lows = half_lows(len_ref, rank)
    for b, ref in enumerate((kv0, kv1, kv2)):
        k_s[b * B : (b + 1) * B, :] = ref[:, :B]
        v_s[b * B : (b + 1) * B, :] = ref[:, B:]
    for source, ref in enumerate((qg0, qg1, qg2, qg3)):
        column = col ^ source
        for h in range(HEADS):
            at = rows(column // 2 * 8 + h * 2 + column % 2)
            q_ref[at, :] = ref[:, h * B : (h + 1) * B]
            g_ref[at, :] = ref[:, (HEADS + h) * B : (HEADS + h + 1) * B]
    m_s[...] = jnp.full(m_s.shape, NEG, jnp.float32)
    l_s[...] = jnp.zeros(l_s.shape, jnp.float32)
    w_s[...] = jnp.zeros(w_s.shape, jnp.float32)
    start_s[...] = document_start(
        len_ref, slab * 4 * B + lax.broadcasted_iota(jnp.int32, (1, 4 * B), 1)
    )

    def first_pass(unit, carry):
        b, half = unit // 2, unit % 2

        @pl.when(unit_needed(rank, b, half, lows))
        def _():
            keys, queries = rows(b), rows(half, HALF)
            s = dot(k_s[keys, :], q_ref[queries, :], NT) * SCALE
            d_ref[keys, queries] = dot(v_s[keys, :], g_ref[queries, :], NT)
            key_pos = (rank - 4 * b) * B + lax.broadcasted_iota(jnp.int32, (B, 2 * B), 0)
            query_pos = (slab * 4 + 2 * half) * B + lax.broadcasted_iota(jnp.int32, (1, 2 * B), 1)
            allowed = (key_pos <= query_pos) & (key_pos >= start_s[:, rows(half, 2 * B)])
            for h in range(HEADS):
                lanes = rows(half * HEADS + h, 2 * B)
                part = jnp.where(allowed, s[:, h * 2 * B : (h + 1) * 2 * B], NEG)
                p_ref[keys, lanes] = part
                m_s[:, lanes] = jnp.maximum(m_s[:, lanes], jnp.max(part.reshape(16, 8, 2 * B), axis=0))

        return carry

    lax.fori_loop(0, 6, first_pass, 0)
    top = jnp.max(m_s[...], axis=0, keepdims=True)
    stat_ref[0:1, :] = top

    def second_pass(unit, carry):
        b, half = unit // 2, unit % 2

        @pl.when(unit_needed(rank, b, half, lows))
        def _():
            keys, queries = rows(b), rows(half, HALF)
            p = jnp.exp(p_ref[keys, queries] - stat_ref[0:1, queries])
            p_ref[keys, queries] = p
            l_s[:, queries] += jnp.sum(p.reshape(16, 8, HALF), axis=0)
            w_s[:, queries] += jnp.sum((p * d_ref[keys, queries]).reshape(16, 8, HALF), axis=0)

        return carry

    lax.fori_loop(0, 6, second_pass, 0)
    stat_ref[1:2, :] = jnp.sum(l_s[...], axis=0, keepdims=True)
    stat_ref[2:3, :] = jnp.sum(w_s[...], axis=0, keepdims=True)
    stat_ref[3:4, :] = jnp.zeros((1, 2 * HALF), jnp.float32)


def scores(rank, lengths, kvs, qgs):
    wide = (3 * B, 2 * HALF)
    return pl.pallas_call(
        scores_kernel,
        out_shape=(
            shape(wide, jnp.float32),
            shape(wide, jnp.float32),
            shape((2 * HALF, B), jnp.bfloat16),
            shape((2 * HALF, B), jnp.bfloat16),
            shape((4, 2 * HALF), jnp.float32),
        ),
        in_specs=[SMEM, SMEM] + [VMEM] * 7,
        out_specs=(VMEM,) * 5,
        scratch_shapes=[
            pltpu.VMEM((3 * B, B), jnp.bfloat16),
            pltpu.VMEM((3 * B, B), jnp.bfloat16),
            pltpu.VMEM((8, 2 * HALF), jnp.float32),
            pltpu.VMEM((8, 2 * HALF), jnp.float32),
            pltpu.VMEM((8, 2 * HALF), jnp.float32),
            pltpu.VMEM((1, 4 * B), jnp.int32),
        ],
        compiler_params=pltpu.CompilerParams(vmem_limit_bytes=20 * MIB),
        cost_estimate=pl.CostEstimate(flops=400_000_000, bytes_accessed=8_000_000, transcendentals=790_000),
        name="scores",
    )(rank, lengths, *kvs, *qgs)


def gradients_kernel(
    where_ref, len_ref, kv0, kv1, kv2, p_ref, d_ref, q_ref, g_ref, st0, st1, st2, st3,
    keep_ref, send_ref, dq_keep_ref, dq_send_ref,
    k_s, dq_s, f_s, delta_s,
):
    rank = where_ref[0]
    lows = half_lows(len_ref, rank)
    for b, ref in enumerate((kv0, kv1, kv2)):
        k_s[b * B : (b + 1) * B, :] = ref[:, :B]
    tops = [st[0:1, :] for st in (st0, st1, st2, st3)]
    top = jnp.maximum(jnp.maximum(tops[0], tops[1]), jnp.maximum(tops[2], tops[3]))
    factors = [jnp.exp(t - top) for t in tops]
    total = sum(st[1:2, :] * f for st, f in zip((st0, st1, st2, st3), factors))
    weighted = sum(st[2:3, :] * f for st, f in zip((st0, st1, st2, st3), factors))
    inverse = 1.0 / total
    f_s[...] = factors[0] * inverse
    delta_s[...] = weighted * inverse
    keep_ref[...] = jnp.zeros(keep_ref.shape, jnp.float32)
    dq_s[...] = jnp.zeros(dq_s.shape, jnp.float32)

    def one_pass(unit, carry):
        b, half = unit // 2, unit % 2

        @pl.when(unit_needed(rank, b, half, lows))
        def _():
            keys, queries = rows(b), rows(half, HALF)
            p = p_ref[keys, queries] * f_s[:, queries]
            ds = (p * (d_ref[keys, queries] - delta_s[:, queries])).astype(jnp.bfloat16)
            keep_ref[keys, B:] += dot(p.astype(jnp.bfloat16), g_ref[queries, :], NN)
            keep_ref[keys, :B] += dot(ds, q_ref[queries, :], NN) * SCALE
            dq_s[:, queries] += dot(k_s[keys, :], ds, TN)

        return carry

    lax.fori_loop(0, 6, one_pass, 0)
    send_ref[...] = keep_ref[...].astype(jnp.bfloat16)
    z = rank % 4 // 2
    dq_keep_ref[...] = dq_s[:, rows(z, HALF)]
    dq_send_ref[...] = dq_s[:, rows(1 - z, HALF)].astype(jnp.bfloat16)


def gradients(rank, lengths, kvs, p, d, q, g, stats):
    return pl.pallas_call(
        gradients_kernel,
        out_shape=(
            shape((3 * B, 2 * B), jnp.float32),
            shape((3 * B, 2 * B), jnp.bfloat16),
            shape((B, HALF), jnp.float32),
            shape((B, HALF), jnp.bfloat16),
        ),
        in_specs=[SMEM, SMEM] + [VMEM] * 11,
        out_specs=(VMEM,) * 4,
        scratch_shapes=[
            pltpu.VMEM((3 * B, B), jnp.bfloat16),
            pltpu.VMEM((B, 2 * HALF), jnp.float32),
            pltpu.VMEM((1, 2 * HALF), jnp.float32),
            pltpu.VMEM((1, 2 * HALF), jnp.float32),
        ],
        compiler_params=pltpu.CompilerParams(vmem_limit_bytes=20 * MIB),
        cost_estimate=pl.CostEstimate(flops=600_000_000, bytes_accessed=8_000_000, transcendentals=8_000),
        name="gradients",
    )(rank, lengths, *kvs, p, d, q, g, *stats)


def query_fold_kernel(where_ref, keep_ref, arrived_ref, mine_ref, send_ref):
    core = where_ref[0] % 2
    for h in range(HEADS):
        part = slice(h * B, (h + 1) * B)
        mine, other = rows(h * 2 + core), rows(h * 2 + 1 - core)
        mine_ref[:, part] = keep_ref[:, mine] + arrived_ref[:, mine].astype(jnp.float32)
        both = keep_ref[:, other] + arrived_ref[:, other].astype(jnp.float32)
        send_ref[:, part] = both.astype(jnp.bfloat16)


def query_fold(rank, keep, arrived):
    return pl.pallas_call(
        query_fold_kernel,
        out_shape=(shape((B, HEADS * B), jnp.float32), shape((B, HEADS * B), jnp.bfloat16)),
        in_specs=[SMEM, VMEM, VMEM],
        out_specs=(VMEM, VMEM),
        compiler_params=pltpu.CompilerParams(vmem_limit_bytes=4 * MIB),
        cost_estimate=pl.CostEstimate(flops=300_000, bytes_accessed=1_200_000, transcendentals=0),
        name="query_fold",
    )(rank, keep, arrived)


def query_end_kernel(mine_ref, arrived_ref, tab_ref, out_ref):
    cosine, sine = split_table(tab_ref[:B, :])
    for h in range(HEADS):
        part = slice(h * B, (h + 1) * B)
        u = (mine_ref[:, part] + arrived_ref[:, part].astype(jnp.float32)).T * SCALE
        out_ref[:, part] = rotated(u, cosine, -sine).astype(jnp.bfloat16)


def query_end(mine, arrived, table):
    return pl.pallas_call(
        query_end_kernel,
        out_shape=shape((B, HEADS * B), jnp.bfloat16),
        in_specs=[VMEM, VMEM, VMEM],
        out_specs=VMEM,
        compiler_params=pltpu.CompilerParams(vmem_limit_bytes=4 * MIB),
        cost_estimate=pl.CostEstimate(flops=300_000, bytes_accessed=700_000, transcendentals=0),
        name="query_end",
    )(mine, arrived, table)


def weight_kernel(
    where_ref, keep_ref, r1, r2, r3, tab_ref, x0, x1, x2a, x2b, x3,
    key_ref, value_ref, own_ref, send_ref, acc,
):
    core = where_ref[0] % 2

    def part(source, b, lanes):
        at = slice(b * B, (b + 1) * B)
        ref = (keep_ref, r1, r2, r3)[source]
        return ref[at, lanes * B : (lanes + 1) * B].astype(jnp.float32)

    grads = []
    for k in range(4):
        key, value = (
            part(k, 0, lanes) + part((k - 1) % 4, 1, lanes) + part((k - 2) % 4, 2, lanes) for lanes in (0, 1)
        )
        cosine, sine = split_table(tab_ref[k * B : (k + 1) * B, :])
        key = rotated(key, cosine, -sine).astype(jnp.bfloat16)
        value = value.astype(jnp.bfloat16)
        if k == 0:
            key_ref[...] = key
            value_ref[...] = value
        grads.append(jnp.concatenate([key, value], 1))
    total = dot(jnp.concatenate([x0[...], x1[...]], 1), jnp.concatenate(grads[:2], 0), NN)
    x2 = jnp.concatenate([x2a[...], x2b[...]], 0)
    total = total + dot(jnp.concatenate([x2, x3[:1024, :]], 1), jnp.concatenate(grads[2:], 0), NN)
    acc[...] = total
    for i in range(32):
        part = slice(i * 16, (i + 1) * 16)
        own_ref[part, :] = acc[rows(i * 2 + core, 16), :]
        send_ref[part, :] = acc[rows(i * 2 + 1 - core, 16), :].astype(jnp.bfloat16)


def weight_part(rank, keep, arrived, table, xs):
    return pl.pallas_call(
        weight_kernel,
        out_shape=(
            shape((B, B), jnp.bfloat16),
            shape((B, B), jnp.bfloat16),
            shape((512, 256), jnp.float32),
            shape((512, 256), jnp.bfloat16),
        ),
        in_specs=[SMEM] + [VMEM] * 10,
        out_specs=(VMEM,) * 4,
        scratch_shapes=[pltpu.VMEM((1024, 256), jnp.float32)],
        compiler_params=pltpu.CompilerParams(vmem_limit_bytes=12 * MIB),
        cost_estimate=pl.CostEstimate(flops=268_000_000, bytes_accessed=3_000_000, transcendentals=0),
        name="weight",
    )(rank, keep, *arrived, table, *xs)


def weight_fold_kernel(own_ref, arrived_ref, out_ref):
    out_ref[...] = (own_ref[...] + arrived_ref[...].astype(jnp.float32)).astype(jnp.bfloat16)


def weight_fold(own, arrived):
    return pl.pallas_call(
        weight_fold_kernel,
        out_shape=pltpu.VMEM((512, 256), jnp.bfloat16),
        in_specs=[VMEM, VMEM],
        out_specs=VMEM,
        compiler_params=pltpu.CompilerParams(vmem_limit_bytes=4 * MIB),
        cost_estimate=pl.CostEstimate(flops=131_072, bytes_accessed=1_000_000, transcendentals=0),
        name="weight_fold",
    )(own, arrived)


def compute(layer_input, query_states, key_states, value_states, output_grad, doc_lengths):
    where = lax.axis_index("ctx").astype(jnp.int32)[None]

    def permute(array, pairs):
        return lax.ppermute(array, "ctx", pairs)

    def around(array, slabs):
        return permute(array, [(i, (i + 4 * slabs) % 16) for i in range(16)])

    def swap(array, bits):
        return permute(array, [(i, i ^ bits) for i in range(16)])

    kv, qg, x, lengths = prepare(
        where,
        key_states[0],
        value_states[0],
        query_states[0],
        output_grad[0],
        layer_input[0],
        doc_lengths,
    )
    qg_z = swap(qg, 2)
    kvs = [kv, around(kv, 1), around(kv, 2)]
    qg_c = swap(qg, 1)
    qg_cz = swap(qg_z, 1)

    xs = slices(where, x)
    x1, x2, x3 = (around(xs[k], k) for k in (1, 2, 3))
    xs = [xs[0], x1, x2, around(x3[1024:], 3), x3]

    p, d, q, g, stat = scores(where, lengths, kvs, (qg, qg_c, qg_z, qg_cz))
    stats = [stat] + [swap(stat, bits) for bits in (1, 2, 3)]
    table = tables(where)
    keep, send, dq_keep, dq_send = gradients(where, lengths, kvs, p, d, q, g, stats)

    arrived = [around(send, k) for k in (1, 2, 3)]
    dq_z = swap(dq_send, 2)
    dq_mine, dq_send = query_fold(where, dq_keep, dq_z)
    dq_c = swap(dq_send, 1)
    query_grad = query_end(dq_mine, dq_c, table)

    key_grad, value_grad, own, send = weight_part(where, keep, arrived, table, xs)
    arrived = swap(send, 1)
    blocks = weight_fold(own, arrived).reshape(32, 16, 256)
    groups = [
        [dp * 16 + slab * 4 + z * 2 + core for dp in range(16) for z in range(2)]
        for slab in range(4)
        for core in range(2)
    ]
    blocks = lax.all_to_all(
        blocks, ("dp", "ctx"), split_axis=0, concat_axis=0, tiled=True, axis_index_groups=groups
    )
    weight_grad = jnp.sum(blocks.astype(jnp.float32), axis=0)
    return query_grad[None], key_grad[None], value_grad[None], weight_grad


def solution(mesh):
    split = P("dp", "ctx", None)
    return jax.shard_map(
        compute,
        mesh=mesh,
        in_specs=(split,) * 5 + (P("dp", None),),
        out_specs=(split, split, split, P(("dp", "ctx"), None)),
        check_vma=False,
    )
```

```python
import math

import jax
import jax.numpy as jnp
from jax import lax
from jax.experimental import pallas as pl
from jax.experimental.pallas import tpu as pltpu
from jax.sharding import PartitionSpec as P


ROPE_BASE = 500000.0
NEG = -1e30
MIB = 1024 * 1024
B = 128
HEADS = 4
HALF = HEADS * 2 * B
NT = (((1,), (1,)), ((), ()))
TN = (((0,), (0,)), ((), ()))
NN = (((1,), (0,)), ((), ()))
SCALE = B**-0.5
LOG2E = 1.4426950408889634


VMEM = pl.BlockSpec(memory_space=pltpu.VMEM)
SMEM = pl.BlockSpec(memory_space=pltpu.SMEM)
HBM = pl.BlockSpec(memory_space=pltpu.HBM)


def dot(a, b, dims):
    return lax.dot_general(a, b, dims, preferred_element_type=jnp.float32)


def shape(dims, dtype):
    return jax.ShapeDtypeStruct(dims, dtype)


def rope_table(first):
    half = B // 2
    index = lax.broadcasted_iota(jnp.int32, (1, half), 1).astype(jnp.float32)
    frequency = jnp.exp(index * (-2.0 * math.log(ROPE_BASE) / B))
    position = first + lax.broadcasted_iota(jnp.int32, (B, 1), 0)
    angles = position.astype(jnp.float32) * frequency
    return jnp.concatenate([jnp.cos(angles), jnp.sin(angles)], 1)


def split_table(table):
    lane = lax.broadcasted_iota(jnp.int32, table.shape, 1)
    swapped = pltpu.roll(table, B // 2, 1)
    low = lane < B // 2
    return jnp.where(low, table, swapped), jnp.where(low, -swapped, table)


def rotated(u, cosine, sine):
    return u * cosine + pltpu.roll(u, B // 2, 1) * sine


def rows(index, size=B):
    return pl.ds(pl.multiple_of(index * size, size), size)


def prepare_kernel(
    where_ref, key_ref, value_ref, query_ref, grad_ref, x_ref, len_ref,
    kv_ref, qg_ref, x_out, len_out,
    key_s, query_s, sem,
):
    copies = [
        pltpu.make_async_copy(key_ref, key_s, sem.at[0]),
        pltpu.make_async_copy(query_ref, query_s, sem.at[1]),
        pltpu.make_async_copy(value_ref, kv_ref.at[:, B:], sem.at[2]),
        pltpu.make_async_copy(grad_ref, qg_ref.at[:, HEADS * B :], sem.at[3]),
        pltpu.make_async_copy(len_ref, len_out, sem.at[4]),
        pltpu.make_async_copy(x_ref, x_out, sem.at[5]),
    ]
    for copy in copies:
        copy.start()
    cosine, sine = split_table(rope_table(where_ref[0] * B))
    copies[0].wait()
    kv_ref[:, :B] = rotated(key_s[...].astype(jnp.float32), cosine, sine).astype(jnp.bfloat16)
    copies[1].wait()
    for h in range(HEADS):
        part = slice(h * B, (h + 1) * B)
        u = query_s[:, part].astype(jnp.float32)
        qg_ref[:, part] = rotated(u, cosine, sine).astype(jnp.bfloat16)
    for copy in copies[2:]:
        copy.wait()


def prepare(rank, keys, values, queries, grads, x, lengths):
    hbm = [pltpu.with_memory_space_constraint(a, pltpu.HBM) for a in (keys, values, queries, grads, x, lengths)]
    keys, values, queries, grads, x, lengths = hbm
    return pl.pallas_call(
        prepare_kernel,
        out_shape=(
            shape((B, 2 * B), jnp.bfloat16),
            shape((B, 2 * HEADS * B), jnp.bfloat16),
            shape((B, 4096), jnp.bfloat16),
            shape((1, 8), jnp.int32),
        ),
        in_specs=[SMEM] + [HBM] * 6,
        out_specs=(VMEM,) * 4,
        scratch_shapes=[
            pltpu.VMEM((B, B), jnp.bfloat16),
            pltpu.VMEM((B, HEADS * B), jnp.bfloat16),
            pltpu.SemaphoreType.DMA((6,)),
        ],
        compiler_params=pltpu.CompilerParams(vmem_limit_bytes=4 * MIB),
        name="prepare",
    )(rank, keys, values, queries, grads, x, lengths)


def slices_kernel(where_ref, x_ref, o0, o1, o2, o3, turned):
    slab = where_ref[0] // 4
    for i in range(32):
        turned[i * B : (i + 1) * B, :] = x_ref[:, i * B : (i + 1) * B].T
    for k, out in enumerate((o0, o1, o2, o3)):
        target = (slab + k) % 4
        for dp in range(16):
            out[dp * 64 : (dp + 1) * 64, :] = turned[rows(dp * 4 + target, 64), :]


def slices(rank, x):
    return pl.pallas_call(
        slices_kernel,
        out_shape=[shape((1024, B), jnp.bfloat16)] * 4,
        in_specs=[SMEM, VMEM],
        out_specs=[VMEM] * 4,
        scratch_shapes=[pltpu.VMEM((4096, B), jnp.bfloat16)],
        compiler_params=pltpu.CompilerParams(vmem_limit_bytes=8 * MIB),
        cost_estimate=pl.CostEstimate(flops=0, bytes_accessed=2_000_000, transcendentals=0),
        name="slices",
    )(rank, x)


def tables_kernel(where_ref, tab_ref):
    rank = where_ref[0]
    for k in range(4):
        tab_ref[k * B : (k + 1) * B, :] = rope_table(((rank // 4 - k + 4) % 4 * 4 + rank % 4) * B)


def tables(rank):
    return pl.pallas_call(
        tables_kernel,
        out_shape=shape((4 * B, B), jnp.float32),
        in_specs=[SMEM],
        out_specs=VMEM,
        compiler_params=pltpu.CompilerParams(vmem_limit_bytes=4 * MIB),
        cost_estimate=pl.CostEstimate(flops=2_000_000, bytes_accessed=260_000, transcendentals=64_000),
        name="tables",
    )(rank)


def document_start(len_ref, position):
    start = position * 0
    end = jnp.int32(0)
    for d in range(8):
        end = end + len_ref[0, d]
        start = jnp.where(position >= end, end, start)
    return start


def column_keys(kvs):
    return jnp.concatenate([kv[:, :B] for kv in kvs], 0)


def heads_below(ref, first):
    return jnp.concatenate([ref[:, (first + h) * B : (first + h + 1) * B] for h in range(HEADS)], 0)


def scores_kernel(
    where_ref, len_ref, kv0, kv1, kv2, qg0, qg1, qg2, qg3, p_ref, d_ref, stat_ref
):
    rank = where_ref[0]
    slab, col = rank // 4, rank % 4
    keys = column_keys((kv0, kv1, kv2))
    values = jnp.concatenate([kv[:, B:] for kv in (kv0, kv1, kv2)], 0)
    row = lax.broadcasted_iota(jnp.int32, (B, B), 0)
    for source, ref in enumerate((qg0, qg1, qg2, qg3)):
        position = (slab * 4 + (col ^ source)) * B + lax.broadcasted_iota(jnp.int32, (1, B), 1)
        start = document_start(len_ref, position)
        allowed = jnp.concatenate(
            [
                (row <= position - (rank - 4 * b) * B) & (row >= start - (rank - 4 * b) * B)
                for b in range(3)
            ],
            0,
        )
        queries, grads = heads_below(ref, 0), heads_below(ref, HEADS)
        for pair in range(2):
            part = slice(pair * 2 * B, (pair + 1) * 2 * B)
            s = dot(keys, queries[part], NT)
            d = dot(values, grads[part], NT)
            for h in range(2):
                here = slice(h * B, (h + 1) * B)
                lanes = slice((source * HEADS + pair * 2 + h) * B, (source * HEADS + pair * 2 + h + 1) * B)
                masked = jnp.where(allowed, s[:, here], NEG)
                top = jnp.max(masked, axis=0, keepdims=True)
                p = jnp.exp2((masked - top) * (SCALE * LOG2E))
                p_ref[:, lanes] = p
                d_ref[:, lanes] = d[:, here]
                stat_ref[0:1, lanes] = top
                stat_ref[1:2, lanes] = jnp.sum(p, axis=0, keepdims=True)
                stat_ref[2:3, lanes] = jnp.sum(p * d[:, here], axis=0, keepdims=True)
    stat_ref[3:4, :] = jnp.zeros((1, 2 * HALF), jnp.float32)


def scores(rank, lengths, kvs, qgs):
    wide = (3 * B, 2 * HALF)
    return pl.pallas_call(
        scores_kernel,
        out_shape=(
            shape(wide, jnp.float32),
            shape(wide, jnp.float32),
            shape((4, 2 * HALF), jnp.float32),
        ),
        in_specs=[SMEM, SMEM] + [VMEM] * 7,
        out_specs=(VMEM,) * 3,
        compiler_params=pltpu.CompilerParams(vmem_limit_bytes=20 * MIB),
        cost_estimate=pl.CostEstimate(flops=400_000_000, bytes_accessed=8_000_000, transcendentals=790_000),
        name="scores",
    )(rank, lengths, *kvs, *qgs)


def gradients_kernel(
    kv0, kv1, kv2, p_ref, d_ref, qg0, qg1, qg2, qg3, st0, st1, st2, st3,
    keep_ref, send_ref, dq0, dq1, dq2, dq3,
):
    keys = column_keys((kv0, kv1, kv2))
    dk = dv = None
    for source, (ref, out) in enumerate(zip((qg0, qg1, qg2, qg3), (dq0, dq1, dq2, dq3))):
        seen = [
            st[:, (source ^ bits) * HEADS * B : ((source ^ bits) + 1) * HEADS * B]
            for bits, st in enumerate((st0, st1, st2, st3))
        ]
        top = jnp.maximum(
            jnp.maximum(seen[0][0:1], seen[1][0:1]), jnp.maximum(seen[2][0:1], seen[3][0:1])
        )
        factors = [jnp.exp2((st[0:1] - top) * (SCALE * LOG2E)) for st in seen]
        inverse = 1.0 / sum(st[1:2] * f for st, f in zip(seen, factors))
        delta = sum(st[2:3] * f for st, f in zip(seen, factors)) * inverse
        lanes = slice(source * HEADS * B, (source + 1) * HEADS * B)
        p = p_ref[:, lanes] * (factors[0] * inverse)
        ds = (p * (d_ref[:, lanes] - delta)).astype(jnp.bfloat16)
        more_v = dot(p.astype(jnp.bfloat16), heads_below(ref, HEADS), NN)
        more_k = dot(ds, heads_below(ref, 0), NN)
        dv = more_v if dv is None else dv + more_v
        dk = more_k if dk is None else dk + more_k
        out[...] = dot(keys, ds, TN).astype(out.dtype)
    dk = dk * SCALE
    keep_ref[:, :B] = dk
    keep_ref[:, B:] = dv
    send_ref[:, :B] = dk.astype(jnp.bfloat16)
    send_ref[:, B:] = dv.astype(jnp.bfloat16)


def gradients(kvs, p, d, qgs, stats):
    return pl.pallas_call(
        gradients_kernel,
        out_shape=(
            shape((3 * B, 2 * B), jnp.float32),
            shape((3 * B, 2 * B), jnp.bfloat16),
            shape((B, HEADS * B), jnp.float32),
            shape((B, HEADS * B), jnp.bfloat16),
            shape((B, HEADS * B), jnp.bfloat16),
            shape((B, HEADS * B), jnp.bfloat16),
        ),
        in_specs=[VMEM] * 13,
        out_specs=(VMEM,) * 6,
        compiler_params=pltpu.CompilerParams(vmem_limit_bytes=20 * MIB),
        cost_estimate=pl.CostEstimate(flops=600_000_000, bytes_accessed=8_000_000, transcendentals=8_000),
        name="gradients",
    )(*kvs, p, d, *qgs, *stats)


def query_end_kernel(mine_ref, r1, r2, r3, tab_ref, out_ref):
    cosine, sine = split_table(tab_ref[:B, :])
    for h in range(HEADS):
        part = slice(h * B, (h + 1) * B)
        u = mine_ref[:, part]
        for ref in (r1, r2, r3):
            u = u + ref[:, part].astype(jnp.float32)
        out_ref[:, part] = rotated(u.T * SCALE, cosine, -sine).astype(jnp.bfloat16)


def query_end(mine, arrived, table):
    return pl.pallas_call(
        query_end_kernel,
        out_shape=shape((B, HEADS * B), jnp.bfloat16),
        in_specs=[VMEM] * 5,
        out_specs=VMEM,
        compiler_params=pltpu.CompilerParams(vmem_limit_bytes=4 * MIB),
        cost_estimate=pl.CostEstimate(flops=300_000, bytes_accessed=900_000, transcendentals=0),
        name="query_end",
    )(mine, *arrived, table)


def weight_kernel(
    where_ref, keep_ref, r1, r2, r3, tab_ref, x0, x1, x2, x3,
    key_ref, value_ref, own_ref, send_ref, acc,
):
    core = where_ref[0] % 2

    def part(source, b, lanes):
        at = slice(b * B, (b + 1) * B)
        ref = (keep_ref, r1, r2, r3)[source]
        return ref[at, lanes * B : (lanes + 1) * B].astype(jnp.float32)

    grads = []
    for k in range(4):
        key, value = (
            part(k, 0, lanes) + part((k - 1) % 4, 1, lanes) + part((k - 2) % 4, 2, lanes) for lanes in (0, 1)
        )
        cosine, sine = split_table(tab_ref[k * B : (k + 1) * B, :])
        key = rotated(key, cosine, -sine).astype(jnp.bfloat16)
        value = value.astype(jnp.bfloat16)
        if k == 0:
            key_ref[...] = key
            value_ref[...] = value
        grads.append(jnp.concatenate([key, value], 1))
    total = dot(jnp.concatenate([x0[...], x1[...]], 1), jnp.concatenate(grads[:2], 0), NN)
    total = total + dot(jnp.concatenate([x2[...], x3[...]], 1), jnp.concatenate(grads[2:], 0), NN)
    acc[...] = total
    for i in range(32):
        part = slice(i * 16, (i + 1) * 16)
        own_ref[part, :] = acc[rows(i * 2 + core, 16), :]
        send_ref[part, :] = acc[rows(i * 2 + 1 - core, 16), :].astype(jnp.bfloat16)


def weight_part(rank, keep, arrived, table, xs):
    return pl.pallas_call(
        weight_kernel,
        out_shape=(
            shape((B, B), jnp.bfloat16),
            shape((B, B), jnp.bfloat16),
            shape((512, 256), jnp.float32),
            shape((512, 256), jnp.bfloat16),
        ),
        in_specs=[SMEM] + [VMEM] * 9,
        out_specs=(VMEM,) * 4,
        scratch_shapes=[pltpu.VMEM((1024, 256), jnp.float32)],
        compiler_params=pltpu.CompilerParams(vmem_limit_bytes=12 * MIB),
        cost_estimate=pl.CostEstimate(flops=268_000_000, bytes_accessed=3_000_000, transcendentals=0),
        name="weight",
    )(rank, keep, *arrived, table, *xs)


def weight_fold_kernel(own_ref, arrived_ref, out_ref):
    out_ref[...] = (own_ref[...] + arrived_ref[...].astype(jnp.float32)).astype(jnp.bfloat16)


def weight_fold(own, arrived):
    return pl.pallas_call(
        weight_fold_kernel,
        out_shape=pltpu.VMEM((512, 256), jnp.bfloat16),
        in_specs=[VMEM, VMEM],
        out_specs=VMEM,
        compiler_params=pltpu.CompilerParams(vmem_limit_bytes=4 * MIB),
        cost_estimate=pl.CostEstimate(flops=131_072, bytes_accessed=1_000_000, transcendentals=0),
        name="weight_fold",
    )(own, arrived)


def compute(layer_input, query_states, key_states, value_states, output_grad, doc_lengths):
    where = lax.axis_index("ctx").astype(jnp.int32)[None]

    def permute(array, pairs):
        return lax.ppermute(array, "ctx", pairs)

    def around(array, slabs):
        return permute(array, [(i, (i + 4 * slabs) % 16) for i in range(16)])

    def swap(array, bits):
        return permute(array, [(i, i ^ bits) for i in range(16)])

    kv, qg, x, lengths = prepare(
        where,
        key_states[0],
        value_states[0],
        query_states[0],
        output_grad[0],
        layer_input[0],
        doc_lengths,
    )
    qg_z = swap(qg, 2)
    kvs = [kv, around(kv, 1), around(kv, 2)]
    qg_c = swap(qg, 1)
    qg_cz = swap(qg_z, 1)

    xs = slices(where, x)
    xs = [xs[0]] + [around(xs[k], k) for k in (1, 2, 3)]

    qgs = (qg, qg_c, qg_z, qg_cz)
    p, d, stat = scores(where, lengths, kvs, qgs)
    stats = [stat] + [swap(stat, bits) for bits in (1, 2, 3)]
    table = tables(where)
    keep, send, mine, *others = gradients(kvs, p, d, qgs, stats)

    arrived = [around(send, k) for k in (1, 2, 3)]
    query_parts = [swap(part, bits) for bits, part in zip((1, 2, 3), others)]
    query_grad = query_end(mine, query_parts, table)

    key_grad, value_grad, own, send = weight_part(where, keep, arrived, table, xs)
    arrived = swap(send, 1)
    blocks = weight_fold(own, arrived).reshape(32, 16, 256)
    groups = [
        [dp * 16 + slab * 4 + z * 2 + core for dp in range(16) for z in range(2)]
        for slab in range(4)
        for core in range(2)
    ]
    blocks = lax.all_to_all(
        blocks, ("dp", "ctx"), split_axis=0, concat_axis=0, tiled=True, axis_index_groups=groups
    )
    weight_grad = jnp.sum(blocks.astype(jnp.float32), axis=0)
    return query_grad[None], key_grad[None], value_grad[None], weight_grad


def solution(mesh):
    split = P("dp", "ctx", None)
    return jax.shard_map(
        compute,
        mesh=mesh,
        in_specs=(split,) * 5 + (P("dp", None),),
        out_specs=(split, split, split, P(("dp", "ctx"), None)),
        check_vma=False,
    )
```

```python
import math

import jax
import jax.numpy as jnp
from jax import lax
from jax.experimental import pallas as pl
from jax.experimental.pallas import tpu as pltpu
from jax.sharding import PartitionSpec as P


ROPE_BASE = 500000.0
NEG = -1e30
MIB = 1024 * 1024
B = 128
HEADS = 4
HALF = HEADS * 2 * B
NT = (((1,), (1,)), ((), ()))
TN = (((0,), (0,)), ((), ()))
NN = (((1,), (0,)), ((), ()))
SCALE = B**-0.5
LOG2E = 1.4426950408889634


VMEM = pl.BlockSpec(memory_space=pltpu.VMEM)
SMEM = pl.BlockSpec(memory_space=pltpu.SMEM)
HBM = pl.BlockSpec(memory_space=pltpu.HBM)


def dot(a, b, dims):
    return lax.dot_general(a, b, dims, preferred_element_type=jnp.float32)


def shape(dims, dtype):
    return jax.ShapeDtypeStruct(dims, dtype)


def rope_table(first):
    half = B // 2
    index = lax.broadcasted_iota(jnp.int32, (1, half), 1).astype(jnp.float32)
    frequency = jnp.exp(index * (-2.0 * math.log(ROPE_BASE) / B))
    position = first + lax.broadcasted_iota(jnp.int32, (B, 1), 0)
    angles = position.astype(jnp.float32) * frequency
    return jnp.concatenate([jnp.cos(angles), jnp.sin(angles)], 1)


def split_table(table):
    lane = lax.broadcasted_iota(jnp.int32, table.shape, 1)
    swapped = pltpu.roll(table, B // 2, 1)
    low = lane < B // 2
    return jnp.where(low, table, swapped), jnp.where(low, -swapped, table)


def rotated(u, cosine, sine):
    return u * cosine + pltpu.roll(u, B // 2, 1) * sine


def rows(index, size=B):
    return pl.ds(pl.multiple_of(index * size, size), size)


def prepare_kernel(
    where_ref, key_ref, value_ref, query_ref, grad_ref, x_ref, len_ref,
    kv_ref, qg_ref, x_out, len_out,
    key_s, query_s, sem,
):
    copies = [
        pltpu.make_async_copy(key_ref, key_s, sem.at[0]),
        pltpu.make_async_copy(query_ref, query_s, sem.at[1]),
        pltpu.make_async_copy(value_ref, kv_ref.at[:, B:], sem.at[2]),
        pltpu.make_async_copy(grad_ref, qg_ref.at[:, HEADS * B :], sem.at[3]),
        pltpu.make_async_copy(len_ref, len_out, sem.at[4]),
        pltpu.make_async_copy(x_ref, x_out, sem.at[5]),
    ]
    for copy in copies:
        copy.start()
    cosine, sine = split_table(rope_table(where_ref[0] * B))
    copies[0].wait()
    kv_ref[:, :B] = rotated(key_s[...].astype(jnp.float32), cosine, sine).astype(jnp.bfloat16)
    copies[1].wait()
    for h in range(HEADS):
        part = slice(h * B, (h + 1) * B)
        u = query_s[:, part].astype(jnp.float32)
        qg_ref[:, part] = rotated(u, cosine, sine).astype(jnp.bfloat16)
    for copy in copies[2:]:
        copy.wait()


def prepare(rank, keys, values, queries, grads, x, lengths):
    hbm = [pltpu.with_memory_space_constraint(a, pltpu.HBM) for a in (keys, values, queries, grads, x, lengths)]
    keys, values, queries, grads, x, lengths = hbm
    return pl.pallas_call(
        prepare_kernel,
        out_shape=(
            shape((B, 2 * B), jnp.bfloat16),
            shape((B, 2 * HEADS * B), jnp.bfloat16),
            shape((B, 4096), jnp.bfloat16),
            shape((1, 8), jnp.int32),
        ),
        in_specs=[SMEM] + [HBM] * 6,
        out_specs=(VMEM,) * 4,
        scratch_shapes=[
            pltpu.VMEM((B, B), jnp.bfloat16),
            pltpu.VMEM((B, HEADS * B), jnp.bfloat16),
            pltpu.SemaphoreType.DMA((6,)),
        ],
        compiler_params=pltpu.CompilerParams(vmem_limit_bytes=4 * MIB),
        name="prepare",
    )(rank, keys, values, queries, grads, x, lengths)


def slices_kernel(where_ref, x_ref, o0, o1, o2, o3, turned):
    slab = where_ref[0] // 4
    for i in range(32):
        tile = x_ref[:, i * B : (i + 1) * B].T
        for j in range(8):
            to, z, core = i % 2 * 2 + j // 4, j // 2 % 2, j % 2
            at = ((to * 2 + core) * 32 + i // 2 * 2 + z) * 16
            turned[at : at + 16, :] = tile[j * 16 : (j + 1) * 16, :]
    for k, out in enumerate((o0, o1, o2, o3)):
        out[...] = turned[rows((slab + k) % 4, 1024), :]


def slices(rank, x):
    return pl.pallas_call(
        slices_kernel,
        out_shape=[shape((1024, B), jnp.bfloat16)] * 4,
        in_specs=[SMEM, VMEM],
        out_specs=[VMEM] * 4,
        scratch_shapes=[pltpu.VMEM((4096, B), jnp.bfloat16)],
        compiler_params=pltpu.CompilerParams(vmem_limit_bytes=8 * MIB),
        cost_estimate=pl.CostEstimate(flops=0, bytes_accessed=2_000_000, transcendentals=0),
        name="slices",
    )(rank, x)


def tables_kernel(where_ref, tab_ref):
    rank = where_ref[0]
    for k in range(4):
        cosine, sine = split_table(rope_table(((rank // 4 - k + 4) % 4 * 4 + rank % 4) * B))
        tab_ref[k * B : (k + 1) * B, :B] = cosine
        tab_ref[k * B : (k + 1) * B, B:] = sine


def tables(rank):
    return pl.pallas_call(
        tables_kernel,
        out_shape=shape((4 * B, 2 * B), jnp.float32),
        in_specs=[SMEM],
        out_specs=VMEM,
        compiler_params=pltpu.CompilerParams(vmem_limit_bytes=4 * MIB),
        cost_estimate=pl.CostEstimate(flops=2_000_000, bytes_accessed=260_000, transcendentals=64_000),
        name="tables",
    )(rank)


def document_start(len_ref, position):
    start = position * 0
    end = jnp.int32(0)
    for d in range(8):
        end = end + len_ref[0, d]
        start = jnp.where(position >= end, end, start)
    return start


def column_keys(kvs):
    return jnp.concatenate([kv[:, :B] for kv in kvs], 0)


def heads_below(ref, first):
    return jnp.concatenate([ref[:, (first + h) * B : (first + h + 1) * B] for h in range(HEADS)], 0)


def scores_kernel(
    where_ref, len_ref, kv0, kv1, kv2, qg0, qg1, qg2, qg3, p_ref, d_ref, stat_ref
):
    rank = where_ref[0]
    slab, col = rank // 4, rank % 4
    keys = column_keys((kv0, kv1, kv2))
    values = jnp.concatenate([kv[:, B:] for kv in (kv0, kv1, kv2)], 0)
    row = lax.broadcasted_iota(jnp.int32, (B, B), 0)
    for source, ref in enumerate((qg0, qg1, qg2, qg3)):
        position = (slab * 4 + (col ^ source)) * B + lax.broadcasted_iota(jnp.int32, (1, B), 1)
        start = document_start(len_ref, position)
        allowed = jnp.concatenate(
            [
                (row <= position - (rank - 4 * b) * B) & (row >= start - (rank - 4 * b) * B)
                for b in range(3)
            ],
            0,
        )
        queries, grads = heads_below(ref, 0), heads_below(ref, HEADS)
        for pair in range(2):
            part = slice(pair * 2 * B, (pair + 1) * 2 * B)
            s = dot(keys, queries[part], NT)
            d = dot(values, grads[part], NT)
            for h in range(2):
                here = slice(h * B, (h + 1) * B)
                lanes = slice((source * HEADS + pair * 2 + h) * B, (source * HEADS + pair * 2 + h + 1) * B)
                masked = jnp.where(allowed, s[:, here], NEG)
                top = jnp.max(masked, axis=0, keepdims=True)
                p = jnp.exp2((masked - top) * (SCALE * LOG2E))
                p_ref[:, lanes] = p
                d_ref[:, lanes] = d[:, here]
                stat_ref[0:1, lanes] = top
                stat_ref[1:2, lanes] = jnp.sum(p, axis=0, keepdims=True)
                stat_ref[2:3, lanes] = jnp.sum(p * d[:, here], axis=0, keepdims=True)
    stat_ref[3:4, :] = jnp.zeros((1, 2 * HALF), jnp.float32)


def scores(rank, lengths, kvs, qgs):
    wide = (3 * B, 2 * HALF)
    return pl.pallas_call(
        scores_kernel,
        out_shape=(
            shape(wide, jnp.float32),
            shape(wide, jnp.float32),
            shape((4, 2 * HALF), jnp.float32),
        ),
        in_specs=[SMEM, SMEM] + [VMEM] * 7,
        out_specs=(VMEM,) * 3,
        compiler_params=pltpu.CompilerParams(vmem_limit_bytes=20 * MIB),
        cost_estimate=pl.CostEstimate(flops=400_000_000, bytes_accessed=8_000_000, transcendentals=790_000),
        name="scores",
    )(rank, lengths, *kvs, *qgs)


def gradients_kernel(
    kv0, kv1, kv2, p_ref, d_ref, qg0, qg1, qg2, qg3, st0, st1, st2, st3,
    keep_ref, send_ref, dq0, dq1, dq2, dq3,
):
    keys = column_keys((kv0, kv1, kv2))
    dk = dv = None
    for source, (ref, out) in enumerate(zip((qg0, qg1, qg2, qg3), (dq0, dq1, dq2, dq3))):
        seen = [
            st[:, (source ^ bits) * HEADS * B : ((source ^ bits) + 1) * HEADS * B]
            for bits, st in enumerate((st0, st1, st2, st3))
        ]
        top = jnp.maximum(
            jnp.maximum(seen[0][0:1], seen[1][0:1]), jnp.maximum(seen[2][0:1], seen[3][0:1])
        )
        factors = [jnp.exp2((st[0:1] - top) * (SCALE * LOG2E)) for st in seen]
        inverse = 1.0 / sum(st[1:2] * f for st, f in zip(seen, factors))
        delta = sum(st[2:3] * f for st, f in zip(seen, factors)) * inverse
        lanes = slice(source * HEADS * B, (source + 1) * HEADS * B)
        p = p_ref[:, lanes] * (factors[0] * inverse)
        ds = (p * (d_ref[:, lanes] - delta)).astype(jnp.bfloat16)
        more_v = dot(p.astype(jnp.bfloat16), heads_below(ref, HEADS), NN)
        more_k = dot(ds, heads_below(ref, 0), NN)
        dv = more_v if dv is None else dv + more_v
        dk = more_k if dk is None else dk + more_k
        out[...] = dot(keys, ds, TN).astype(out.dtype)
    dk = dk * SCALE
    keep_ref[:, :B] = dk
    keep_ref[:, B:] = dv
    send_ref[:, :B] = dk.astype(jnp.bfloat16)
    send_ref[:, B:] = dv.astype(jnp.bfloat16)


def gradients(kvs, p, d, qgs, stats):
    return pl.pallas_call(
        gradients_kernel,
        out_shape=(
            shape((3 * B, 2 * B), jnp.float32),
            shape((3 * B, 2 * B), jnp.bfloat16),
            shape((B, HEADS * B), jnp.float32),
            shape((B, HEADS * B), jnp.bfloat16),
            shape((B, HEADS * B), jnp.bfloat16),
            shape((B, HEADS * B), jnp.bfloat16),
        ),
        in_specs=[VMEM] * 13,
        out_specs=(VMEM,) * 6,
        compiler_params=pltpu.CompilerParams(vmem_limit_bytes=20 * MIB),
        cost_estimate=pl.CostEstimate(flops=600_000_000, bytes_accessed=8_000_000, transcendentals=8_000),
        name="gradients",
    )(*kvs, p, d, *qgs, *stats)


def query_end_kernel(mine_ref, r1, r2, r3, tab_ref, out_ref):
    cosine, sine = tab_ref[:B, :B], tab_ref[:B, B:]
    for h in range(HEADS):
        part = slice(h * B, (h + 1) * B)
        u = mine_ref[:, part]
        for ref in (r1, r2, r3):
            u = u + ref[:, part].astype(jnp.float32)
        out_ref[:, part] = rotated(u.T * SCALE, cosine, -sine).astype(jnp.bfloat16)


def query_end(mine, arrived, table):
    return pl.pallas_call(
        query_end_kernel,
        out_shape=shape((B, HEADS * B), jnp.bfloat16),
        in_specs=[VMEM] * 5,
        out_specs=VMEM,
        compiler_params=pltpu.CompilerParams(vmem_limit_bytes=4 * MIB),
        cost_estimate=pl.CostEstimate(flops=300_000, bytes_accessed=900_000, transcendentals=0),
        name="query_end",
    )(mine, *arrived, table)


def weight_kernel(
    where_ref, keep_ref, r1, r2, r3, tab_ref, x0, x1, x2, x3,
    key_ref, value_ref, send_ref, g01_ref, g23_ref,
):
    core = where_ref[0] % 2

    def part(source, b, lanes):
        at = slice(b * B, (b + 1) * B)
        ref = (keep_ref, r1, r2, r3)[source]
        return ref[at, lanes * B : (lanes + 1) * B].astype(jnp.float32)

    grads = []
    for k in range(4):
        key, value = (
            part(k, 0, lanes) + part((k - 1) % 4, 1, lanes) + part((k - 2) % 4, 2, lanes) for lanes in (0, 1)
        )
        cosine, sine = tab_ref[k * B : (k + 1) * B, :B], tab_ref[k * B : (k + 1) * B, B:]
        key = rotated(key, cosine, -sine).astype(jnp.bfloat16)
        value = value.astype(jnp.bfloat16)
        if k == 0:
            key_ref[...] = key
            value_ref[...] = value
        grads.append(jnp.concatenate([key, value], 1))
    low, high = jnp.concatenate(grads[:2], 0), jnp.concatenate(grads[2:], 0)
    g01_ref[...] = low
    g23_ref[...] = high
    send_ref[...] = half_of_weight(1 - core, (x0, x1, x2, x3), low, high).astype(jnp.bfloat16)


def half_of_weight(core, xs, low, high):
    at = rows(core, 512)
    total = dot(jnp.concatenate([xs[0][at, :], xs[1][at, :]], 1), low, NN)
    return total + dot(jnp.concatenate([xs[2][at, :], xs[3][at, :]], 1), high, NN)


def own_half_kernel(where_ref, g01_ref, g23_ref, x0, x1, x2, x3, own_ref):
    core = where_ref[0] % 2
    own_ref[...] = half_of_weight(core, (x0, x1, x2, x3), g01_ref[...], g23_ref[...])


def own_half(rank, low, high, xs):
    return pl.pallas_call(
        own_half_kernel,
        out_shape=shape((512, 256), jnp.float32),
        in_specs=[SMEM] + [VMEM] * 6,
        out_specs=VMEM,
        compiler_params=pltpu.CompilerParams(vmem_limit_bytes=12 * MIB),
        cost_estimate=pl.CostEstimate(flops=134_000_000, bytes_accessed=1_800_000, transcendentals=0),
        name="own_half",
    )(rank, low, high, *xs)


def weight_part(rank, keep, arrived, table, xs):
    return pl.pallas_call(
        weight_kernel,
        out_shape=(
            shape((B, B), jnp.bfloat16),
            shape((B, B), jnp.bfloat16),
            shape((512, 256), jnp.bfloat16),
            shape((256, 256), jnp.bfloat16),
            shape((256, 256), jnp.bfloat16),
        ),
        in_specs=[SMEM] + [VMEM] * 9,
        out_specs=(VMEM,) * 5,
        compiler_params=pltpu.CompilerParams(vmem_limit_bytes=12 * MIB),
        cost_estimate=pl.CostEstimate(flops=134_000_000, bytes_accessed=3_000_000, transcendentals=0),
        name="weight",
    )(rank, keep, *arrived, table, *xs)


def weight_fold_kernel(own_ref, arrived_ref, out_ref):
    out_ref[...] = (own_ref[...] + arrived_ref[...].astype(jnp.float32)).astype(jnp.bfloat16)


def weight_fold(own, arrived):
    return pl.pallas_call(
        weight_fold_kernel,
        out_shape=pltpu.VMEM((512, 256), jnp.bfloat16),
        in_specs=[VMEM, VMEM],
        out_specs=VMEM,
        compiler_params=pltpu.CompilerParams(vmem_limit_bytes=4 * MIB),
        cost_estimate=pl.CostEstimate(flops=131_072, bytes_accessed=1_000_000, transcendentals=0),
        name="weight_fold",
    )(own, arrived)


def compute(layer_input, query_states, key_states, value_states, output_grad, doc_lengths):
    where = lax.axis_index("ctx").astype(jnp.int32)[None]

    def permute(array, pairs):
        return lax.ppermute(array, "ctx", pairs)

    def around(array, slabs):
        return permute(array, [(i, (i + 4 * slabs) % 16) for i in range(16)])

    def swap(array, bits):
        return permute(array, [(i, i ^ bits) for i in range(16)])

    kv, qg, x, lengths = prepare(
        where,
        key_states[0],
        value_states[0],
        query_states[0],
        output_grad[0],
        layer_input[0],
        doc_lengths,
    )
    qg_z = swap(qg, 2)
    kvs = [kv, around(kv, 1), around(kv, 2)]
    qg_c = swap(qg, 1)
    qg_cz = swap(qg_z, 1)

    xs = slices(where, x)
    xs = [xs[0]] + [around(xs[k], k) for k in (1, 2, 3)]

    qgs = (qg, qg_c, qg_z, qg_cz)
    p, d, stat = scores(where, lengths, kvs, qgs)
    stats = [stat] + [swap(stat, bits) for bits in (1, 2, 3)]
    table = tables(where)
    keep, send, mine, *others = gradients(kvs, p, d, qgs, stats)

    arrived = [around(send, k) for k in (1, 2, 3)]
    query_parts = [swap(part, bits) for bits, part in zip((1, 2, 3), others)]
    query_grad = query_end(mine, query_parts, table)

    key_grad, value_grad, send, low, high = weight_part(where, keep, arrived, table, xs)
    arrived = swap(send, 1)
    own = own_half(where, low, high, xs)
    blocks = weight_fold(own, arrived).reshape(32, 16, 256)
    groups = [
        [dp * 16 + slab * 4 + z * 2 + core for dp in range(16) for z in range(2)]
        for slab in range(4)
        for core in range(2)
    ]
    blocks = lax.all_to_all(
        blocks, ("dp", "ctx"), split_axis=0, concat_axis=0, tiled=True, axis_index_groups=groups
    )
    weight_grad = jnp.sum(blocks.astype(jnp.float32), axis=0)
    return query_grad[None], key_grad[None], value_grad[None], weight_grad


def solution(mesh):
    split = P("dp", "ctx", None)
    return jax.shard_map(
        compute,
        mesh=mesh,
        in_specs=(split,) * 5 + (P("dp", None),),
        out_specs=(split, split, split, P(("dp", "ctx"), None)),
        check_vma=False,
    )
```

```python
import math

import jax
import jax.numpy as jnp
from jax import lax
from jax.experimental import pallas as pl
from jax.experimental.pallas import tpu as pltpu
from jax.sharding import PartitionSpec as P


ROPE_BASE = 500000.0
NEG = -1e30
MIB = 1024 * 1024
B = 128
HEADS = 4
HALF = HEADS * 2 * B
NT = (((1,), (1,)), ((), ()))
TN = (((0,), (0,)), ((), ()))
NN = (((1,), (0,)), ((), ()))
SCALE = B**-0.5
LOG2E = 1.4426950408889634


VMEM = pl.BlockSpec(memory_space=pltpu.VMEM)
SMEM = pl.BlockSpec(memory_space=pltpu.SMEM)
HBM = pl.BlockSpec(memory_space=pltpu.HBM)


def dot(a, b, dims):
    return lax.dot_general(a, b, dims, preferred_element_type=jnp.float32)


def shape(dims, dtype):
    return jax.ShapeDtypeStruct(dims, dtype)


def rope_table(first):
    half = B // 2
    index = lax.broadcasted_iota(jnp.int32, (1, half), 1).astype(jnp.float32)
    frequency = jnp.exp(index * (-2.0 * math.log(ROPE_BASE) / B))
    position = first + lax.broadcasted_iota(jnp.int32, (B, 1), 0)
    angles = position.astype(jnp.float32) * frequency
    return jnp.concatenate([jnp.cos(angles), jnp.sin(angles)], 1)


def split_table(table):
    lane = lax.broadcasted_iota(jnp.int32, table.shape, 1)
    swapped = pltpu.roll(table, B // 2, 1)
    low = lane < B // 2
    return jnp.where(low, table, swapped), jnp.where(low, -swapped, table)


def rotated(u, cosine, sine):
    return u * cosine + pltpu.roll(u, B // 2, 1) * sine


def rows(index, size=B):
    return pl.ds(pl.multiple_of(index * size, size), size)


def prepare_kernel(
    where_ref, key_ref, value_ref, query_ref, grad_ref, x_ref, len_ref,
    kv_ref, qg_ref, q_out, x_out, len_out,
    key_s, query_s, sem,
):
    copies = [
        pltpu.make_async_copy(key_ref, key_s, sem.at[0]),
        pltpu.make_async_copy(query_ref, query_s, sem.at[1]),
        pltpu.make_async_copy(value_ref, kv_ref.at[:, B:], sem.at[2]),
        pltpu.make_async_copy(grad_ref, qg_ref.at[:, HEADS * B :], sem.at[3]),
        pltpu.make_async_copy(len_ref, len_out, sem.at[4]),
        pltpu.make_async_copy(x_ref, x_out, sem.at[5]),
    ]
    for copy in copies:
        copy.start()
    cosine, sine = split_table(rope_table(where_ref[0] * B))
    copies[0].wait()
    kv_ref[:, :B] = rotated(key_s[...].astype(jnp.float32), cosine, sine).astype(jnp.bfloat16)
    copies[1].wait()
    for h in range(HEADS):
        part = slice(h * B, (h + 1) * B)
        u = query_s[:, part].astype(jnp.float32)
        turned = rotated(u, cosine, sine).astype(jnp.bfloat16)
        qg_ref[:, part] = turned
        q_out[:, part] = turned
    for copy in copies[2:]:
        copy.wait()


def prepare(rank, keys, values, queries, grads, x, lengths):
    hbm = [pltpu.with_memory_space_constraint(a, pltpu.HBM) for a in (keys, values, queries, grads, x, lengths)]
    keys, values, queries, grads, x, lengths = hbm
    return pl.pallas_call(
        prepare_kernel,
        out_shape=(
            shape((B, 2 * B), jnp.bfloat16),
            shape((B, 2 * HEADS * B), jnp.bfloat16),
            shape((B, HEADS * B), jnp.bfloat16),
            shape((B, 4096), jnp.bfloat16),
            shape((1, 8), jnp.int32),
        ),
        in_specs=[SMEM] + [HBM] * 6,
        out_specs=(VMEM,) * 5,
        scratch_shapes=[
            pltpu.VMEM((B, B), jnp.bfloat16),
            pltpu.VMEM((B, HEADS * B), jnp.bfloat16),
            pltpu.SemaphoreType.DMA((6,)),
        ],
        compiler_params=pltpu.CompilerParams(vmem_limit_bytes=4 * MIB),
        name="prepare",
    )(rank, keys, values, queries, grads, x, lengths)


def slices_kernel(where_ref, x_ref, o0, o1, o2, o3, turned):
    slab = where_ref[0] // 4
    for i in range(32):
        tile = x_ref[:, i * B : (i + 1) * B].T
        for j in range(8):
            to, z, core = i % 2 * 2 + j // 4, j // 2 % 2, j % 2
            at = ((to * 2 + core) * 32 + i // 2 * 2 + z) * 16
            turned[at : at + 16, :] = tile[j * 16 : (j + 1) * 16, :]
    for k, out in enumerate((o0, o1, o2, o3)):
        out[...] = turned[rows((slab + k) % 4, 1024), :]


def slices(rank, x):
    return pl.pallas_call(
        slices_kernel,
        out_shape=[shape((1024, B), jnp.bfloat16)] * 4,
        in_specs=[SMEM, VMEM],
        out_specs=[VMEM] * 4,
        scratch_shapes=[pltpu.VMEM((4096, B), jnp.bfloat16)],
        compiler_params=pltpu.CompilerParams(vmem_limit_bytes=8 * MIB),
        cost_estimate=pl.CostEstimate(flops=0, bytes_accessed=2_000_000, transcendentals=0),
        name="slices",
    )(rank, x)


def tables_kernel(where_ref, tab_ref):
    rank = where_ref[0]
    for k in range(4):
        cosine, sine = split_table(rope_table(((rank // 4 - k + 4) % 4 * 4 + rank % 4) * B))
        tab_ref[k * B : (k + 1) * B, :B] = cosine
        tab_ref[k * B : (k + 1) * B, B:] = sine


def tables(rank):
    return pl.pallas_call(
        tables_kernel,
        out_shape=shape((4 * B, 2 * B), jnp.float32),
        in_specs=[SMEM],
        out_specs=VMEM,
        compiler_params=pltpu.CompilerParams(vmem_limit_bytes=4 * MIB),
        cost_estimate=pl.CostEstimate(flops=2_000_000, bytes_accessed=260_000, transcendentals=64_000),
        name="tables",
    )(rank)


def document_start(len_ref, position):
    start = position * 0
    end = jnp.int32(0)
    for d in range(8):
        end = end + len_ref[0, d]
        start = jnp.where(position >= end, end, start)
    return start


def column_keys(kvs):
    return jnp.concatenate([kv[:, :B] for kv in kvs], 0)


def heads_below(ref, first):
    return jnp.concatenate([ref[:, (first + h) * B : (first + h + 1) * B] for h in range(HEADS)], 0)


def by_source(qg0, qg1, q2, g2, q3, g3):
    for ref in (qg0, qg1):
        yield heads_below(ref, 0), heads_below(ref, HEADS)
    for q, g in ((q2, g2), (q3, g3)):
        yield heads_below(q, 0), heads_below(g, 0)


def in_lanes(rows_of_heads):
    return jnp.concatenate([rows_of_heads[h : h + 1, :] for h in range(HEADS)], 1)


def scores_kernel(
    where_ref, len_ref, kv0, kv1, kv2, qg0, qg1, q2, g2, q3, g3, p_ref, d_ref, stat_ref
):
    rank = where_ref[0]
    slab, col = rank // 4, rank % 4
    keys = column_keys((kv0, kv1, kv2))
    values = jnp.concatenate([kv[:, B:] for kv in (kv0, kv1, kv2)], 0)
    row = lax.broadcasted_iota(jnp.int32, (B, B), 0)
    for source, (queries, grads) in enumerate(by_source(qg0, qg1, q2, g2, q3, g3)):
        position = (slab * 4 + (col ^ source)) * B + lax.broadcasted_iota(jnp.int32, (1, B), 1)
        start = document_start(len_ref, position)
        allowed = jnp.concatenate(
            [
                (row >= start - (rank - 4 * b) * B) & (row <= position - rank * B)
                if b == 0
                else row >= start - (rank - 4 * b) * B
                for b in range(3)
            ],
            0,
        )
        for pair in range(2):
            part = slice(pair * 2 * B, (pair + 1) * 2 * B)
            s = dot(keys, queries[part], NT)
            d = dot(values, grads[part], NT)
            for h in range(2):
                here = slice(h * B, (h + 1) * B)
                lanes = slice((source * HEADS + pair * 2 + h) * B, (source * HEADS + pair * 2 + h + 1) * B)
                masked = jnp.where(allowed, s[:, here], NEG)
                top = jnp.max(masked, axis=0, keepdims=True)
                p = jnp.exp2((masked - top) * (SCALE * LOG2E))
                p_ref[:, lanes] = p
                d_ref[:, lanes] = d[:, here]
                sums = (top, jnp.sum(p, axis=0, keepdims=True), jnp.sum(p * d[:, here], axis=0, keepdims=True))
                for kind, value in enumerate(sums):
                    at = kind * 4 * HEADS + source * HEADS + pair * 2 + h
                    stat_ref[at : at + 1, :] = value


def scores(rank, lengths, kvs, qgs):
    wide = (3 * B, 2 * HALF)
    return pl.pallas_call(
        scores_kernel,
        out_shape=(
            shape(wide, jnp.float32),
            shape(wide, jnp.float32),
            shape((12 * HEADS, B), jnp.float32),
        ),
        in_specs=[SMEM, SMEM] + [VMEM] * 9,
        out_specs=(VMEM,) * 3,
        compiler_params=pltpu.CompilerParams(vmem_limit_bytes=20 * MIB),
        cost_estimate=pl.CostEstimate(flops=400_000_000, bytes_accessed=8_000_000, transcendentals=790_000),
        name="scores",
    )(rank, lengths, *kvs, *qgs)


def gradients_kernel(
    kv0, kv1, kv2, p_ref, d_ref, qg0, qg1, q2, g2, q3, g3, st0, st1, st2, st3,
    keep_ref, send_ref, dq0, dq1, dq2, dq3,
):
    keys = column_keys((kv0, kv1, kv2))
    dk = dv = None
    outs = (dq0, dq1, dq2, dq3)
    for source, (queries, grads) in enumerate(by_source(qg0, qg1, q2, g2, q3, g3)):
        tops, totals, sums = (
            [
                st[(kind * 4 + (source ^ bits)) * HEADS : (kind * 4 + (source ^ bits) + 1) * HEADS, :]
                for bits, st in enumerate((st0, st1, st2, st3))
            ]
            for kind in range(3)
        )
        top = jnp.maximum(jnp.maximum(tops[0], tops[1]), jnp.maximum(tops[2], tops[3]))
        factors = [jnp.exp2((t - top) * (SCALE * LOG2E)) for t in tops]
        inverse = 1.0 / sum(t * f for t, f in zip(totals, factors))
        delta = in_lanes(sum(t * f for t, f in zip(sums, factors)) * inverse)
        factor = in_lanes(factors[0] * inverse)
        lanes = slice(source * HEADS * B, (source + 1) * HEADS * B)
        p = p_ref[:, lanes] * factor
        ds = (p * (d_ref[:, lanes] - delta)).astype(jnp.bfloat16)
        more_v = dot(p.astype(jnp.bfloat16), grads, NN)
        more_k = dot(ds, queries, NN)
        dv = more_v if dv is None else dv + more_v
        dk = more_k if dk is None else dk + more_k
        outs[source][...] = dot(keys, ds, TN).astype(outs[source].dtype)
    dk = dk * SCALE
    keep_ref[:, :B] = dk
    keep_ref[:, B:] = dv
    send_ref[:, :B] = dk.astype(jnp.bfloat16)
    send_ref[:, B:] = dv.astype(jnp.bfloat16)


def gradients(kvs, p, d, qgs, stats):
    return pl.pallas_call(
        gradients_kernel,
        out_shape=(
            shape((3 * B, 2 * B), jnp.float32),
            shape((3 * B, 2 * B), jnp.bfloat16),
            shape((B, HEADS * B), jnp.float32),
            shape((B, HEADS * B), jnp.bfloat16),
            shape((B, HEADS * B), jnp.bfloat16),
            shape((B, HEADS * B), jnp.bfloat16),
        ),
        in_specs=[VMEM] * 15,
        out_specs=(VMEM,) * 6,
        compiler_params=pltpu.CompilerParams(vmem_limit_bytes=20 * MIB),
        cost_estimate=pl.CostEstimate(flops=600_000_000, bytes_accessed=8_000_000, transcendentals=8_000),
        name="gradients",
    )(*kvs, p, d, *qgs, *stats)


def query_end_kernel(mine_ref, r1, r2, r3, tab_ref, g01_ref, out_ref, key_ref, value_ref):
    key_ref[...] = g01_ref[:B, :B]
    value_ref[...] = g01_ref[:B, B:]
    cosine, sine = tab_ref[:B, :B], tab_ref[:B, B:]
    for h in range(HEADS):
        part = slice(h * B, (h + 1) * B)
        u = mine_ref[:, part]
        for ref in (r1, r2, r3):
            u = u + ref[:, part].astype(jnp.float32)
        out_ref[:, part] = rotated(u.T * SCALE, cosine, -sine).astype(jnp.bfloat16)


def query_end(mine, arrived, table, low):
    return pl.pallas_call(
        query_end_kernel,
        out_shape=(
            shape((B, HEADS * B), jnp.bfloat16),
            shape((B, B), jnp.bfloat16),
            shape((B, B), jnp.bfloat16),
        ),
        in_specs=[VMEM] * 6,
        out_specs=(VMEM,) * 3,
        compiler_params=pltpu.CompilerParams(vmem_limit_bytes=4 * MIB),
        cost_estimate=pl.CostEstimate(flops=300_000, bytes_accessed=900_000, transcendentals=0),
        name="query_end",
    )(mine, *arrived, table, low)


def weight_kernel(
    where_ref, keep_ref, r1, r2, r3, tab_ref, x0, x1, x2, x3,
    send_ref, g01_ref, g23_ref,
):
    core = where_ref[0] % 2

    def part(source, b, lanes):
        at = slice(b * B, (b + 1) * B)
        ref = (keep_ref, r1, r2, r3)[source]
        return ref[at, lanes * B : (lanes + 1) * B].astype(jnp.float32)

    grads = []
    for k in range(4):
        key, value = (
            part(k, 0, lanes) + part((k - 1) % 4, 1, lanes) + part((k - 2) % 4, 2, lanes) for lanes in (0, 1)
        )
        cosine, sine = tab_ref[k * B : (k + 1) * B, :B], tab_ref[k * B : (k + 1) * B, B:]
        key = rotated(key, cosine, -sine).astype(jnp.bfloat16)
        value = value.astype(jnp.bfloat16)
        grads.append(jnp.concatenate([key, value], 1))
    low, high = jnp.concatenate(grads[:2], 0), jnp.concatenate(grads[2:], 0)
    g01_ref[...] = low
    g23_ref[...] = high
    send_ref[...] = half_of_weight(1 - core, (x0, x1, x2, x3), low, high).astype(jnp.bfloat16)


def half_of_weight(core, xs, low, high):
    at = rows(core, 512)
    total = dot(jnp.concatenate([xs[0][at, :], xs[1][at, :]], 1), low, NN)
    return total + dot(jnp.concatenate([xs[2][at, :], xs[3][at, :]], 1), high, NN)


def own_half_kernel(where_ref, g01_ref, g23_ref, x0, x1, x2, x3, own_ref):
    core = where_ref[0] % 2
    own_ref[...] = half_of_weight(core, (x0, x1, x2, x3), g01_ref[...], g23_ref[...])


def own_half(rank, low, high, xs):
    return pl.pallas_call(
        own_half_kernel,
        out_shape=shape((512, 256), jnp.float32),
        in_specs=[SMEM] + [VMEM] * 6,
        out_specs=VMEM,
        compiler_params=pltpu.CompilerParams(vmem_limit_bytes=12 * MIB),
        cost_estimate=pl.CostEstimate(flops=134_000_000, bytes_accessed=1_800_000, transcendentals=0),
        name="own_half",
    )(rank, low, high, *xs)


def weight_part(rank, keep, arrived, table, xs):
    return pl.pallas_call(
        weight_kernel,
        out_shape=(
            shape((512, 256), jnp.bfloat16),
            shape((256, 256), jnp.bfloat16),
            shape((256, 256), jnp.bfloat16),
        ),
        in_specs=[SMEM] + [VMEM] * 9,
        out_specs=(VMEM,) * 3,
        compiler_params=pltpu.CompilerParams(vmem_limit_bytes=12 * MIB),
        cost_estimate=pl.CostEstimate(flops=134_000_000, bytes_accessed=3_000_000, transcendentals=0),
        name="weight",
    )(rank, keep, *arrived, table, *xs)


def weight_fold_kernel(own_ref, arrived_ref, out_ref, total, sem):
    copies = []
    for i in range(4):
        part = slice(i * B, (i + 1) * B)
        total[part, :] = (own_ref[part, :] + arrived_ref[part, :].astype(jnp.float32)).astype(jnp.bfloat16)
        copies.append(pltpu.make_async_copy(total.at[part], out_ref.at[part], sem.at[i]))
        copies[-1].start()
    for copy in copies:
        copy.wait()


def weight_fold(own, arrived):
    return pl.pallas_call(
        weight_fold_kernel,
        out_shape=shape((512, 256), jnp.bfloat16),
        in_specs=[VMEM, VMEM],
        out_specs=HBM,
        scratch_shapes=[pltpu.VMEM((512, 256), jnp.bfloat16), pltpu.SemaphoreType.DMA((4,))],
        compiler_params=pltpu.CompilerParams(vmem_limit_bytes=4 * MIB),
        cost_estimate=pl.CostEstimate(flops=131_072, bytes_accessed=1_000_000, transcendentals=0),
        name="weight_fold",
    )(own, arrived)


def compute(layer_input, query_states, key_states, value_states, output_grad, doc_lengths):
    where = lax.axis_index("ctx").astype(jnp.int32)[None]

    def permute(array, pairs):
        return lax.ppermute(array, "ctx", pairs)

    def around(array, slabs):
        return permute(array, [(i, (i + 4 * slabs) % 16) for i in range(16)])

    def swap(array, bits):
        return permute(array, [(i, i ^ bits) for i in range(16)])

    g_z = swap(output_grad[0], 2)
    kv, qg, q, x, lengths = prepare(
        where,
        key_states[0],
        value_states[0],
        query_states[0],
        output_grad[0],
        layer_input[0],
        doc_lengths,
    )
    q_z = swap(q, 2)
    kvs = [kv, around(kv, 1), around(kv, 2)]
    qg_c = swap(qg, 1)
    q_cz, g_cz = swap(q_z, 1), swap(g_z, 1)

    xs = slices(where, x)
    xs = [xs[0]] + [around(xs[k], k) for k in (1, 2, 3)]

    qgs = (qg, qg_c, q_z, g_z, q_cz, g_cz)
    p, d, stat = scores(where, lengths, kvs, qgs)
    stats = [stat] + [swap(stat, bits) for bits in (1, 2, 3)]
    table = tables(where)
    keep, send, mine, *others = gradients(kvs, p, d, qgs, stats)

    arrived = [around(send, k) for k in (1, 2, 3)]
    query_parts = [swap(part, bits) for bits, part in zip((1, 2, 3), others)]
    send, low, high = weight_part(where, keep, arrived, table, xs)
    arrived = swap(send, 1)
    own = own_half(where, low, high, xs)
    blocks = weight_fold(own, arrived).reshape(32, 16, 256)
    groups = [
        [dp * 16 + slab * 4 + z * 2 + core for dp in range(16) for z in range(2)]
        for slab in range(4)
        for core in range(2)
    ]
    blocks = lax.all_to_all(blocks, ("dp", "ctx"), split_axis=0, concat_axis=0, tiled=True, axis_index_groups=groups)
    query_grad, key_grad, value_grad = query_end(mine, query_parts, table, low)
    weight_grad = jnp.sum(blocks.astype(jnp.float32), axis=0)
    return query_grad[None], key_grad[None], value_grad[None], weight_grad


def solution(mesh):
    split = P("dp", "ctx", None)
    return jax.shard_map(
        compute,
        mesh=mesh,
        in_specs=(split,) * 5 + (P("dp", None),),
        out_specs=(split, split, split, P(("dp", "ctx"), None)),
        check_vma=False,
    )
```

```python
import math

import jax
import jax.numpy as jnp
from jax import lax
from jax.experimental import pallas as pl
from jax.experimental.pallas import tpu as pltpu
from jax.sharding import PartitionSpec as P


ROPE_BASE = 500000.0
NEG = -1e30
MIB = 1024 * 1024
B = 128
HEADS = 4
HALF = HEADS * 2 * B
NT = (((1,), (1,)), ((), ()))
TN = (((0,), (0,)), ((), ()))
NN = (((1,), (0,)), ((), ()))
SCALE = B**-0.5
LOG2E = 1.4426950408889634


VMEM = pl.BlockSpec(memory_space=pltpu.VMEM)
SMEM = pl.BlockSpec(memory_space=pltpu.SMEM)
HBM = pl.BlockSpec(memory_space=pltpu.HBM)


def dot(a, b, dims):
    return lax.dot_general(a, b, dims, preferred_element_type=jnp.float32)


def shape(dims, dtype):
    return jax.ShapeDtypeStruct(dims, dtype)


def rope_table(first):
    half = B // 2
    index = lax.broadcasted_iota(jnp.int32, (1, half), 1).astype(jnp.float32)
    frequency = jnp.exp(index * (-2.0 * math.log(ROPE_BASE) / B))
    position = first + lax.broadcasted_iota(jnp.int32, (B, 1), 0)
    angles = position.astype(jnp.float32) * frequency
    return jnp.concatenate([jnp.cos(angles), jnp.sin(angles)], 1)


def split_table(table):
    lane = lax.broadcasted_iota(jnp.int32, table.shape, 1)
    swapped = pltpu.roll(table, B // 2, 1)
    low = lane < B // 2
    return jnp.where(low, table, swapped), jnp.where(low, -swapped, table)


def rotated(u, cosine, sine):
    return u * cosine + pltpu.roll(u, B // 2, 1) * sine


def rows(index, size=B):
    return pl.ds(pl.multiple_of(index * size, size), size)


def prepare_kernel(
    where_ref, key_ref, value_ref, query_ref, grad_ref, x_ref, len_ref,
    kv_ref, qg_ref, x_out, len_out,
    key_s, query_s, sem,
):
    copies = [
        pltpu.make_async_copy(key_ref, key_s, sem.at[0]),
        pltpu.make_async_copy(query_ref, query_s, sem.at[1]),
        pltpu.make_async_copy(value_ref, kv_ref.at[:, B:], sem.at[2]),
        pltpu.make_async_copy(grad_ref, qg_ref.at[:, HEADS * B :], sem.at[3]),
        pltpu.make_async_copy(len_ref, len_out, sem.at[4]),
        pltpu.make_async_copy(x_ref, x_out, sem.at[5]),
    ]
    for copy in copies:
        copy.start()
    cosine, sine = split_table(rope_table(where_ref[0] * B))
    copies[0].wait()
    kv_ref[:, :B] = rotated(key_s[...].astype(jnp.float32), cosine, sine).astype(jnp.bfloat16)
    copies[1].wait()
    for h in range(HEADS):
        part = slice(h * B, (h + 1) * B)
        u = query_s[:, part].astype(jnp.float32)
        qg_ref[:, part] = rotated(u, cosine, sine).astype(jnp.bfloat16)
    for copy in copies[2:]:
        copy.wait()


def prepare(rank, keys, values, queries, grads, x, lengths):
    hbm = [pltpu.with_memory_space_constraint(a, pltpu.HBM) for a in (keys, values, queries, grads, x, lengths)]
    keys, values, queries, grads, x, lengths = hbm
    return pl.pallas_call(
        prepare_kernel,
        out_shape=(
            shape((B, 2 * B), jnp.bfloat16),
            shape((B, 2 * HEADS * B), jnp.bfloat16),
            shape((B, 4096), jnp.bfloat16),
            shape((1, 8), jnp.int32),
        ),
        in_specs=[SMEM] + [HBM] * 6,
        out_specs=(VMEM,) * 4,
        scratch_shapes=[
            pltpu.VMEM((B, B), jnp.bfloat16),
            pltpu.VMEM((B, HEADS * B), jnp.bfloat16),
            pltpu.SemaphoreType.DMA((6,)),
        ],
        compiler_params=pltpu.CompilerParams(vmem_limit_bytes=4 * MIB),
        name="prepare",
    )(rank, keys, values, queries, grads, x, lengths)


def slices_kernel(where_ref, x_ref, o0, o1, o2, o3, turned):
    slab = where_ref[0] // 4
    for i in range(32):
        tile = x_ref[:, i * B : (i + 1) * B].T
        for j in range(8):
            to, z, core = i % 2 * 2 + j // 4, j // 2 % 2, j % 2
            at = ((to * 2 + core) * 32 + i // 2 * 2 + z) * 16
            turned[at : at + 16, :] = tile[j * 16 : (j + 1) * 16, :]
    for k, out in enumerate((o0, o1, o2, o3)):
        out[...] = turned[rows((slab + k) % 4, 1024), :]


def slices(rank, x):
    return pl.pallas_call(
        slices_kernel,
        out_shape=[shape((1024, B), jnp.bfloat16)] * 4,
        in_specs=[SMEM, VMEM],
        out_specs=[VMEM] * 4,
        scratch_shapes=[pltpu.VMEM((4096, B), jnp.bfloat16)],
        compiler_params=pltpu.CompilerParams(vmem_limit_bytes=8 * MIB),
        cost_estimate=pl.CostEstimate(flops=0, bytes_accessed=2_000_000, transcendentals=0),
        name="slices",
    )(rank, x)


def tables_kernel(where_ref, tab_ref):
    rank = where_ref[0]
    for k in range(4):
        cosine, sine = split_table(rope_table(((rank // 4 - k + 4) % 4 * 4 + rank % 4) * B))
        tab_ref[k * B : (k + 1) * B, :B] = cosine
        tab_ref[k * B : (k + 1) * B, B:] = sine


def tables(rank):
    return pl.pallas_call(
        tables_kernel,
        out_shape=shape((4 * B, 2 * B), jnp.float32),
        in_specs=[SMEM],
        out_specs=VMEM,
        compiler_params=pltpu.CompilerParams(vmem_limit_bytes=4 * MIB),
        cost_estimate=pl.CostEstimate(flops=2_000_000, bytes_accessed=260_000, transcendentals=64_000),
        name="tables",
    )(rank)


def document_start(len_ref, position):
    start = position * 0
    end = jnp.int32(0)
    for d in range(8):
        end = end + len_ref[0, d]
        start = jnp.where(position >= end, end, start)
    return start


def column_keys(kvs):
    return jnp.concatenate([kv[:, :B] for kv in kvs], 0)


def heads_below(ref, first):
    return jnp.concatenate([ref[:, (first + h) * B : (first + h + 1) * B] for h in range(HEADS)], 0)


def in_lanes(rows_of_heads):
    return jnp.concatenate([rows_of_heads[h : h + 1, :] for h in range(HEADS)], 1)


def scores_kernel(
    where_ref, len_ref, kv0, kv1, kv2, qg0, qg1, qg2, qg3, p_ref, d_ref, stat_ref
):
    rank = where_ref[0]
    slab, col = rank // 4, rank % 4
    keys = column_keys((kv0, kv1, kv2))
    values = jnp.concatenate([kv[:, B:] for kv in (kv0, kv1, kv2)], 0)
    row = lax.broadcasted_iota(jnp.int32, (B, B), 0)
    for source, ref in enumerate((qg0, qg1, qg2, qg3)):
        position = (slab * 4 + (col ^ source)) * B + lax.broadcasted_iota(jnp.int32, (1, B), 1)
        start = document_start(len_ref, position)
        allowed = jnp.concatenate(
            [
                (row >= start - (rank - 4 * b) * B) & (row <= position - rank * B)
                if b == 0
                else row >= start - (rank - 4 * b) * B
                for b in range(3)
            ],
            0,
        )
        queries, grads = heads_below(ref, 0), heads_below(ref, HEADS)
        for pair in range(2):
            part = slice(pair * 2 * B, (pair + 1) * 2 * B)
            s = dot(keys, queries[part], NT)
            d = dot(values, grads[part], NT)
            for h in range(2):
                here = slice(h * B, (h + 1) * B)
                lanes = slice((source * HEADS + pair * 2 + h) * B, (source * HEADS + pair * 2 + h + 1) * B)
                masked = jnp.where(allowed, s[:, here], NEG)
                top = jnp.max(masked, axis=0, keepdims=True)
                p = jnp.exp2((masked - top) * (SCALE * LOG2E))
                p_ref[:, lanes] = p
                d_ref[:, lanes] = d[:, here]
                sums = (top, jnp.sum(p, axis=0, keepdims=True), jnp.sum(p * d[:, here], axis=0, keepdims=True))
                for kind, value in enumerate(sums):
                    at = kind * 4 * HEADS + source * HEADS + pair * 2 + h
                    stat_ref[at : at + 1, :] = value


def scores(rank, lengths, kvs, qgs):
    wide = (3 * B, 2 * HALF)
    return pl.pallas_call(
        scores_kernel,
        out_shape=(
            shape(wide, jnp.float32),
            shape(wide, jnp.float32),
            shape((12 * HEADS, B), jnp.float32),
        ),
        in_specs=[SMEM, SMEM] + [VMEM] * 7,
        out_specs=(VMEM,) * 3,
        compiler_params=pltpu.CompilerParams(vmem_limit_bytes=20 * MIB),
        cost_estimate=pl.CostEstimate(flops=400_000_000, bytes_accessed=8_000_000, transcendentals=790_000),
        name="scores",
    )(rank, lengths, *kvs, *qgs)


def gradients_kernel(
    kv0, kv1, kv2, p_ref, d_ref, qg0, qg1, qg2, qg3, st0, st1, st2, st3,
    keep_ref, send_ref, dq0, dq1, dq2, dq3,
):
    keys = column_keys((kv0, kv1, kv2))
    dk = dv = None
    for source, (ref, out) in enumerate(zip((qg0, qg1, qg2, qg3), (dq0, dq1, dq2, dq3))):
        tops, totals, sums = (
            [
                st[(kind * 4 + (source ^ bits)) * HEADS : (kind * 4 + (source ^ bits) + 1) * HEADS, :]
                for bits, st in enumerate((st0, st1, st2, st3))
            ]
            for kind in range(3)
        )
        top = jnp.maximum(jnp.maximum(tops[0], tops[1]), jnp.maximum(tops[2], tops[3]))
        factors = [jnp.exp2((t - top) * (SCALE * LOG2E)) for t in tops]
        inverse = 1.0 / sum(t * f for t, f in zip(totals, factors))
        delta = in_lanes(sum(t * f for t, f in zip(sums, factors)) * inverse)
        factor = in_lanes(factors[0] * inverse)
        lanes = slice(source * HEADS * B, (source + 1) * HEADS * B)
        p = p_ref[:, lanes] * factor
        ds = (p * (d_ref[:, lanes] - delta)).astype(jnp.bfloat16)
        more_v = dot(p.astype(jnp.bfloat16), heads_below(ref, HEADS), NN)
        more_k = dot(ds, heads_below(ref, 0), NN)
        dv = more_v if dv is None else dv + more_v
        dk = more_k if dk is None else dk + more_k
        out[...] = dot(keys, ds, TN).astype(out.dtype)
    dk = dk * SCALE
    keep_ref[:, :B] = dk
    keep_ref[:, B:] = dv
    send_ref[:, :B] = dk.astype(jnp.bfloat16)
    send_ref[:, B:] = dv.astype(jnp.bfloat16)


def gradients(kvs, p, d, qgs, stats):
    return pl.pallas_call(
        gradients_kernel,
        out_shape=(
            shape((3 * B, 2 * B), jnp.float32),
            shape((3 * B, 2 * B), jnp.bfloat16),
            shape((B, HEADS * B), jnp.float32),
            shape((B, HEADS * B), jnp.bfloat16),
            shape((B, HEADS * B), jnp.bfloat16),
            shape((B, HEADS * B), jnp.bfloat16),
        ),
        in_specs=[VMEM] * 13,
        out_specs=(VMEM,) * 6,
        compiler_params=pltpu.CompilerParams(vmem_limit_bytes=20 * MIB),
        cost_estimate=pl.CostEstimate(flops=600_000_000, bytes_accessed=8_000_000, transcendentals=8_000),
        name="gradients",
    )(*kvs, p, d, *qgs, *stats)


def query_end_kernel(mine_ref, r1, r2, r3, tab_ref, g01_ref, out_ref, key_ref, value_ref):
    key_ref[...] = g01_ref[:B, :B]
    value_ref[...] = g01_ref[:B, B:]
    cosine, sine = tab_ref[:B, :B], tab_ref[:B, B:]
    for h in range(HEADS):
        part = slice(h * B, (h + 1) * B)
        u = mine_ref[:, part]
        for ref in (r1, r2, r3):
            u = u + ref[:, part].astype(jnp.float32)
        out_ref[:, part] = rotated(u.T * SCALE, cosine, -sine).astype(jnp.bfloat16)


def query_end(mine, arrived, table, low):
    return pl.pallas_call(
        query_end_kernel,
        out_shape=(
            shape((B, HEADS * B), jnp.bfloat16),
            shape((B, B), jnp.bfloat16),
            shape((B, B), jnp.bfloat16),
        ),
        in_specs=[VMEM] * 6,
        out_specs=(VMEM,) * 3,
        compiler_params=pltpu.CompilerParams(vmem_limit_bytes=4 * MIB),
        cost_estimate=pl.CostEstimate(flops=300_000, bytes_accessed=900_000, transcendentals=0),
        name="query_end",
    )(mine, *arrived, table, low)


def weight_kernel(
    where_ref, keep_ref, r1, r2, r3, tab_ref, x0, x1, x2, x3,
    send_ref, g01_ref, g23_ref,
):
    core = where_ref[0] % 2

    def part(source, b, lanes):
        at = slice(b * B, (b + 1) * B)
        ref = (keep_ref, r1, r2, r3)[source]
        return ref[at, lanes * B : (lanes + 1) * B].astype(jnp.float32)

    grads = []
    for k in range(4):
        key, value = (
            part(k, 0, lanes) + part((k - 1) % 4, 1, lanes) + part((k - 2) % 4, 2, lanes) for lanes in (0, 1)
        )
        cosine, sine = tab_ref[k * B : (k + 1) * B, :B], tab_ref[k * B : (k + 1) * B, B:]
        key = rotated(key, cosine, -sine).astype(jnp.bfloat16)
        value = value.astype(jnp.bfloat16)
        grads.append(jnp.concatenate([key, value], 1))
    low, high = jnp.concatenate(grads[:2], 0), jnp.concatenate(grads[2:], 0)
    g01_ref[...] = low
    g23_ref[...] = high
    send_ref[...] = half_of_weight(1 - core, (x0, x1, x2, x3), low, high).astype(jnp.bfloat16)


def half_of_weight(core, xs, low, high):
    at = rows(core, 512)
    total = dot(jnp.concatenate([xs[0][at, :], xs[1][at, :]], 1), low, NN)
    return total + dot(jnp.concatenate([xs[2][at, :], xs[3][at, :]], 1), high, NN)


def own_half_kernel(where_ref, g01_ref, g23_ref, x0, x1, x2, x3, own_ref):
    core = where_ref[0] % 2
    own_ref[...] = half_of_weight(core, (x0, x1, x2, x3), g01_ref[...], g23_ref[...])


def own_half(rank, low, high, xs):
    return pl.pallas_call(
        own_half_kernel,
        out_shape=shape((512, 256), jnp.float32),
        in_specs=[SMEM] + [VMEM] * 6,
        out_specs=VMEM,
        compiler_params=pltpu.CompilerParams(vmem_limit_bytes=12 * MIB),
        cost_estimate=pl.CostEstimate(flops=134_000_000, bytes_accessed=1_800_000, transcendentals=0),
        name="own_half",
    )(rank, low, high, *xs)


def weight_part(rank, keep, arrived, table, xs):
    return pl.pallas_call(
        weight_kernel,
        out_shape=(
            shape((512, 256), jnp.bfloat16),
            shape((256, 256), jnp.bfloat16),
            shape((256, 256), jnp.bfloat16),
        ),
        in_specs=[SMEM] + [VMEM] * 9,
        out_specs=(VMEM,) * 3,
        compiler_params=pltpu.CompilerParams(vmem_limit_bytes=12 * MIB),
        cost_estimate=pl.CostEstimate(flops=134_000_000, bytes_accessed=3_000_000, transcendentals=0),
        name="weight",
    )(rank, keep, *arrived, table, *xs)


def weight_fold_kernel(own_ref, arrived_ref, out_ref, total, sem):
    copies = []
    for i in range(4):
        part = slice(i * B, (i + 1) * B)
        total[part, :] = (own_ref[part, :] + arrived_ref[part, :].astype(jnp.float32)).astype(jnp.bfloat16)
        copies.append(pltpu.make_async_copy(total.at[part], out_ref.at[part], sem.at[i]))
        copies[-1].start()
    for copy in copies:
        copy.wait()


def weight_fold(own, arrived):
    return pl.pallas_call(
        weight_fold_kernel,
        out_shape=shape((512, 256), jnp.bfloat16),
        in_specs=[VMEM, VMEM],
        out_specs=HBM,
        scratch_shapes=[pltpu.VMEM((512, 256), jnp.bfloat16), pltpu.SemaphoreType.DMA((4,))],
        compiler_params=pltpu.CompilerParams(vmem_limit_bytes=4 * MIB),
        cost_estimate=pl.CostEstimate(flops=131_072, bytes_accessed=1_000_000, transcendentals=0),
        name="weight_fold",
    )(own, arrived)


def compute(layer_input, query_states, key_states, value_states, output_grad, doc_lengths):
    where = lax.axis_index("ctx").astype(jnp.int32)[None]

    def permute(array, pairs):
        return lax.ppermute(array, "ctx", pairs)

    def around(array, slabs):
        return permute(array, [(i, (i + 4 * slabs) % 16) for i in range(16)])

    def swap(array, bits):
        return permute(array, [(i, i ^ bits) for i in range(16)])

    kv, qg, x, lengths = prepare(
        where,
        key_states[0],
        value_states[0],
        query_states[0],
        output_grad[0],
        layer_input[0],
        doc_lengths,
    )
    qg_z = swap(qg, 2)
    kvs = [kv, around(kv, 1), around(kv, 2)]
    qg_c = swap(qg, 1)
    qg_cz = swap(qg_z, 1)

    xs = slices(where, x)
    xs = [xs[0]] + [around(xs[k], k) for k in (1, 2, 3)]

    qgs = (qg, qg_c, qg_z, qg_cz)
    p, d, stat = scores(where, lengths, kvs, qgs)
    stats = [stat] + [swap(stat, bits) for bits in (1, 2, 3)]
    table = tables(where)
    keep, send, mine, *others = gradients(kvs, p, d, qgs, stats)

    arrived = [around(send, k) for k in (1, 2, 3)]
    *others, arrived[1] = lax.optimization_barrier((*others, arrived[1]))
    query_parts = [swap(part, bits) for bits, part in zip((1, 2, 3), others)]
    send, low, high = weight_part(where, keep, arrived, table, xs)
    arrived = swap(send, 1)
    own = own_half(where, low, high, xs)
    blocks = weight_fold(own, arrived).reshape(32, 16, 256)
    groups = [
        [dp * 16 + slab * 4 + z * 2 + core for dp in range(16) for z in range(2)]
        for slab in range(4)
        for core in range(2)
    ]
    blocks = lax.all_to_all(blocks, ("dp", "ctx"), split_axis=0, concat_axis=0, tiled=True, axis_index_groups=groups)
    query_grad, key_grad, value_grad = query_end(mine, query_parts, table, low)
    weight_grad = jnp.sum(blocks.astype(jnp.float32), axis=0)
    return query_grad[None], key_grad[None], value_grad[None], weight_grad


def solution(mesh):
    split = P("dp", "ctx", None)
    return jax.shard_map(
        compute,
        mesh=mesh,
        in_specs=(split,) * 5 + (P("dp", None),),
        out_specs=(split, split, split, P(("dp", "ctx"), None)),
        check_vma=False,
    )
```
